32 devices in a mesh: dp: 16 (over z, x, core), mp: 2 (over y).
Axes of the slice: x: 2, y: 2, z: 4, core: 2. Of those that a mesh axis runs over, the one named last changes fastest.
Arguments:
- inputs: bfloat16 [2, 78, 16384], P(None, None, 'dp'), may hold values from -6 to 6
- targets: float32 [2, 78, 16384], P(None, None, 'dp'), may hold values from -6 to 6
- senders: int32 [2, 32768], P(None, 'dp'), may hold values from 0 to 767
- receivers: int32 [2, 32768], P(None, 'dp'), may hold values from 0 to 511
- g2m_dst: int32 [2, 16384], P(None, 'dp'), may hold values from 0 to 511
- m2g_src: int32 [2, 3, 16384], P(None, None, 'dp'), may hold values from 0 to 511
- delta_scale: float32 [78], replicated, may hold values from 0.5 to 2
- level_index: int32 [78], replicated, may hold values from 0 to 12
- step_count: int32 [], replicated, may hold values from 2 to 20
- soap_owner: int32 [8], replicated, may hold values from 0 to 15, as said below
- edge_first: float32 [2, 768, 256], P(None, None, 'mp'), may hold values from -0.21875 to 0.21875
- node_first: float32 [2, 512, 256], P(None, None, 'mp'), may hold values from -0.25 to 0.25
- second: float32 [4, 256, 256], P(None, 'mp'), may hold values from -0.375 to 0.375
- io_weights: float32 [2, 78, 256], replicated, may hold values from -0.375 to 0.375
- vectors: float32 [12, 256], replicated, may hold values from 0.25 to 1.75
- edge_first_m: float32 [2, 768, 256], replicated, may hold values from -3.5762787e-07 to 3.5762787e-07
- node_first_m: float32 [2, 512, 256], replicated, may hold values from -3.5762787e-07 to 3.5762787e-07
- second_m: float32 [4, 256, 256], replicated, may hold values from -3.5762787e-07 to 3.5762787e-07
- edge_first_v: float32 [2, 768, 256], replicated, may hold values from 2.6e-15 to 1.05e-14
- node_first_v: float32 [2, 512, 256], replicated, may hold values from 2.6e-15 to 1.05e-14
- second_v: float32 [4, 256, 256], replicated, may hold values from 2.6e-15 to 1.05e-14
- io_m: float32 [2, 78, 256], replicated, may hold values from -3.5762787e-07 to 3.5762787e-07
- io_v: float32 [2, 78, 256], replicated, may hold values from 2.6e-15 to 1.05e-14
- vector_m: float32 [12, 256], replicated, may hold values from -9.536743e-07 to 9.536743e-07
- vector_v: float32 [12, 256], replicated, may hold values from 2.4e-14 to 9.5e-14
- edge_left_stat: float32 [2, 768, 768], replicated, may hold values from -1.3e-09 to 1.3e-08, as said below
- edge_left_basis: float32 [2, 768, 768], replicated, may hold values from -1 to 1, as said below
- node_left_stat: float32 [2, 512, 512], replicated, may hold values from -1.3e-09 to 1.3e-08, as said below
- node_left_basis: float32 [2, 512, 512], replicated, may hold values from -1 to 1, as said below
- second_left_stat: float32 [4, 256, 256], replicated, may hold values from -1.3e-09 to 1.3e-08, as said below
- second_left_basis: float32 [4, 256, 256], replicated, may hold values from -1 to 1, as said below
- right_stat: float32 [8, 256, 256], replicated, may hold values from -1.3e-09 to 1.3e-08, as said below
- right_basis: float32 [8, 256, 256], replicated, may hold values from -1 to 1, as said below
Outputs:
- loss: float32 [], replicated
- grad_norm: float32 [], replicated
- new_edge_first: float32 [2, 768, 256], P(None, None, 'mp')
- edge_first_copy: bfloat16 [2, 768, 256], P(None, None, 'mp')
- new_node_first: float32 [2, 512, 256], P(None, None, 'mp')
- node_first_copy: bfloat16 [2, 512, 256], P(None, None, 'mp')
- new_second: float32 [4, 256, 256], P(None, 'mp')
- second_copy: bfloat16 [4, 256, 256], P(None, 'mp')
- new_io: float32 [2, 78, 256], replicated
- io_copy: bfloat16 [2, 78, 256], replicated
- new_vectors: float32 [12, 256], replicated
- vectors_copy: bfloat16 [12, 256], replicated
- out_edge_first_m: float32 [2, 768, 256], replicated
- out_node_first_m: float32 [2, 512, 256], replicated
- out_second_m: float32 [4, 256, 256], replicated
- out_edge_first_v: float32 [2, 768, 256], replicated
- out_node_first_v: float32 [2, 512, 256], replicated
- out_second_v: float32 [4, 256, 256], replicated
- out_io_m: float32 [2, 78, 256], replicated
- out_io_v: float32 [2, 78, 256], replicated
- out_vector_m: float32 [12, 256], replicated
- out_vector_v: float32 [12, 256], replicated
- input_grad: float32 [2, 78, 16384], P(None, None, 'dp')
The draws below stay inside these ranges and needn't reach their ends.
Inputs may be any that keep to these rules, and one draw needn't show every extreme that they name: `soap_owner`: distinct owners. `edge_left_stat`: symmetric and diagonally dominant with a positive diagonal. `node_left_stat`: symmetric and diagonally dominant with a positive diagonal. `second_left_stat`: symmetric and diagonally dominant with a positive diagonal. `right_stat`: symmetric and diagonally dominant with a positive diagonal. `edge_left_basis`: each matrix orthogonal. `node_left_basis`: each matrix orthogonal. `second_left_basis`: each matrix orthogonal. `right_basis`: each matrix orthogonal.
All inputs are finite; a program needn't handle non-finite values.
Results may differ from the reference program's by a relative error of at most 0.019.
Values may be sent and summed in bfloat16 or wider, within the bound.
A program may use at most 256 MiB of HBM per device.

```python
import math
import jax
import jax.numpy as jnp
from jax import lax

L = 256
F = 78
LEVELS = 13
NODE_DEV = 512
MICRO = 2
LAYERS = 2
EDGE_DEV = 2048
GRID_DEV = 1024
EDGES = 32768
GRID = 16384
VEC = 12
N_DP = 16
N_MP = 2


STAT_SCALE = 1.27e-09


def spd_matrix(key, count, order):
    keys = jax.random.split(key, 2)
    diagonal = jax.random.uniform(keys[0], (count, order), minval=1.0, maxval=10.0)
    noise = jax.random.uniform(keys[1], (count, order, order), minval=-1.0, maxval=1.0) * (0.45 / order)
    symmetric = noise + jnp.swapaxes(noise, 1, 2)
    return (STAT_SCALE * (symmetric + diagonal[:, :, None] * jnp.eye(order, dtype=jnp.float32))).astype(jnp.float32)


def orthogonal(key, count, order):
    keys = jax.random.split(key, 3)
    rows = jnp.arange(order, dtype=jnp.float32)[:, None]
    cols = jnp.arange(order, dtype=jnp.float32)[None, :]
    table = jnp.sqrt(2.0 / order) * jnp.cos(jnp.pi * (2.0 * rows + 1.0) * cols / (2.0 * order))
    table = jnp.where(cols == 0.0, table * jnp.sqrt(0.5), table).astype(jnp.float32)
    orders = jax.vmap(lambda k: jax.random.permutation(k, order))(jax.random.split(keys[0], count))
    picked = jnp.moveaxis(jnp.take(table, orders, axis=1), 1, 0)
    row_signs = jnp.where(jax.random.bernoulli(keys[1], 0.5, (count, order, 1)), 1.0, -1.0)
    col_signs = jnp.where(jax.random.bernoulli(keys[2], 0.5, (count, 1, order)), 1.0, -1.0)
    return (picked * row_signs * col_signs).astype(jnp.float32)


def draw_soap_owner(key, part):
    count = 4 * LAYERS
    spots = jnp.arange(count, dtype=jnp.int32) * (N_DP - 1) // (count - 1)
    return jax.random.permutation(jax.random.fold_in(key, 19), spots).astype(jnp.int32)


def draw_edge_left_stat(key, part):
    return spd_matrix(jax.random.fold_in(key, 11), LAYERS, 3 * L)


def draw_edge_left_basis(key, part):
    return orthogonal(jax.random.fold_in(key, 12), LAYERS, 3 * L)


def draw_node_left_stat(key, part):
    return spd_matrix(jax.random.fold_in(key, 13), LAYERS, 2 * L)


def draw_node_left_basis(key, part):
    return orthogonal(jax.random.fold_in(key, 14), LAYERS, 2 * L)


def draw_second_left_stat(key, part):
    return spd_matrix(jax.random.fold_in(key, 15), 2 * LAYERS, L)


def draw_second_left_basis(key, part):
    return orthogonal(jax.random.fold_in(key, 16), 2 * LAYERS, L)


def draw_right_stat(key, part):
    return spd_matrix(jax.random.fold_in(key, 17), 4 * LAYERS, L)


def draw_right_basis(key, part):
    return orthogonal(jax.random.fold_in(key, 18), 4 * LAYERS, L)


def touch_ends(result, own_key, smallest, largest):
    longest = result.shape.index(max(result.shape))
    spots = []
    for shift in (0, 1):
        where = [jax.random.randint(jax.random.fold_in(own_key, axis), (), 0, length) for axis, length in enumerate(result.shape)]
        where[longest] = (where[longest] + shift) % result.shape[longest]
        spots.append(tuple(where))
    return result.at[spots[0]].set(smallest).at[spots[1]].set(largest)


def level_of(own_key, shape, pieces, low, largest):
    def one(dim, parts):
        draws = jax.random.uniform(jax.random.fold_in(jax.random.fold_in(own_key, 6), dim), (parts,), jnp.float32, low / len(pieces), largest / len(pieces))
        return jnp.repeat(jnp.exp(draws), shape[dim] // parts).reshape((-1,) + (1,) * (len(shape) - dim - 1))

    level = one(*pieces[0])
    for cut in pieces[1:]:
        level = level * one(*cut)
    return level


def bell_draw(rng, extent, width, most, pieces=(), held_as=jnp.bfloat16):
    array = width * jax.random.normal(rng, extent, jnp.float32)
    if pieces:
        array = array * level_of(rng, extent, pieces, -0.22, 0.18)
    return jnp.clip(array, -most, most).astype(held_as)


def setup_inputs(seed: int = 0) -> dict:
    key_of = jax.random.split(jax.random.key(seed), 34)
    inputs = bell_draw(key_of[0], (MICRO, F, GRID), 1.0, 6.0, ((2, 16),))
    targets = bell_draw(key_of[1], (MICRO, F, GRID), 1.0, 6.0, ((2, 16),), jnp.float32)
    senders = touch_ends(jax.random.randint(key_of[2], (MICRO, EDGES), 0, NODE_DEV * 3 // 2), jax.random.fold_in(key_of[2], 1), 0, (NODE_DEV * 3 // 2) - 1).astype(jnp.int32)
    receivers = touch_ends(jax.random.randint(key_of[3], (MICRO, EDGES), 0, NODE_DEV), jax.random.fold_in(key_of[3], 1), 0, NODE_DEV - 1).astype(jnp.int32)
    g2m_dst = touch_ends(jax.random.randint(key_of[4], (MICRO, GRID), 0, NODE_DEV), jax.random.fold_in(key_of[4], 1), 0, NODE_DEV - 1).astype(jnp.int32)
    m2g_src = touch_ends(jax.random.randint(key_of[5], (MICRO, 3, GRID), 0, NODE_DEV), jax.random.fold_in(key_of[5], 1), 0, NODE_DEV - 1).astype(jnp.int32)
    delta_scale = jnp.clip(jnp.exp(jax.random.uniform(key_of[6], (F,), jnp.float32, math.log(0.5), math.log(2.0))), 0.5, 2.0)
    level_index = touch_ends(jax.random.randint(key_of[7], (F,), 0, LEVELS), jax.random.fold_in(key_of[7], 1), 0, LEVELS - 1).astype(jnp.int32)
    step_count = jax.random.randint(key_of[8], (), 2, 21).astype(jnp.int32)
    soap_owner = draw_soap_owner(jax.random.fold_in(key_of[33], 71), 0)
    edge_first = bell_draw(key_of[10], (LAYERS, 3 * L, L), (3 * L) ** -0.5, 0.21875, ((2, 2),), jnp.float32)
    node_first = bell_draw(key_of[11], (LAYERS, 2 * L, L), (2 * L) ** -0.5, 0.25, ((2, 2),), jnp.float32)
    second = bell_draw(key_of[12], (2 * LAYERS, L, L), L ** -0.5, 0.375, ((1, 2),), jnp.float32)
    io_weights = bell_draw(key_of[13], (2, F, L), L ** -0.5, 0.375, (), jnp.float32)
    vectors = jnp.clip(1.0 + 0.15 * jax.random.normal(key_of[14], (VEC, L), jnp.float32), 0.25, 1.75)
    edge_first_m = bell_draw(key_of[15], (LAYERS, 3 * L, L), (5.7e-8), 3.5762786865234375e-07, (), jnp.float32)
    node_first_m = bell_draw(key_of[16], (LAYERS, 2 * L, L), (5.7e-8), 3.5762786865234375e-07, (), jnp.float32)
    second_m = bell_draw(key_of[17], (2 * LAYERS, L, L), (5.7e-8), 3.5762786865234375e-07, (), jnp.float32)
    edge_first_v = jnp.clip(jnp.exp(jax.random.uniform(key_of[18], (LAYERS, 3 * L, L), jnp.float32, math.log(2.6000000306073074e-15), math.log(1.0499999985149125e-14))), 2.6000000306073074e-15, 1.0499999985149125e-14)
    node_first_v = jnp.clip(jnp.exp(jax.random.uniform(key_of[19], (LAYERS, 2 * L, L), jnp.float32, math.log(2.6000000306073074e-15), math.log(1.0499999985149125e-14))), 2.6000000306073074e-15, 1.0499999985149125e-14)
    second_v = jnp.clip(jnp.exp(jax.random.uniform(key_of[20], (2 * LAYERS, L, L), jnp.float32, math.log(2.6000000306073074e-15), math.log(1.0499999985149125e-14))), 2.6000000306073074e-15, 1.0499999985149125e-14)
    io_m = bell_draw(key_of[21], (2, F, L), (5.7e-8), 3.5762786865234375e-07, (), jnp.float32)
    io_v = jnp.clip(jnp.exp(jax.random.uniform(key_of[22], (2, F, L), jnp.float32, math.log(2.6000000306073074e-15), math.log(1.0499999985149125e-14))), 2.6000000306073074e-15, 1.0499999985149125e-14)
    vector_m = bell_draw(key_of[23], (VEC, L), (1.7e-7), 9.5367431640625e-07, (), jnp.float32)
    vector_v = jnp.clip(jnp.exp(jax.random.uniform(key_of[24], (VEC, L), jnp.float32, math.log(2.3999999240026902e-14), math.log(9.499999663884276e-14))), 2.3999999240026902e-14, 9.499999663884276e-14)
    edge_left_stat = draw_edge_left_stat(jax.random.fold_in(key_of[33], 71), 0)
    edge_left_basis = draw_edge_left_basis(jax.random.fold_in(key_of[33], 71), 0)
    node_left_stat = draw_node_left_stat(jax.random.fold_in(key_of[33], 71), 0)
    node_left_basis = draw_node_left_basis(jax.random.fold_in(key_of[33], 71), 0)
    second_left_stat = draw_second_left_stat(jax.random.fold_in(key_of[33], 71), 0)
    second_left_basis = draw_second_left_basis(jax.random.fold_in(key_of[33], 71), 0)
    right_stat = draw_right_stat(jax.random.fold_in(key_of[33], 71), 0)
    right_basis = draw_right_basis(jax.random.fold_in(key_of[33], 71), 0)
    return {"inputs": inputs, "targets": targets, "senders": senders, "receivers": receivers, "g2m_dst": g2m_dst, "m2g_src": m2g_src, "delta_scale": delta_scale, "level_index": level_index, "step_count": step_count, "soap_owner": soap_owner, "edge_first": edge_first, "node_first": node_first, "second": second, "io_weights": io_weights, "vectors": vectors, "edge_first_m": edge_first_m, "node_first_m": node_first_m, "second_m": second_m, "edge_first_v": edge_first_v, "node_first_v": node_first_v, "second_v": second_v, "io_m": io_m, "io_v": io_v, "vector_m": vector_m, "vector_v": vector_v, "edge_left_stat": edge_left_stat, "edge_left_basis": edge_left_basis, "node_left_stat": node_left_stat, "node_left_basis": node_left_basis, "second_left_stat": second_left_stat, "second_left_basis": second_left_basis, "right_stat": right_stat, "right_basis": right_basis}


HIGH = lax.Precision.HIGHEST
CLIP = 0.0005
BETA_ONE = 0.9
BETA_TWO = 0.99
STAT_BETA = 0.95
EPSILON = 1e-08
RATE = 0.15
VECTOR_RATE = 0.7
DECAY = 0.01

@jax.custom_vjp
def low(v):
    return lax.optimization_barrier(v.astype(jnp.bfloat16)).astype(jnp.float32)

@jax.custom_vjp
def low_back(v):
    return v

def low_keep(v):
    return (low(v), None)

def low_pass(kept, grad):
    return (grad,)

def back_keep(v):
    return (v, None)

def back_low(kept, grad):
    return (low(grad),)
low.defvjp(low_keep, low_pass)
low_back.defvjp(back_keep, back_low)

def layer_norm(value, gain, bias):
    shape = (-1,) + (1,) * (value.ndim - 1)
    mean = lax.optimization_barrier(jnp.mean(value, axis=0, keepdims=True))
    centred = value - mean
    var = lax.optimization_barrier(jnp.mean(centred * centred, axis=0, keepdims=True))
    return centred * lax.rsqrt(var + 1e-05) * gain.reshape(shape) + bias.reshape(shape)

def take_cols(values, index):
    return jnp.take_along_axis(values, index[None], axis=2)

def seg_sum(values, index, count):
    blocks = values.shape[1]
    flat = (index + jnp.arange(blocks, dtype=jnp.int32)[:, None] * count).reshape(-1)
    rows = jnp.moveaxis(values, 0, -1).reshape(-1, values.shape[0])
    summed = jax.ops.segment_sum(rows, flat, num_segments=blocks * count)
    return jnp.moveaxis(summed.reshape(blocks, count, values.shape[0]), -1, 0)

def mlp(inner, first, second):
    span = first.shape[1] // N_MP
    total = 0.0
    for group in range(N_MP):
        piece = low_back(inner)
        pre = low_back(jnp.einsum('ih,idr->hdr', low(first[:, group * span:(group + 1) * span]), piece, precision=HIGH))
        hidden = low(jax.nn.silu(pre))
        total = total + low(jnp.einsum('hl,hdr->ldr', low(second[group * span:(group + 1) * span]), hidden, precision=HIGH))
    return low_back(total)

def forward_loss(edge_first, node_first, second, io_weights, vectors, inputs, targets, senders, receivers, g2m_dst, m2g_src, delta_scale, level_index):
    blocks = N_DP
    level_weight = (level_index + 1).astype(jnp.float32) / LEVELS
    weight_in = low(io_weights[0])
    weight_out = low(io_weights[1])
    total = 0.0
    for batch in range(MICRO):
        fields = inputs[batch].reshape(F, blocks, GRID_DEV)
        goal = targets[batch].reshape(F, blocks, GRID_DEV) / delta_scale[:, None, None]
        send = senders[batch].reshape(blocks, EDGE_DEV)
        recv = receivers[batch].reshape(blocks, EDGE_DEV)
        grid = low_back(jnp.einsum('fl,fdg->ldg', weight_in, fields, precision=HIGH))
        encoded = low_back(seg_sum(low(grid), g2m_dst[batch].reshape(blocks, GRID_DEV), NODE_DEV))
        mesh = layer_norm(encoded, vectors[0], vectors[1])
        edge = None
        for layer in range(LAYERS):
            mesh_b = low(mesh)
            extended = jnp.concatenate([mesh_b, jnp.roll(mesh_b, 1, axis=1)], axis=2)
            sent = low_back(take_cols(extended, send))
            recv_side = low_back(take_cols(mesh_b, recv))
            if layer == 0:
                edge = sent - recv_side
            edge_total = mlp(jnp.concatenate([low(edge), sent, recv_side], axis=0), edge_first[layer], second[2 * layer])
            edge = edge + layer_norm(edge_total, vectors[2 + 4 * layer], vectors[3 + 4 * layer])
            gathered = low_back(seg_sum(low(edge), recv, NODE_DEV))
            node_total = mlp(jnp.concatenate([mesh_b, low(gathered)], axis=0), node_first[layer], second[2 * layer + 1])
            mesh = mesh + layer_norm(node_total, vectors[4 + 4 * layer], vectors[5 + 4 * layer])
        mesh_b = low(mesh)
        decoded = 0.0
        for source in range(3):
            decoded = decoded + take_cols(mesh_b, m2g_src[batch, source].reshape(blocks, GRID_DEV))
        decoded = low_back(decoded)
        final = grid + layer_norm(decoded, vectors[VEC - 2], vectors[VEC - 1])
        pred = low_back(jnp.einsum('fl,ldg->fdg', weight_out, low(final), precision=HIGH))
        resid = pred - goal
        total = total + jnp.sum(level_weight[:, None, None] * resid * resid)
    return total / (MICRO * F * GRID_DEV * N_DP)

def orthonormal(matrix):
    gram = jnp.einsum('bij,bik->bjk', matrix, matrix, precision=HIGH)
    lower = jnp.linalg.cholesky(gram)
    return jnp.swapaxes(jax.scipy.linalg.solve_triangular(lower, jnp.swapaxes(matrix, 1, 2), lower=True), 1, 2)

def rotate(left, matrix, right):
    return jnp.einsum('bia,bic->bac', left, jnp.einsum('bij,bjc->bic', matrix, right, precision=HIGH), precision=HIGH)

def soap_step(grad, moment, second_moment, left_stat, left_basis, right_stat, right_basis, corr_one, corr_two):
    left_stat = STAT_BETA * left_stat + (1.0 - STAT_BETA) * jnp.einsum('bij,bkj->bik', grad, grad, precision=HIGH)
    right_stat = STAT_BETA * right_stat + (1.0 - STAT_BETA) * jnp.einsum('bji,bjk->bik', grad, grad, precision=HIGH)
    left_basis = orthonormal(jnp.einsum('bij,bjk->bik', left_stat, left_basis, precision=HIGH))
    right_basis = orthonormal(jnp.einsum('bij,bjk->bik', right_stat, right_basis, precision=HIGH))
    moment = BETA_ONE * moment + (1.0 - BETA_ONE) * grad
    rot_grad = rotate(left_basis, grad, right_basis)
    second_moment = BETA_TWO * second_moment + (1.0 - BETA_TWO) * rot_grad * rot_grad
    normed = rotate(left_basis, moment, right_basis) / corr_one / (jnp.sqrt(second_moment / corr_two) + EPSILON)
    update = jnp.einsum('bia,bac->bic', left_basis, jnp.einsum('bac,bjc->baj', normed, right_basis, precision=HIGH), precision=HIGH)
    return (update, moment, second_moment)

def adamw(weight, grad, moment, second_moment, corr_one, corr_two, decay, rate):
    moment = BETA_ONE * moment + (1.0 - BETA_ONE) * grad
    second_moment = BETA_TWO * second_moment + (1.0 - BETA_TWO) * grad * grad
    weight = weight - rate * (moment / corr_one / (jnp.sqrt(second_moment / corr_two) + EPSILON) + decay * weight)
    return (weight, moment, second_moment)

def reference(inputs, targets, senders, receivers, g2m_dst, m2g_src, delta_scale, level_index, step_count, soap_owner, edge_first, node_first, second, io_weights, vectors, edge_first_m, node_first_m, second_m, edge_first_v, node_first_v, second_v, io_m, io_v, vector_m, vector_v, edge_left_stat, edge_left_basis, node_left_stat, node_left_basis, second_left_stat, second_left_basis, right_stat, right_basis):
    fields_all = inputs.astype(jnp.float32)

    def loss_of(p_edge, p_node, p_second, p_io, p_vec, p_fields):
        return forward_loss(p_edge, p_node, p_second, p_io, p_vec, p_fields, targets, senders, receivers, g2m_dst, m2g_src, delta_scale, level_index)
    loss, back = jax.vjp(loss_of, edge_first, node_first, second, io_weights, vectors, fields_all)
    every = back(jnp.ones_like(loss))
    grads = every[:5]
    input_grad = every[5] * (MICRO * F * GRID_DEV * N_DP)
    squares = jnp.float32(0.0)
    for grad in grads:
        squares = squares + jnp.sum(grad * grad)
    grad_norm = jnp.sqrt(squares)
    clip = jnp.minimum(1.0, CLIP / (grad_norm + 1e-06))
    clipped = [grad * clip for grad in grads]
    steps = step_count.astype(jnp.float32)
    corr_one = 1.0 - jnp.power(BETA_ONE, steps)
    corr_two = 1.0 - jnp.power(BETA_TWO, steps)
    upd_edge, m_edge, v_edge = soap_step(clipped[0], edge_first_m, edge_first_v, edge_left_stat, edge_left_basis, right_stat[:LAYERS], right_basis[:LAYERS], corr_one, corr_two)
    upd_node, m_node, v_node = soap_step(clipped[1], node_first_m, node_first_v, node_left_stat, node_left_basis, right_stat[LAYERS:2 * LAYERS], right_basis[LAYERS:2 * LAYERS], corr_one, corr_two)
    upd_second, m_second, v_second = soap_step(clipped[2], second_m, second_v, second_left_stat, second_left_basis, right_stat[2 * LAYERS:], right_basis[2 * LAYERS:], corr_one, corr_two)
    new_edge = edge_first - RATE * (upd_edge + DECAY * edge_first)
    new_node = node_first - RATE * (upd_node + DECAY * node_first)
    new_second = second - RATE * (upd_second + DECAY * second)
    new_io, m_io, v_io = adamw(io_weights, clipped[3], io_m, io_v, corr_one, corr_two, DECAY, RATE)
    new_vec, m_vec, v_vec = adamw(vectors, clipped[4], vector_m, vector_v, corr_one, corr_two, 0.0, VECTOR_RATE)
    return (loss, grad_norm, new_edge, new_edge.astype(jnp.bfloat16), new_node, new_node.astype(jnp.bfloat16), new_second, new_second.astype(jnp.bfloat16), new_io, new_io.astype(jnp.bfloat16), new_vec, new_vec.astype(jnp.bfloat16), m_edge, m_node, m_second, v_edge, v_node, v_second, m_io, v_io, m_vec, v_vec, input_grad)
```

```python
import functools

import jax
import jax.numpy as jnp
from jax import lax
from jax.experimental import pallas as pl
from jax.experimental.pallas import tpu as pltpu
from jax.sharding import PartitionSpec as P

LEVELS = 13
NODE_DEV = 512
CLIP = 0.0005
BETA_ONE = 0.9
BETA_TWO = 0.99
STAT_BETA = 0.95
EPSILON = 1e-08
RATE = 0.15
VECTOR_RATE = 0.7
DECAY = 0.01
HIGH = lax.Precision.HIGHEST

BLOCK = 128
AHEAD = 4
STAT_SCALE = 2.0**28
HALF = 512
CHIPS = 4
PLANE = 8


def mm(a, b, lhs=1, rhs=0):
    return lax.dot_general(
        a, b, (((lhs,), (rhs,)), ((), ())), precision=HIGH, preferred_element_type=jnp.float32
    )


def inverse_factors(blocks):
    tiles = BLOCK // 8
    shape = (8, BLOCK)
    lane = lax.broadcasted_iota(jnp.int32, shape, 1)
    sub = lax.broadcasted_iota(jnp.int32, shape, 0)
    eye = [jnp.where(lane == sub + 8 * t, 1.0, 0.0).astype(jnp.float32) for t in range(tiles)]
    states = []
    for block in blocks:
        rows = [block[8 * t : 8 * t + 8, :] for t in range(tiles)]
        cols = {
            j: [jnp.broadcast_to(rows[t][:, j : j + 1], shape) for t in range(tiles)]
            for j in range(AHEAD)
        }
        states.append((rows, list(eye), cols))
    for j in range(BLOCK):
        first, s = divmod(j, 8)
        for rows, inv, cols in states:
            col = cols.pop(j)
            pivot = jnp.broadcast_to(col[first][s : s + 1, :], shape)
            recip = 1.0 / pivot
            row = jnp.broadcast_to(rows[first][s : s + 1, :], shape)
            inv_row = jnp.broadcast_to(inv[first][s : s + 1, :], shape)
            factor = [None] * tiles
            for t in range(first, tiles):
                factor[t] = col[t] * recip
            factor[first] = jnp.where(sub > s, factor[first], 0.0)
            for ahead in range(j + 1, min(j + AHEAD, BLOCK)):
                entry = jnp.broadcast_to(cols[ahead][first][s : s + 1, :], shape)
                for t in range(first, tiles):
                    cols[ahead][t] = cols[ahead][t] - factor[t] * entry
            for t in range(first, tiles):
                rows[t] = rows[t] - factor[t] * row
                inv[t] = inv[t] - factor[t] * inv_row
            if j + AHEAD < BLOCK:
                at = j + AHEAD
                cols[at] = [
                    jnp.broadcast_to(rows[t][:, at : at + 1], shape) if t >= first else None
                    for t in range(tiles)
                ]
    results = []
    for rows, inv, cols in states:
        scaled = []
        for t in range(tiles):
            diag = jnp.sum(rows[t] * eye[t], axis=1, keepdims=True)
            scaled.append(inv[t] * lax.rsqrt(diag))
        results.append(jnp.concatenate(scaled, axis=0))
    return results


def soap_kernel(
    sizes,
    where_ref,
    scal_ref,
    half_ref,
    tail_ref,
    m0, m1, m2,
    v0, v1, v2,
    ls0, ls1, ls2,
    lb0, lb1, lb2,
    rs_hbm,
    rb_hbm,
    rot_ref,
    upd_ref,
    stat,
    basis,
    both,
    second,
    rstat,
    rbasis,
    table,
    inv,
    rgram,
    rinv,
    sems,
):
    order = stat.shape[0]
    width = rstat.shape[0]
    blocks = order // BLOCK
    kind = where_ref[0]
    index = where_ref[1]
    matrix = where_ref[2]
    copies = []
    for k, (size, mom, sec, left, base) in enumerate(
        zip(sizes, (m0, m1, m2), (v0, v1, v2), (ls0, ls1, ls2), (lb0, lb1, lb2))
    ):
        @pl.when(kind == k)
        def _():
            if size < order:
                row = lax.broadcasted_iota(jnp.int32, (order, order), 0)
                col = lax.broadcasted_iota(jnp.int32, (order, order), 1)
                unit = jnp.where(row == col, 1.0, 0.0).astype(jnp.float32)
                stat[...] = unit * (1.0 / STAT_SCALE)
                basis[...] = unit
                both[...] = jnp.zeros_like(both)
                second[...] = jnp.zeros_like(second)
            todo = [
                pltpu.make_async_copy(left.at[index], stat.at[pl.ds(0, size), pl.ds(0, size)], sems.at[0]),
                pltpu.make_async_copy(base.at[index], basis.at[pl.ds(0, size), pl.ds(0, size)], sems.at[1]),
                pltpu.make_async_copy(
                    mom.at[index], both.at[pl.ds(0, size), pl.ds(width, width)], sems.at[2]
                ),
                pltpu.make_async_copy(sec.at[index], second.at[pl.ds(0, size)], sems.at[3]),
                pltpu.make_async_copy(rs_hbm.at[matrix], rstat, sems.at[4]),
                pltpu.make_async_copy(rb_hbm.at[matrix], rbasis, sems.at[5]),
            ]
            for copy in todo:
                copy.start()
            held = HALF if k < 2 else width
            first = 0 if k < 2 else HALF - width
            both[:held, :width] = half_ref[first:, :].astype(jnp.float32)
            if size > HALF:
                both[HALF:size, :width] = tail_ref[: size - HALF, :].astype(jnp.float32)
            for copy in todo:
                copy.wait()

    clip, corr_one, corr_two = scal_ref[0], scal_ref[1], scal_ref[2]
    grad = both[:, :width] * clip
    both[:, :width] = grad
    both[:, width:] = BETA_ONE * both[:, width:] + (1.0 - BETA_ONE) * grad
    keep, fresh = STAT_SCALE * STAT_BETA, STAT_SCALE * (1.0 - STAT_BETA)
    stat[...] = keep * stat[...] + fresh * mm(grad, grad, 1, 1)
    rstat[...] = keep * rstat[...] + fresh * mm(grad, grad, 0, 0)
    table[:, :order] = mm(basis[...], stat[...], 0, 0)
    table[:, order:] = mm(table[:, :order], both[...])
    basis[...] = mm(stat[...], basis[...])
    stat[...] = basis[...]
    table[:, :order] = mm(table[:, :order], table[:, :order], 1, 1)
    rbasis[...] = mm(rstat[...], rbasis[...])
    rgram[...] = mm(rbasis[...], rbasis[...], 0, 0)

    def panel(k):
        at = pl.ds(pl.multiple_of(k * BLOCK, BLOCK), BLOCK)
        table[at, :] = mm(inv[at, :], table[at, :])

        def trail(i, carry):
            rows = pl.ds(pl.multiple_of(i * BLOCK, BLOCK), BLOCK)
            table[rows, :] = table[rows, :] - mm(table[at, rows], table[at, :], 0, 0)
            return carry

        lax.fori_loop(k + 1, blocks, trail, 0)

    def two(k, carry):
        at = pl.ds(pl.multiple_of(k * BLOCK, BLOCK), BLOCK)
        inv[at, :], rinv[at, :] = inverse_factors([table[at, at], rgram[at, at]])

        @pl.when(k == 0)
        def _():
            upper = mm(rinv[:BLOCK, :], rgram[:BLOCK, BLOCK:])
            rgram[:BLOCK, BLOCK:] = upper
            rgram[BLOCK:, BLOCK:] = rgram[BLOCK:, BLOCK:] - mm(upper, upper, 0, 0)

        panel(k)
        return carry

    def one(k, carry):
        at = pl.ds(pl.multiple_of(k * BLOCK, BLOCK), BLOCK)
        inv[at, :] = inverse_factors([table[at, at]])[0]
        panel(k)
        return carry

    lax.fori_loop(0, width // BLOCK, two, 0)
    lax.fori_loop(width // BLOCK, blocks, one, 0)
    left_part = mm(rbasis[:, :BLOCK], rinv[:BLOCK, :], 1, 1)
    right_part = mm(
        rbasis[:, BLOCK:] - mm(left_part, rgram[:BLOCK, BLOCK:]), rinv[BLOCK:, :], 1, 1
    )
    rbasis[:, :BLOCK] = left_part
    rbasis[:, BLOCK:] = right_part
    rot = mm(table[:, order : order + width], rbasis[...])
    rot_ref[...] = rot.astype(rot_ref.dtype)
    moment = mm(table[:, order + width :], rbasis[...])
    grown = BETA_TWO * second[...] + (1.0 - BETA_TWO) * rot * rot
    normed = moment / corr_one / (jnp.sqrt(grown / corr_two) + EPSILON)
    second[...] = mm(normed, rbasis[...], 1, 1)

    def back(step, carry):
        k = blocks - 1 - step
        at = pl.ds(pl.multiple_of(k * BLOCK, BLOCK), BLOCK)
        part = mm(inv[at, :], second[at, :], 0, 0)
        both[at, :width] = part
        second[...] = second[...] - mm(table[:, at], part)
        return carry

    lax.fori_loop(0, blocks, back, 0)
    update = mm(stat[...], both[:, :width]).astype(upd_ref.dtype)
    upd_ref[0] = update[:, : width // 2]
    upd_ref[1] = update[:, width // 2 :]


def soap(where, scal, half, tail, moms, seconds, lefts, bases, rstat, rbasis, out_dtype):
    order = max(a.shape[1] for a in lefts)
    width = rstat.shape[1]
    sizes = tuple(a.shape[1] for a in lefts)
    f32 = jnp.float32
    any_ = pl.BlockSpec(memory_space=pl.ANY)
    smem = pl.BlockSpec(memory_space=pltpu.SMEM)
    vmem = pl.BlockSpec(memory_space=pltpu.VMEM)
    return pl.pallas_call(
        functools.partial(soap_kernel, sizes),
        out_shape=[
            jax.ShapeDtypeStruct((order, width), out_dtype),
            jax.ShapeDtypeStruct((2, order, width // 2), out_dtype),
        ],
        in_specs=[smem, smem, vmem, vmem] + [any_] * 14,
        out_specs=[vmem, vmem],
        scratch_shapes=[
            pltpu.VMEM((order, order), f32),
            pltpu.VMEM((order, order), f32),
            pltpu.VMEM((order, 2 * width), f32),
            pltpu.VMEM((order, width), f32),
            pltpu.VMEM((width, width), f32),
            pltpu.VMEM((width, width), f32),
            pltpu.VMEM((order, order + 2 * width), f32),
            pltpu.VMEM((order, BLOCK), f32),
            pltpu.VMEM((width, width), f32),
            pltpu.VMEM((width, BLOCK), f32),
            pltpu.SemaphoreType.DMA((6,)),
        ],
        compiler_params=pltpu.CompilerParams(vmem_limit_bytes=56 * 2**20),
        name="soap",
    )(where, scal, half, tail, *moms, *seconds, *lefts, *bases, rstat, rbasis)


def place():
    dp = lax.axis_index("dp")
    core = lax.rem(dp, 2)
    chip = 2 * lax.axis_index("mp") + lax.rem(lax.div(dp, 2), 2)
    return core, chip, 2 * chip + core, lax.div(dp, 4), lax.axis_size("dp") // 4


def device(core, chip, group):
    return (4 * group + 2 * lax.rem(chip, 2) + core, lax.div(chip, 2))


def other(core, chip, turn):
    spot = lax.rem(2 * chip + core + turn, PLANE)
    return lax.rem(spot, 2), lax.div(spot, 2), spot


def remote(src, dst, send, recv, target):
    return pltpu.make_async_remote_copy(
        src_ref=src, dst_ref=dst, send_sem=send, recv_sem=recv, device_id=target,
        device_id_type=pl.DeviceIdType.MESH,
    )


def greet(targets):
    barrier = pltpu.get_barrier_semaphore()
    for target in targets:
        pl.semaphore_signal(
            barrier, inc=1, device_id=target, device_id_type=pl.DeviceIdType.MESH
        )
    pl.semaphore_wait(barrier, len(targets))


def fold(value):
    rows = jnp.sum(value.reshape(value.shape[0] // 8, 8, value.shape[1]), axis=0)
    return rows[:, :128] + rows[:, 128:]


def reduce_kernel(
    e0, e1, n0, n1, s0, s1, s2, s3, extra, loss_ref,
    half_ref, tail_ref, norm_ref, total_ref,
    from_core, acc, from_plane, part, from_group, full, tail,
    plane_loss, group_loss, plane_norm,
    core_s, core_r, plane_s, plane_r, group_s, group_r, full_s, full_r, tail_s, tail_r,
    ploss_s, ploss_r, gloss_s, gloss_r, norm_s, norm_r,
):
    f32, bf16 = jnp.float32, jnp.bfloat16
    core, chip, spot, group, groups = place()
    rows = HALF // groups
    partner = device(1 - core, chip, group)
    plane = [device(*other(core, chip, t)[:2], group) for t in range(1, PLANE)]
    along = [device(core, chip, lax.rem(group + t, groups)) for t in range(1, groups)]
    greet(plane + along)

    quarter = HALF // 2
    pieces = {0: [[(ref, 0, HALF, 0)] for ref in (e0, e1, n0, n1)], 1: []}
    for p, (ref, begin) in enumerate(((e0, HALF), (e1, HALF), (extra, 0), (extra, quarter))):
        pieces[1].append([(ref, begin, quarter, 0), ((s0, s1, s2, s3)[p], 0, quarter, quarter)])

    def core_copy(p, i, piece):
        ref, begin, size, to = piece
        return remote(
            ref.at[pl.ds(begin, size)], from_core.at[p, pl.ds(to, size)],
            core_s.at[p, i], core_r.at[p, i], partner,
        )

    for c in range(2):
        @pl.when(core == c)
        def _():
            for p in range(CHIPS):
                for i, piece in enumerate(pieces[1 - c][p]):
                    core_copy(p, i, piece).start()

    loss_sends = []
    for t in range(1, PLANE):
        copy = remote(
            loss_ref, plane_loss.at[spot], ploss_s.at[t - 1], ploss_r.at[spot], plane[t - 1]
        )
        copy.start()
        loss_sends.append(copy)
    plane_loss[spot] = loss_ref[...]

    def chunk(index):
        return pl.ds(pl.multiple_of(index * rows, rows), rows)

    def plane_copy(p, turn, index):
        return remote(
            acc.at[p, chunk(index)], from_plane.at[turn - 1, chunk(index)],
            plane_s.at[index, turn - 1], plane_r.at[index, turn - 1], device(core, p, group),
        )

    for p in range(CHIPS):
        for c in range(2):
            @pl.when(core == c)
            def _():
                for i, piece in enumerate(pieces[c][p]):
                    ref, begin, size, to = piece
                    core_copy(p, i, piece).wait_recv()
                    total = ref[begin : begin + size, :].astype(f32) + from_core[
                        p, to : to + size, :
                    ].astype(f32)
                    acc[p, to : to + size, :] = total.astype(bf16)
        turn = lax.rem(p - chip + CHIPS, CHIPS)

        @pl.when(turn != 0)
        def _():
            def go(i, carry):
                plane_copy(p, turn, lax.rem(group + i, groups)).start()
                return carry

            lax.fori_loop(1, groups + 1, go, 0)

    for t in range(1, PLANE):
        _, _, source = other(core, chip, t)
        remote(
            loss_ref, plane_loss.at[source], ploss_s.at[t - 1], ploss_r.at[source], partner
        ).wait_recv()
    total = plane_loss[0]
    for t in range(1, PLANE):
        total = total + plane_loss[t]
    group_loss[group] = total
    for t in range(1, groups):
        copy = remote(
            group_loss.at[group], group_loss.at[group], gloss_s.at[t - 1], gloss_r.at[group],
            along[t - 1],
        )
        copy.start()
        loss_sends.append(copy)

    def gather_plane(index):
        total = acc[chip, chunk(index), :].astype(f32)
        for turn in range(1, CHIPS):
            plane_copy(chip, turn, index).wait_recv()
            total = total + from_plane[turn - 1, chunk(index), :].astype(f32)
        return total

    def group_copy(turn):
        target = lax.rem(group + turn, groups)
        return remote(
            part.at[chunk(target)], from_group.at[turn - 1], group_s.at[turn - 1],
            group_r.at[turn - 1], device(core, chip, target),
        )

    def plane_step(turn, carry):
        target = lax.rem(group + turn, groups)
        part[chunk(target), :] = gather_plane(target).astype(bf16)
        group_copy(turn).start()
        return carry

    lax.fori_loop(1, groups, plane_step, 0)

    def group_step(turn, total):
        group_copy(turn).wait_recv()
        return total + from_group[turn - 1].astype(f32)

    total = lax.fori_loop(1, groups, group_step, gather_plane(group))
    full[chunk(group), :] = total.astype(bf16)

    def full_copy(turn, owner, target):
        return remote(
            full.at[chunk(owner)], full.at[chunk(owner)], full_s.at[turn - 1],
            full_r.at[turn - 1], device(core, chip, target),
        )

    def full_go(turn, carry):
        full_copy(turn, group, lax.rem(group + turn, groups)).start()
        return carry

    def full_wait(turn, carry):
        full_copy(turn, lax.rem(group + groups - turn, groups), group).wait_recv()
        return carry

    lax.fori_loop(1, groups, full_go, 0)
    lax.fori_loop(1, groups, full_wait, 0)

    swap = remote(full.at[pl.ds(0, quarter)], tail, tail_s, tail_r, partner)
    swap.start()
    squares = full[...].astype(f32)
    plane_norm[spot] = fold(squares * squares)
    norm_sends = []
    for t in range(1, PLANE):
        copy = remote(
            plane_norm.at[spot], plane_norm.at[spot], norm_s.at[t - 1], norm_r.at[spot],
            plane[t - 1],
        )
        copy.start()
        norm_sends.append(copy)
    half_ref[...] = full[...]
    for t in range(1, groups):
        source = lax.rem(group + t, groups)
        remote(
            group_loss.at[source], group_loss.at[source], gloss_s.at[t - 1], gloss_r.at[source],
            partner,
        ).wait_recv()
    total = group_loss[0]
    for t in range(1, groups):
        total = total + group_loss[t]
    total_ref[...] = total
    for t in range(1, PLANE):
        _, _, source = other(core, chip, t)
        remote(
            plane_norm.at[source], plane_norm.at[source], norm_s.at[t - 1], norm_r.at[source],
            partner,
        ).wait_recv()
    total = plane_norm[0]
    for t in range(1, PLANE):
        total = total + plane_norm[t]
    norm_ref[...] = total
    swap.wait_recv()
    tail_ref[...] = tail[...]

    swap.wait_send()
    for copy in loss_sends + norm_sends:
        copy.wait_send()
    for c in range(2):
        @pl.when(core == c)
        def _():
            for p in range(CHIPS):
                for i, piece in enumerate(pieces[1 - c][p]):
                    core_copy(p, i, piece).wait_send()
    def plane_done(index, carry):
        for turn in range(1, CHIPS):
            plane_copy(lax.rem(chip + turn, CHIPS), turn, index).wait_send()
        return carry

    lax.fori_loop(0, groups, plane_done, 0)

    def group_done(turn, carry):
        group_copy(turn).wait_send()
        full_copy(turn, group, group).wait_send()
        return carry

    lax.fori_loop(1, groups, group_done, 0)


def reduce_grads(firsts, seconds, extra, loss):
    groups = lax.axis_size("dp") // 4
    width = extra.shape[1]
    f32, bf16 = jnp.float32, jnp.bfloat16
    rows = HALF // groups
    away = max(groups - 1, 1)
    dma = pltpu.SemaphoreType.DMA
    vmem = pl.BlockSpec(memory_space=pltpu.VMEM)
    tile = (8, 128)
    return pl.pallas_call(
        reduce_kernel,
        out_shape=[
            jax.ShapeDtypeStruct((HALF, width), bf16),
            jax.ShapeDtypeStruct((HALF // 2, width), bf16),
            jax.ShapeDtypeStruct(tile, f32),
            jax.ShapeDtypeStruct(tile, f32),
        ],
        in_specs=[vmem] * 10,
        out_specs=[vmem] * 4,
        scratch_shapes=[
            pltpu.VMEM((CHIPS, HALF, width), bf16),
            pltpu.VMEM((CHIPS, HALF, width), bf16),
            pltpu.VMEM((CHIPS - 1, HALF, width), bf16),
            pltpu.VMEM((HALF, width), bf16),
            pltpu.VMEM((away, rows, width), bf16),
            pltpu.VMEM((HALF, width), bf16),
            pltpu.VMEM((HALF // 2, width), bf16),
            pltpu.VMEM((PLANE, *tile), f32),
            pltpu.VMEM((groups, *tile), f32),
            pltpu.VMEM((PLANE, *tile), f32),
            dma((CHIPS, 2)), dma((CHIPS, 2)),
            dma((groups, CHIPS - 1)), dma((groups, CHIPS - 1)),
            dma((away,)), dma((away,)), dma((away,)), dma((away,)),
            dma(()), dma(()),
            dma((PLANE - 1,)), dma((PLANE,)),
            dma((away,)), dma((groups,)),
            dma((PLANE - 1,)), dma((PLANE,)),
        ],
        compiler_params=pltpu.CompilerParams(collective_id=0, has_side_effects=True),
        name="reduce_grads",
    )(*firsts, *seconds, extra, loss)


def gather_kernel(
    half_ref, rot_ref, upd_ref,
    gall, rall, ufirst, usecond,
    far_s, far_r, near_s, near_r,
):
    core, chip, spot, group, groups = place()
    width = half_ref.shape[1]
    partner = device(1 - core, chip, group)
    peers = [device(core, lax.rem(chip + t, CHIPS), group) for t in range(1, CHIPS)]
    greet(peers + [partner])

    def tall(p):
        return 3 * width if p < 2 else HALF

    def spots(c, p):
        if c == 0:
            rows = pl.ds(0, tall(p))
            return (gall.at[p, pl.ds(0, HALF)], rall.at[p, rows], ufirst.at[p, rows])
        return (
            gall.at[p, pl.ds(HALF, HALF)], rall.at[p, pl.ds(3 * width, width)], usecond.at[p]
        )

    def own(c, p, member):
        if c == 0:
            rows = pl.ds(0, tall(p))
            return (half_ref, rot_ref.at[rows], upd_ref.at[member, rows])
        side = pl.ds(pl.multiple_of(member * (width // 2), width // 2), width // 2)
        return (half_ref, rot_ref.at[pl.ds(0, width)], upd_ref.at[:, side])

    def branches(wanted=None):
        for c in range(2):
            for p in range(CHIPS):
                yield c, p, (core == c) & (chip == p)

    for c, p, here in branches():
        @pl.when(here)
        def _():
            to = spots(c, p)
            for i in range(3):
                for t in range(1, CHIPS):
                    q = lax.rem(chip + t, CHIPS)
                    remote(
                        own(c, p, lax.div(q, 2))[i], to[i], far_s.at[t - 1, i], far_r.at[p, i],
                        device(core, q, group),
                    ).start()
                remote(
                    own(c, p, lax.div(chip, 2))[i], to[i], near_s.at[p, i], near_r.at[p, i], partner
                ).start()
            mine = own(c, p, lax.div(chip, 2))
            for i in range(3):
                to[i][...] = mine[i][...]
    for i in range(3):
        for c in range(2):
            for p in range(CHIPS):
                @pl.when((core == c) & (chip != p))
                def _():
                    to = spots(c, p)[i]
                    remote(to, to, far_s.at[0, i], far_r.at[p, i], partner).wait_recv()
                    remote(to, to, near_s.at[p, i], near_r.at[p, i], partner).start()
    for c in range(2):
        @pl.when(core == c)
        def _():
            for p in range(CHIPS):
                for i in range(3):
                    to = spots(1 - c, p)[i]
                    remote(to, to, near_s.at[p, i], near_r.at[p, i], partner).wait_recv()
                    to = spots(c, p)[i]
                    remote(to, to, near_s.at[p, i], near_r.at[p, i], partner).wait_send()
    for c, p, here in branches():
        @pl.when(here)
        def _():
            for i in range(3):
                for t in range(1, CHIPS):
                    to = spots(c, p)[i]
                    remote(to, to, far_s.at[t - 1, i], far_r.at[p, i], partner).wait_send()


def gather_results(half, rot, upd):
    width = half.shape[1]
    bf16 = jnp.bfloat16
    dma = pltpu.SemaphoreType.DMA
    vmem = pl.BlockSpec(memory_space=pltpu.VMEM)
    return pl.pallas_call(
        gather_kernel,
        out_shape=[
            jax.ShapeDtypeStruct((CHIPS, 2 * HALF, width), bf16),
            jax.ShapeDtypeStruct((CHIPS, 2 * HALF, width), bf16),
            jax.ShapeDtypeStruct((CHIPS, 3 * width, width // 2), bf16),
            jax.ShapeDtypeStruct((CHIPS, 2, width // 2, width // 2), bf16),
        ],
        in_specs=[vmem] * 3,
        out_specs=[vmem] * 4,
        scratch_shapes=[
            dma((CHIPS - 1, 3)), dma((CHIPS, 3)), dma((CHIPS, 3)), dma((CHIPS, 3)),
        ],
        compiler_params=pltpu.CompilerParams(collective_id=1, has_side_effects=True),
        name="gather_results",
    )(half, rot, upd)


def shifted(block, axis, distance):
    devices = range(lax.axis_size(axis))
    route = [((i - distance) % len(devices), i) for i in devices]
    return lax.ppermute(block, axis, route)


def one_hot(index, count):
    return (lax.broadcasted_iota(jnp.int32, (count, index.shape[0]), 0) == index[None, :]).astype(
        jnp.bfloat16
    )


def spread(values, table):
    return jnp.dot(values, table, preferred_element_type=jnp.float32)


def collect(values, table):
    return lax.dot_general(
        values, table, (((1,), (1,)), ((), ())), preferred_element_type=jnp.float32
    )


def layer_norm(value, gain, bias):
    mean = jnp.mean(value, axis=0, keepdims=True)
    centred = value - mean
    var = jnp.mean(centred * centred, axis=0, keepdims=True)
    return centred * lax.rsqrt(var + 1e-05) * gain[:, None] + bias[:, None]


def silu_slope(pre):
    sigma = jax.nn.sigmoid(pre)
    return sigma * (1.0 + pre * (1.0 - sigma))


def mlp_forward(inner, first, second):
    pre = jnp.einsum("ih,ir->hr", first, inner, preferred_element_type=jnp.float32)
    hidden = jax.nn.silu(pre).astype(jnp.bfloat16)
    total = jnp.einsum("hl,hr->lr", second, hidden, preferred_element_type=jnp.float32)
    return (pre, hidden, total)


def mlp_backward(inner, first, second, pre, hidden, dtotal):
    dtotal_b = dtotal.astype(jnp.bfloat16)
    dsecond = jnp.einsum("hr,lr->hl", hidden, dtotal_b, preferred_element_type=jnp.float32)
    dhidden = jnp.einsum("hl,lr->hr", second, dtotal_b, preferred_element_type=jnp.float32)
    dpre = (dhidden * silu_slope(pre)).astype(jnp.bfloat16)
    dfirst = jnp.einsum("ir,hr->ih", inner, dpre, preferred_element_type=jnp.float32)
    dinner = jnp.einsum("ih,hr->ir", first, dpre, preferred_element_type=jnp.float32)
    return (dinner, dfirst, dsecond)


def adamw(weight, grad, moment, second_moment, corr_one, corr_two, decay, rate):
    moment = BETA_ONE * moment + (1.0 - BETA_ONE) * grad
    second_moment = BETA_TWO * second_moment + (1.0 - BETA_TWO) * grad * grad
    weight = weight - rate * (
        moment / corr_one / (jnp.sqrt(second_moment / corr_two) + EPSILON) + decay * weight
    )
    return (weight, moment, second_moment)


def swapped(part):
    return lax.ppermute(part, "mp", [(0, 1), (1, 0)])


def joined(mine, theirs, member, axis):
    first = member == 0
    return jnp.concatenate([jnp.where(first, mine, theirs), jnp.where(first, theirs, mine)], axis=axis)


def micro_batch(
    fields, targets, senders, receivers, g2m_dst, m2g_src, delta_scale, level_weight,
    count_all, edge_w, node_w, second_w, weight_in, weight_out, vectors,
):
    layers = len(edge_w)
    width = vectors.shape[1]
    count_vec = vectors.shape[0]
    nodes = NODE_DEV
    halo = nodes // 2
    grid = jnp.einsum("fl,fg->lg", weight_in, fields, preferred_element_type=jnp.float32)
    to_mesh = one_hot(g2m_dst, nodes)
    encoded = collect(grid.astype(jnp.bfloat16), to_mesh)
    mesh, enc_back = jax.vjp(layer_norm, encoded, vectors[0], vectors[1])
    send_tab = one_hot(senders, nodes + halo)
    recv_tab = one_hot(receivers, nodes)
    edge = None
    kept = []
    for layer in range(layers):
        mesh_b = mesh.astype(jnp.bfloat16)
        remote = shifted(mesh_b[:, :halo], "dp", 1)
        sent = spread(jnp.concatenate([mesh_b, remote], axis=1), send_tab).astype(jnp.bfloat16)
        recv_side = spread(mesh_b, recv_tab).astype(jnp.bfloat16)
        if layer == 0:
            edge = sent.astype(jnp.float32) - recv_side.astype(jnp.float32)
        edge_in = jnp.concatenate([edge.astype(jnp.bfloat16), sent, recv_side], axis=0)
        edge_pre, edge_hidden, edge_total = mlp_forward(edge_in, edge_w[layer], second_w[2 * layer])
        edge_out, edge_back = jax.vjp(
            layer_norm, edge_total, vectors[2 + 4 * layer], vectors[3 + 4 * layer]
        )
        edge = edge + edge_out
        gathered = collect(edge.astype(jnp.bfloat16), recv_tab)
        node_in = jnp.concatenate([mesh_b, gathered.astype(jnp.bfloat16)], axis=0)
        node_pre, node_hidden, node_total = mlp_forward(
            node_in, node_w[layer], second_w[2 * layer + 1]
        )
        node_out, node_back = jax.vjp(
            layer_norm, node_total, vectors[4 + 4 * layer], vectors[5 + 4 * layer]
        )
        mesh = mesh + node_out
        kept.append(
            (edge_in, edge_pre, edge_hidden, edge_back, node_in, node_pre, node_hidden, node_back)
        )
    to_grid = (
        one_hot(m2g_src[0], nodes).astype(jnp.float32)
        + one_hot(m2g_src[1], nodes).astype(jnp.float32)
        + one_hot(m2g_src[2], nodes).astype(jnp.float32)
    ).astype(jnp.bfloat16)
    decoded = spread(mesh.astype(jnp.bfloat16), to_grid)
    dec_out, dec_back = jax.vjp(layer_norm, decoded, vectors[count_vec - 2], vectors[count_vec - 1])
    final_b = (grid + dec_out).astype(jnp.bfloat16)
    pred = jnp.einsum("fl,lg->fg", weight_out, final_b, preferred_element_type=jnp.float32)
    resid = pred - targets / delta_scale[:, None]
    weighted = level_weight[:, None] * resid
    loss = jnp.sum(weighted * resid)
    dpred = (weighted * (2.0 / count_all)).astype(jnp.bfloat16)
    dweight_out = jnp.einsum("fg,lg->fl", dpred, final_b, preferred_element_type=jnp.float32)
    dfinal = jnp.einsum("fl,fg->lg", weight_out, dpred, preferred_element_type=jnp.float32)
    ddecoded, dec_gain, dec_bias = dec_back(dfinal)
    dmesh = collect(ddecoded.astype(jnp.bfloat16), to_grid)
    dedge = None
    dedge_w = [None] * layers
    dnode_w = [None] * layers
    dsecond_w = [None] * (2 * layers)
    dvec = [None] * count_vec
    dvec[-2:] = [dec_gain, dec_bias]
    for layer in reversed(range(layers)):
        edge_in, edge_pre, edge_hidden, edge_back, node_in, node_pre, node_hidden, node_back = kept[
            layer
        ]
        dnode_total, dvec[4 + 4 * layer], dvec[5 + 4 * layer] = node_back(dmesh)
        dnode_in, dnode_w[layer], dsecond_w[2 * layer + 1] = mlp_backward(
            node_in, node_w[layer], second_w[2 * layer + 1], node_pre, node_hidden, dnode_total
        )
        dmesh_b = dnode_in[:width]
        dedge_out = spread(dnode_in[width:].astype(jnp.bfloat16), recv_tab)
        if dedge is not None:
            dedge_out = dedge_out + dedge
        dedge_total, dvec[2 + 4 * layer], dvec[3 + 4 * layer] = edge_back(dedge_out)
        dedge_in, dedge_w[layer], dsecond_w[2 * layer] = mlp_backward(
            edge_in, edge_w[layer], second_w[2 * layer], edge_pre, edge_hidden, dedge_total
        )
        dedge = dedge_out + dedge_in[:width]
        dsent = dedge_in[width : 2 * width]
        drecv = dedge_in[2 * width :]
        if layer == 0:
            dsent = dsent + dedge
            drecv = drecv - dedge
        dextended = collect(dsent.astype(jnp.bfloat16), send_tab)
        dmesh_b = dmesh_b + collect(drecv.astype(jnp.bfloat16), recv_tab) + dextended[:, :nodes]
        back = shifted(dextended[:, nodes:].astype(jnp.bfloat16), "dp", -1).astype(jnp.float32)
        dmesh = dmesh + dmesh_b + jnp.pad(back, ((0, 0), (0, nodes - halo)))
    dencoded, dvec[0], dvec[1] = enc_back(dmesh)
    dgrid_b = (dfinal + spread(dencoded.astype(jnp.bfloat16), to_mesh)).astype(jnp.bfloat16)
    dweight_in = jnp.einsum("fg,lg->fl", fields, dgrid_b, preferred_element_type=jnp.float32)
    field_grad = (
        jnp.einsum("fl,lg->fg", weight_in, dgrid_b, preferred_element_type=jnp.float32) * count_all
    )
    extra = jnp.concatenate([dweight_in, dweight_out, jnp.stack(dvec)], axis=0)
    return (dedge_w + dnode_w, dsecond_w, extra, loss, field_grad)


def body(
    inputs, targets, senders, receivers, g2m_dst, m2g_src, delta_scale, level_index, step_count,
    soap_owner, edge_first, node_first, second, io_weights, vectors,
    edge_first_m, node_first_m, second_m, edge_first_v, node_first_v, second_v,
    io_m, io_v, vector_m, vector_v,
    edge_left_stat, edge_left_basis, node_left_stat, node_left_basis,
    second_left_stat, second_left_basis, right_stat, right_basis,
):
    layers = edge_first.shape[0]
    micro = inputs.shape[0]
    width = vectors.shape[1]
    fields_count = inputs.shape[1]
    member = lax.axis_index("mp")
    count_all = float(micro * fields_count * inputs.shape[2] * lax.axis_size("dp"))
    edge_w, node_w, second_w = [], [], []
    for layer in range(layers):
        pair = second[2 * layer : 2 * layer + 2].astype(jnp.bfloat16)
        for part, axis, into in (
            (edge_first[layer].astype(jnp.bfloat16), 1, edge_w),
            (pair, 1, second_w),
            (node_first[layer].astype(jnp.bfloat16), 1, node_w),
        ):
            whole = joined(part, swapped(part), member, axis)
            into.extend([whole] if whole.ndim == 2 else [whole[0], whole[1]])
    weight_in = io_weights[0].astype(jnp.bfloat16)
    weight_out = io_weights[1].astype(jnp.bfloat16)
    level_weight = (level_index + 1).astype(jnp.float32) / LEVELS

    mine = [
        lax.dynamic_index_in_dim(a, member, 0, keepdims=False)
        for a in (inputs, targets, senders, receivers, g2m_dst, m2g_src)
    ]
    firsts, seconds, extra, loss, field_grad = micro_batch(
        *mine, delta_scale, level_weight, count_all, edge_w, node_w, second_w,
        weight_in, weight_out, vectors,
    )
    away = swapped(field_grad.astype(jnp.bfloat16)).astype(jnp.float32)
    input_grad = joined(field_grad[None], away[None], member, 0)
    narrow = lambda a: a.astype(jnp.bfloat16)
    extra = jnp.pad(narrow(extra), ((0, HALF - extra.shape[0]), (0, 0)))
    half, tail, norm_tile, loss_tile = reduce_grads(
        [narrow(a) for a in firsts], [narrow(a) for a in seconds], extra,
        jnp.broadcast_to(loss * (1.0 / 1024.0), (8, 128)),
    )
    loss = jnp.sum(loss_tile) / count_all
    grad_norm = jnp.sqrt(jnp.sum(norm_tile))
    clip = jnp.minimum(1.0, CLIP / (grad_norm + 1e-06))
    steps = step_count.astype(jnp.float32)
    corr_one = 1.0 - jnp.power(BETA_ONE, steps)
    corr_two = 1.0 - jnp.power(BETA_TWO, steps)

    core, chip, _, _, _ = place()
    where = jnp.stack([
        jnp.where(core == 1, 2, chip // layers),
        jnp.where(core == 1, chip, chip % layers),
        CHIPS * core + chip,
    ]).astype(jnp.int32)
    scal = jnp.stack([clip, corr_one, corr_two])
    rot, upd = soap(
        where, scal, half, tail,
        (edge_first_m, node_first_m, second_m),
        (edge_first_v, node_first_v, second_v),
        (edge_left_stat, node_left_stat, second_left_stat),
        (edge_left_basis, node_left_basis, second_left_basis),
        right_stat, right_basis, jnp.bfloat16,
    )
    gall, rall, ufirst, usecond = gather_results(half, rot, upd)

    def cut(a):
        wide = a.astype(jnp.float32)
        return (
            wide[:layers, : 3 * width], wide[layers:, :HALF], wide[:, 3 * width :],
            wide[layers:, HALF : 3 * width],
        )

    grads, turned = cut(gall), cut(rall)
    firsts, seconds_out = [], []
    for k, (mom, sec) in enumerate(
        ((edge_first_m, edge_first_v), (node_first_m, node_first_v), (second_m, second_v))
    ):
        firsts.append(BETA_ONE * mom + (1.0 - BETA_ONE) * (clip * grads[k]))
        seconds_out.append(BETA_TWO * sec + (1.0 - BETA_TWO) * turned[k] * turned[k])
    new_edge = edge_first - RATE * (
        ufirst[:layers].astype(jnp.float32) + DECAY * edge_first
    )
    new_node = node_first - RATE * (
        ufirst[layers:, :HALF].astype(jnp.float32) + DECAY * node_first
    )
    upd_second = jnp.concatenate([usecond[:, 0], usecond[:, 1]], axis=2)
    new_second = second - RATE * (upd_second.astype(jnp.float32) + DECAY * second)
    rest = grads[3].reshape(HALF, width)
    io_rows = io_weights.shape[0] * io_weights.shape[1]
    grad_io = rest[:io_rows].reshape(io_weights.shape)
    grad_vectors = rest[io_rows : io_rows + vectors.shape[0]]
    new_io, m_io, v_io = adamw(
        io_weights, grad_io * clip, io_m, io_v, corr_one, corr_two, DECAY, RATE
    )
    new_vec, m_vec, v_vec = adamw(
        vectors, grad_vectors * clip, vector_m, vector_v, corr_one, corr_two, 0.0, VECTOR_RATE
    )
    return (
        loss,
        grad_norm,
        new_edge,
        new_edge.astype(jnp.bfloat16),
        new_node,
        new_node.astype(jnp.bfloat16),
        new_second,
        new_second.astype(jnp.bfloat16),
        new_io,
        new_io.astype(jnp.bfloat16),
        new_vec,
        new_vec.astype(jnp.bfloat16),
        *firsts,
        *seconds_out,
        m_io,
        v_io,
        m_vec,
        v_vec,
        input_grad,
    )


def solution(mesh):
    return jax.shard_map(
        body,
        mesh=mesh,
        in_specs=(
            P(None, None, "dp"),
            P(None, None, "dp"),
            P(None, "dp"),
            P(None, "dp"),
            P(None, "dp"),
            P(None, None, "dp"),
            P(),
            P(),
            P(),
            P(),
            P(None, None, "mp"),
            P(None, None, "mp"),
            P(None, "mp", None),
            P(),
            P(),
            P(),
            P(),
            P(),
            P(),
            P(),
            P(),
            P(),
            P(),
            P(),
            P(),
            P(),
            P(),
            P(),
            P(),
            P(),
            P(),
            P(),
            P(),
        ),
        out_specs=(
            P(),
            P(),
            P(None, None, "mp"),
            P(None, None, "mp"),
            P(None, None, "mp"),
            P(None, None, "mp"),
            P(None, "mp", None),
            P(None, "mp", None),
            P(),
            P(),
            P(),
            P(),
            P(),
            P(),
            P(),
            P(),
            P(),
            P(),
            P(),
            P(),
            P(),
            P(),
            P(None, None, "dp"),
        ),
        check_vma=False,
    )
```

```python
import functools

import jax
import jax.numpy as jnp
from jax import lax
from jax.experimental import pallas as pl
from jax.experimental.pallas import tpu as pltpu
from jax.sharding import PartitionSpec as P

LEVELS = 13
NODE_DEV = 512
CLIP = 0.0005
BETA_ONE = 0.9
BETA_TWO = 0.99
STAT_BETA = 0.95
EPSILON = 1e-08
RATE = 0.15
VECTOR_RATE = 0.7
DECAY = 0.01
HIGH = lax.Precision.HIGHEST

BLOCK = 128
AHEAD = 4
STAT_SCALE = 2.0**28
HALF = 512
CHIPS = 4
PLANE = 8


def mm(a, b, lhs=1, rhs=0):
    return lax.dot_general(
        a, b, (((lhs,), (rhs,)), ((), ())), precision=HIGH, preferred_element_type=jnp.float32
    )


def inverse_factors(blocks):
    tiles = BLOCK // 8
    shape = (8, BLOCK)
    lane = lax.broadcasted_iota(jnp.int32, shape, 1)
    sub = lax.broadcasted_iota(jnp.int32, shape, 0)
    eye = [jnp.where(lane == sub + 8 * t, 1.0, 0.0).astype(jnp.float32) for t in range(tiles)]
    states = []
    for block in blocks:
        rows = [block[8 * t : 8 * t + 8, :] for t in range(tiles)]
        cols = {
            j: [jnp.broadcast_to(rows[t][:, j : j + 1], shape) for t in range(tiles)]
            for j in range(AHEAD)
        }
        states.append((rows, list(eye), cols))
    for j in range(BLOCK):
        first, s = divmod(j, 8)
        for rows, inv, cols in states:
            col = cols.pop(j)
            pivot = jnp.broadcast_to(col[first][s : s + 1, :], shape)
            recip = 1.0 / pivot
            row = jnp.broadcast_to(rows[first][s : s + 1, :], shape)
            inv_row = jnp.broadcast_to(inv[first][s : s + 1, :], shape)
            factor = [None] * tiles
            for t in range(first, tiles):
                factor[t] = col[t] * recip
            factor[first] = jnp.where(sub > s, factor[first], 0.0)
            for ahead in range(j + 1, min(j + AHEAD, BLOCK)):
                entry = jnp.broadcast_to(cols[ahead][first][s : s + 1, :], shape)
                for t in range(first, tiles):
                    cols[ahead][t] = cols[ahead][t] - factor[t] * entry
            for t in range(first, tiles):
                rows[t] = rows[t] - factor[t] * row
                inv[t] = inv[t] - factor[t] * inv_row
            if j + AHEAD < BLOCK:
                at = j + AHEAD
                cols[at] = [
                    jnp.broadcast_to(rows[t][:, at : at + 1], shape) if t >= first else None
                    for t in range(tiles)
                ]
    results = []
    for rows, inv, cols in states:
        scaled = []
        for t in range(tiles):
            diag = jnp.sum(rows[t] * eye[t], axis=1, keepdims=True)
            scaled.append(inv[t] * lax.rsqrt(diag))
        results.append(jnp.concatenate(scaled, axis=0))
    return results


def soap_kernel(
    sizes,
    where_ref,
    scal_ref,
    half_ref,
    tail_ref,
    m0, m1, m2,
    v0, v1, v2,
    ls0, ls1, ls2,
    lb0, lb1, lb2,
    rs_hbm,
    rb_hbm,
    rot_ref,
    upd_ref,
    stat,
    basis,
    both,
    second,
    rstat,
    rbasis,
    table,
    inv,
    rgram,
    rinv,
    sems,
):
    order = stat.shape[0]
    width = rstat.shape[0]
    blocks = order // BLOCK
    kind = where_ref[0]
    index = where_ref[1]
    matrix = where_ref[2]
    copies = []
    for k, (size, mom, sec, left, base) in enumerate(
        zip(sizes, (m0, m1, m2), (v0, v1, v2), (ls0, ls1, ls2), (lb0, lb1, lb2))
    ):
        @pl.when(kind == k)
        def _():
            if size < order:
                row = lax.broadcasted_iota(jnp.int32, (order, order), 0)
                col = lax.broadcasted_iota(jnp.int32, (order, order), 1)
                unit = jnp.where(row == col, 1.0, 0.0).astype(jnp.float32)
                stat[...] = unit * (1.0 / STAT_SCALE)
                basis[...] = unit
                both[...] = jnp.zeros_like(both)
                second[...] = jnp.zeros_like(second)
            todo = [
                pltpu.make_async_copy(left.at[index], stat.at[pl.ds(0, size), pl.ds(0, size)], sems.at[0]),
                pltpu.make_async_copy(base.at[index], basis.at[pl.ds(0, size), pl.ds(0, size)], sems.at[1]),
                pltpu.make_async_copy(
                    mom.at[index], both.at[pl.ds(0, size), pl.ds(width, width)], sems.at[2]
                ),
                pltpu.make_async_copy(sec.at[index], second.at[pl.ds(0, size)], sems.at[3]),
                pltpu.make_async_copy(rs_hbm.at[matrix], rstat, sems.at[4]),
                pltpu.make_async_copy(rb_hbm.at[matrix], rbasis, sems.at[5]),
            ]
            for copy in todo:
                copy.start()
            held = HALF if k < 2 else width
            first = 0 if k < 2 else HALF - width
            both[:held, :width] = half_ref[first:, :].astype(jnp.float32)
            if size > HALF:
                both[HALF:size, :width] = tail_ref[: size - HALF, :].astype(jnp.float32)
            for copy in todo:
                copy.wait()

    clip, corr_one, corr_two = scal_ref[0], scal_ref[1], scal_ref[2]
    grad = both[:, :width] * clip
    both[:, :width] = grad
    both[:, width:] = BETA_ONE * both[:, width:] + (1.0 - BETA_ONE) * grad
    keep, fresh = STAT_SCALE * STAT_BETA, STAT_SCALE * (1.0 - STAT_BETA)
    stat[...] = keep * stat[...] + fresh * mm(grad, grad, 1, 1)
    rstat[...] = keep * rstat[...] + fresh * mm(grad, grad, 0, 0)
    table[:, :order] = mm(basis[...], stat[...], 0, 0)
    table[:, order:] = mm(table[:, :order], both[...])
    basis[...] = mm(stat[...], basis[...])
    stat[...] = basis[...]
    table[:, :order] = mm(table[:, :order], table[:, :order], 1, 1)
    rbasis[...] = mm(rstat[...], rbasis[...])
    rgram[...] = mm(rbasis[...], rbasis[...], 0, 0)

    def panel(k):
        at = pl.ds(pl.multiple_of(k * BLOCK, BLOCK), BLOCK)
        table[at, :] = mm(inv[at, :], table[at, :])

        def trail(i, carry):
            rows = pl.ds(pl.multiple_of(i * BLOCK, BLOCK), BLOCK)
            table[rows, :] = table[rows, :] - mm(table[at, rows], table[at, :], 0, 0)
            return carry

        lax.fori_loop(k + 1, blocks, trail, 0)

    def two(k, carry):
        at = pl.ds(pl.multiple_of(k * BLOCK, BLOCK), BLOCK)
        inv[at, :], rinv[at, :] = inverse_factors([table[at, at], rgram[at, at]])

        @pl.when(k == 0)
        def _():
            upper = mm(rinv[:BLOCK, :], rgram[:BLOCK, BLOCK:])
            rgram[:BLOCK, BLOCK:] = upper
            rgram[BLOCK:, BLOCK:] = rgram[BLOCK:, BLOCK:] - mm(upper, upper, 0, 0)

        panel(k)
        return carry

    def one(k, carry):
        at = pl.ds(pl.multiple_of(k * BLOCK, BLOCK), BLOCK)
        inv[at, :] = inverse_factors([table[at, at]])[0]
        panel(k)
        return carry

    lax.fori_loop(0, width // BLOCK, two, 0)
    lax.fori_loop(width // BLOCK, blocks, one, 0)
    left_part = mm(rbasis[:, :BLOCK], rinv[:BLOCK, :], 1, 1)
    right_part = mm(
        rbasis[:, BLOCK:] - mm(left_part, rgram[:BLOCK, BLOCK:]), rinv[BLOCK:, :], 1, 1
    )
    rbasis[:, :BLOCK] = left_part
    rbasis[:, BLOCK:] = right_part
    rot = mm(table[:, order : order + width], rbasis[...])
    rot_ref[...] = rot.astype(rot_ref.dtype)
    moment = mm(table[:, order + width :], rbasis[...])
    grown = BETA_TWO * second[...] + (1.0 - BETA_TWO) * rot * rot
    normed = moment / corr_one / (jnp.sqrt(grown / corr_two) + EPSILON)
    second[...] = mm(normed, rbasis[...], 1, 1)

    def back(step, carry):
        k = blocks - 1 - step
        at = pl.ds(pl.multiple_of(k * BLOCK, BLOCK), BLOCK)
        part = mm(inv[at, :], second[at, :], 0, 0)
        both[at, :width] = part
        second[...] = second[...] - mm(table[:, at], part)
        return carry

    lax.fori_loop(0, blocks, back, 0)
    update = mm(stat[...], both[:, :width]).astype(upd_ref.dtype)
    upd_ref[0] = update[:, : width // 2]
    upd_ref[1] = update[:, width // 2 :]


def soap(where, scal, half, tail, moms, seconds, lefts, bases, rstat, rbasis, out_dtype):
    order = max(a.shape[1] for a in lefts)
    width = rstat.shape[1]
    sizes = tuple(a.shape[1] for a in lefts)
    f32 = jnp.float32
    any_ = pl.BlockSpec(memory_space=pl.ANY)
    smem = pl.BlockSpec(memory_space=pltpu.SMEM)
    vmem = pl.BlockSpec(memory_space=pltpu.VMEM)
    return pl.pallas_call(
        functools.partial(soap_kernel, sizes),
        out_shape=[
            jax.ShapeDtypeStruct((order, width), out_dtype),
            jax.ShapeDtypeStruct((2, order, width // 2), out_dtype),
        ],
        in_specs=[smem, smem, vmem, vmem] + [any_] * 14,
        out_specs=[vmem, vmem],
        scratch_shapes=[
            pltpu.VMEM((order, order), f32),
            pltpu.VMEM((order, order), f32),
            pltpu.VMEM((order, 2 * width), f32),
            pltpu.VMEM((order, width), f32),
            pltpu.VMEM((width, width), f32),
            pltpu.VMEM((width, width), f32),
            pltpu.VMEM((order, order + 2 * width), f32),
            pltpu.VMEM((order, BLOCK), f32),
            pltpu.VMEM((width, width), f32),
            pltpu.VMEM((width, BLOCK), f32),
            pltpu.SemaphoreType.DMA((6,)),
        ],
        compiler_params=pltpu.CompilerParams(vmem_limit_bytes=56 * 2**20),
        name="soap",
    )(where, scal, half, tail, *moms, *seconds, *lefts, *bases, rstat, rbasis)


def place():
    dp = lax.axis_index("dp")
    core = lax.rem(dp, 2)
    chip = 2 * lax.axis_index("mp") + lax.rem(lax.div(dp, 2), 2)
    return core, chip, 2 * chip + core, lax.div(dp, 4), lax.axis_size("dp") // 4


def device(core, chip, group):
    return (4 * group + 2 * lax.rem(chip, 2) + core, lax.div(chip, 2))


def other(core, chip, turn):
    spot = lax.rem(2 * chip + core + turn, PLANE)
    return lax.rem(spot, 2), lax.div(spot, 2), spot


def remote(src, dst, send, recv, target):
    return pltpu.make_async_remote_copy(
        src_ref=src, dst_ref=dst, send_sem=send, recv_sem=recv, device_id=target,
        device_id_type=pl.DeviceIdType.MESH,
    )


def greet(targets):
    barrier = pltpu.get_barrier_semaphore()
    for target in targets:
        pl.semaphore_signal(
            barrier, inc=1, device_id=target, device_id_type=pl.DeviceIdType.MESH
        )
    pl.semaphore_wait(barrier, len(targets))


def fold(value):
    rows = jnp.sum(value.reshape(value.shape[0] // 8, 8, value.shape[1]), axis=0)
    return rows[:, :128] + rows[:, 128:]


def reduce_kernel(
    e0, e1, n0, n1, s0, s1, s2, s3, extra, loss_ref, field_ref,
    half_ref, tail_ref, norm_ref, total_ref, away_ref,
    from_core, acc, from_plane, part, from_group, full, tail,
    plane_loss, group_loss, plane_norm,
    core_s, core_r, plane_s, plane_r, group_s, group_r, full_s, full_r, tail_s, tail_r,
    ploss_s, ploss_r, gloss_s, gloss_r, norm_s, norm_r, field_s, field_r,
):
    f32, bf16 = jnp.float32, jnp.bfloat16
    core, chip, spot, group, groups = place()
    rows = HALF // groups
    partner = device(1 - core, chip, group)
    plane = [device(*other(core, chip, t)[:2], group) for t in range(1, PLANE)]
    along = [device(core, chip, lax.rem(group + t, groups)) for t in range(1, groups)]
    greet(plane + along)

    quarter = HALF // 2
    pieces = {0: [[(ref, 0, HALF, 0)] for ref in (e0, e1, n0, n1)], 1: []}
    for p, (ref, begin) in enumerate(((e0, HALF), (e1, HALF), (extra, 0), (extra, quarter))):
        pieces[1].append([(ref, begin, quarter, 0), ((s0, s1, s2, s3)[p], 0, quarter, quarter)])

    def core_copy(p, i, piece):
        ref, begin, size, to = piece
        return remote(
            ref.at[pl.ds(begin, size)], from_core.at[p, pl.ds(to, size)],
            core_s.at[p, i], core_r.at[p, i], partner,
        )

    for c in range(2):
        @pl.when(core == c)
        def _():
            for p in range(CHIPS):
                for i, piece in enumerate(pieces[1 - c][p]):
                    core_copy(p, i, piece).start()

    loss_sends = []
    for t in range(1, PLANE):
        copy = remote(
            loss_ref, plane_loss.at[spot], ploss_s.at[t - 1], ploss_r.at[spot], plane[t - 1]
        )
        copy.start()
        loss_sends.append(copy)
    plane_loss[spot] = loss_ref[...]

    def chunk(index):
        return pl.ds(pl.multiple_of(index * rows, rows), rows)

    def plane_copy(p, turn, index):
        return remote(
            acc.at[p, chunk(index)], from_plane.at[turn - 1, chunk(index)],
            plane_s.at[index, turn - 1], plane_r.at[index, turn - 1], device(core, p, group),
        )

    for p in range(CHIPS):
        for c in range(2):
            @pl.when(core == c)
            def _():
                for i, piece in enumerate(pieces[c][p]):
                    ref, begin, size, to = piece
                    core_copy(p, i, piece).wait_recv()
                    total = ref[begin : begin + size, :].astype(f32) + from_core[
                        p, to : to + size, :
                    ].astype(f32)
                    acc[p, to : to + size, :] = total.astype(bf16)
        turn = lax.rem(p - chip + CHIPS, CHIPS)

        @pl.when(turn != 0)
        def _():
            def go(i, carry):
                plane_copy(p, turn, lax.rem(group + i, groups)).start()
                return carry

            lax.fori_loop(1, groups + 1, go, 0)

    for t in range(1, PLANE):
        _, _, source = other(core, chip, t)
        remote(
            loss_ref, plane_loss.at[source], ploss_s.at[t - 1], ploss_r.at[source], partner
        ).wait_recv()
    total = plane_loss[0]
    for t in range(1, PLANE):
        total = total + plane_loss[t]
    group_loss[group] = total
    for t in range(1, groups):
        copy = remote(
            group_loss.at[group], group_loss.at[group], gloss_s.at[t - 1], gloss_r.at[group],
            along[t - 1],
        )
        copy.start()
        loss_sends.append(copy)

    def gather_plane(index):
        total = acc[chip, chunk(index), :].astype(f32)
        for turn in range(1, CHIPS):
            plane_copy(chip, turn, index).wait_recv()
            total = total + from_plane[turn - 1, chunk(index), :].astype(f32)
        return total

    def group_copy(turn):
        target = lax.rem(group + turn, groups)
        return remote(
            part.at[chunk(target)], from_group.at[turn - 1], group_s.at[turn - 1],
            group_r.at[turn - 1], device(core, chip, target),
        )

    def plane_step(turn, carry):
        target = lax.rem(group + turn, groups)
        part[chunk(target), :] = gather_plane(target).astype(bf16)
        group_copy(turn).start()
        return carry

    lax.fori_loop(1, groups, plane_step, 0)

    def group_step(turn, total):
        group_copy(turn).wait_recv()
        return total + from_group[turn - 1].astype(f32)

    total = lax.fori_loop(1, groups, group_step, gather_plane(group))
    full[chunk(group), :] = total.astype(bf16)

    def full_copy(turn, owner, target):
        return remote(
            full.at[chunk(owner)], full.at[chunk(owner)], full_s.at[turn - 1],
            full_r.at[turn - 1], device(core, chip, target),
        )

    def full_go(turn, carry):
        full_copy(turn, group, lax.rem(group + turn, groups)).start()
        return carry

    def full_wait(turn, carry):
        full_copy(turn, lax.rem(group + groups - turn, groups), group).wait_recv()
        return carry

    lax.fori_loop(1, groups, full_go, 0)
    lax.fori_loop(1, groups, full_wait, 0)

    field = remote(
        field_ref, away_ref, field_s, field_r,
        device(core, lax.rem(chip + CHIPS // 2, CHIPS), group),
    )
    field.start()
    swap = remote(full.at[pl.ds(0, quarter)], tail, tail_s, tail_r, partner)
    swap.start()
    squares = full[...].astype(f32)
    plane_norm[spot] = fold(squares * squares)
    norm_sends = []
    for t in range(1, PLANE):
        copy = remote(
            plane_norm.at[spot], plane_norm.at[spot], norm_s.at[t - 1], norm_r.at[spot],
            plane[t - 1],
        )
        copy.start()
        norm_sends.append(copy)
    half_ref[...] = full[...]
    for t in range(1, groups):
        source = lax.rem(group + t, groups)
        remote(
            group_loss.at[source], group_loss.at[source], gloss_s.at[t - 1], gloss_r.at[source],
            partner,
        ).wait_recv()
    total = group_loss[0]
    for t in range(1, groups):
        total = total + group_loss[t]
    total_ref[...] = total
    for t in range(1, PLANE):
        _, _, source = other(core, chip, t)
        remote(
            plane_norm.at[source], plane_norm.at[source], norm_s.at[t - 1], norm_r.at[source],
            partner,
        ).wait_recv()
    total = plane_norm[0]
    for t in range(1, PLANE):
        total = total + plane_norm[t]
    norm_ref[...] = total
    swap.wait_recv()
    tail_ref[...] = tail[...]

    field.wait()
    swap.wait_send()
    for copy in loss_sends + norm_sends:
        copy.wait_send()
    for c in range(2):
        @pl.when(core == c)
        def _():
            for p in range(CHIPS):
                for i, piece in enumerate(pieces[1 - c][p]):
                    core_copy(p, i, piece).wait_send()
    def plane_done(index, carry):
        for turn in range(1, CHIPS):
            plane_copy(lax.rem(chip + turn, CHIPS), turn, index).wait_send()
        return carry

    lax.fori_loop(0, groups, plane_done, 0)

    def group_done(turn, carry):
        group_copy(turn).wait_send()
        full_copy(turn, group, group).wait_send()
        return carry

    lax.fori_loop(1, groups, group_done, 0)


def reduce_grads(firsts, seconds, extra, loss, field):
    groups = lax.axis_size("dp") // 4
    width = extra.shape[1]
    f32, bf16 = jnp.float32, jnp.bfloat16
    rows = HALF // groups
    away = max(groups - 1, 1)
    dma = pltpu.SemaphoreType.DMA
    vmem = pl.BlockSpec(memory_space=pltpu.VMEM)
    tile = (8, 128)
    return pl.pallas_call(
        reduce_kernel,
        out_shape=[
            jax.ShapeDtypeStruct((HALF, width), bf16),
            jax.ShapeDtypeStruct((HALF // 2, width), bf16),
            jax.ShapeDtypeStruct(tile, f32),
            jax.ShapeDtypeStruct(tile, f32),
            jax.ShapeDtypeStruct(field.shape, bf16),
        ],
        in_specs=[vmem] * 11,
        out_specs=[vmem] * 5,
        scratch_shapes=[
            pltpu.VMEM((CHIPS, HALF, width), bf16),
            pltpu.VMEM((CHIPS, HALF, width), bf16),
            pltpu.VMEM((CHIPS - 1, HALF, width), bf16),
            pltpu.VMEM((HALF, width), bf16),
            pltpu.VMEM((away, rows, width), bf16),
            pltpu.VMEM((HALF, width), bf16),
            pltpu.VMEM((HALF // 2, width), bf16),
            pltpu.VMEM((PLANE, *tile), f32),
            pltpu.VMEM((groups, *tile), f32),
            pltpu.VMEM((PLANE, *tile), f32),
            dma((CHIPS, 2)), dma((CHIPS, 2)),
            dma((groups, CHIPS - 1)), dma((groups, CHIPS - 1)),
            dma((away,)), dma((away,)), dma((away,)), dma((away,)),
            dma(()), dma(()),
            dma((PLANE - 1,)), dma((PLANE,)),
            dma((away,)), dma((groups,)),
            dma((PLANE - 1,)), dma((PLANE,)), dma(()), dma(()),
        ],
        compiler_params=pltpu.CompilerParams(collective_id=0, has_side_effects=True),
        name="reduce_grads",
    )(*firsts, *seconds, extra, loss, field)


def gather_kernel(
    half_ref, rot_ref, upd_ref,
    gall, rall, ufirst, usecond,
    far_s, far_r, near_s, near_r,
):
    core, chip, spot, group, groups = place()
    width = half_ref.shape[1]
    partner = device(1 - core, chip, group)
    peers = [device(core, lax.rem(chip + t, CHIPS), group) for t in range(1, CHIPS)]
    greet(peers + [partner])

    def tall(p):
        return 3 * width if p < 2 else HALF

    def spots(c, p):
        if c == 0:
            rows = pl.ds(0, tall(p))
            return (gall.at[p, pl.ds(0, HALF)], rall.at[p, rows], ufirst.at[p, rows])
        return (
            gall.at[p, pl.ds(HALF, HALF)], rall.at[p, pl.ds(3 * width, width)], usecond.at[p]
        )

    def own(c, p, member):
        if c == 0:
            rows = pl.ds(0, tall(p))
            return (half_ref, rot_ref.at[rows], upd_ref.at[member, rows])
        side = pl.ds(pl.multiple_of(member * (width // 2), width // 2), width // 2)
        return (half_ref, rot_ref.at[pl.ds(0, width)], upd_ref.at[:, side])

    def branches(wanted=None):
        for c in range(2):
            for p in range(CHIPS):
                yield c, p, (core == c) & (chip == p)

    for c, p, here in branches():
        @pl.when(here)
        def _():
            to = spots(c, p)
            for i in range(3):
                for t in range(1, CHIPS):
                    q = lax.rem(chip + t, CHIPS)
                    remote(
                        own(c, p, lax.div(q, 2))[i], to[i], far_s.at[t - 1, i], far_r.at[p, i],
                        device(core, q, group),
                    ).start()
                remote(
                    own(c, p, lax.div(chip, 2))[i], to[i], near_s.at[p, i], near_r.at[p, i], partner
                ).start()
            mine = own(c, p, lax.div(chip, 2))
            for i in range(3):
                to[i][...] = mine[i][...]
    for i in range(3):
        for c in range(2):
            for p in range(CHIPS):
                @pl.when((core == c) & (chip != p))
                def _():
                    to = spots(c, p)[i]
                    remote(to, to, far_s.at[0, i], far_r.at[p, i], partner).wait_recv()
                    remote(to, to, near_s.at[p, i], near_r.at[p, i], partner).start()
    for c in range(2):
        @pl.when(core == c)
        def _():
            for p in range(CHIPS):
                for i in range(3):
                    to = spots(1 - c, p)[i]
                    remote(to, to, near_s.at[p, i], near_r.at[p, i], partner).wait_recv()
                    to = spots(c, p)[i]
                    remote(to, to, near_s.at[p, i], near_r.at[p, i], partner).wait_send()
    for c, p, here in branches():
        @pl.when(here)
        def _():
            for i in range(3):
                for t in range(1, CHIPS):
                    to = spots(c, p)[i]
                    remote(to, to, far_s.at[t - 1, i], far_r.at[p, i], partner).wait_send()


def gather_results(half, rot, upd):
    width = half.shape[1]
    bf16 = jnp.bfloat16
    dma = pltpu.SemaphoreType.DMA
    vmem = pl.BlockSpec(memory_space=pltpu.VMEM)
    return pl.pallas_call(
        gather_kernel,
        out_shape=[
            jax.ShapeDtypeStruct((CHIPS, 2 * HALF, width), bf16),
            jax.ShapeDtypeStruct((CHIPS, 2 * HALF, width), bf16),
            jax.ShapeDtypeStruct((CHIPS, 3 * width, width // 2), bf16),
            jax.ShapeDtypeStruct((CHIPS, 2, width // 2, width // 2), bf16),
        ],
        in_specs=[vmem] * 3,
        out_specs=[vmem] * 4,
        scratch_shapes=[
            dma((CHIPS - 1, 3)), dma((CHIPS, 3)), dma((CHIPS, 3)), dma((CHIPS, 3)),
        ],
        compiler_params=pltpu.CompilerParams(collective_id=1, has_side_effects=True),
        name="gather_results",
    )(half, rot, upd)


def dot(a, b):
    return jnp.dot(a, b, preferred_element_type=jnp.float32)


def dot_t(a, b):
    return lax.dot_general(a, b, (((1,), (1,)), ((), ())), preferred_element_type=jnp.float32)


def one_hot(index, first, count):
    rows = lax.broadcasted_iota(jnp.int32, (count, index.shape[1]), 0) + first
    return jnp.where(rows == index, 1.0, 0.0).astype(jnp.bfloat16)


def normalise(value):
    mean = jnp.mean(value, axis=0, keepdims=True)
    centred = value - mean
    scale = lax.rsqrt(jnp.mean(centred * centred, axis=0, keepdims=True) + 1e-05)
    return centred * scale, scale


def normalise_back(grad, hat, scale, gain):
    inner = grad * gain
    return scale * (
        inner
        - jnp.mean(inner, axis=0, keepdims=True)
        - hat * jnp.mean(inner * hat, axis=0, keepdims=True)
    )


def turned(value):
    return value.astype(jnp.float32).T.astype(jnp.bfloat16)


def step_kernel(
    inputs, targets, senders, receivers, g2m, m2g, delta, level, vec,
    edge_half, node_half, second_half, io, io_t,
    e0, e1, n0, n1, s0, s1, s2, s3, extra, loss_ref, field_ref, narrow_ref,
    send_tab, recv_tab, g2m_tab, m2g_tab, fields, goal,
    edge_w, edge_t, node_w, node_t, second_w, second_t, got_edge, got_node, got_second,
    grid, enc_hat, enc_scale, mesh, mesh_b, halo_s, halo_r,
    edge, edge_in, edge_slope, edge_hid, edge_hat, edge_scale,
    node_in, node_slope, node_hid, node_hat, node_scale, agg,
    dec_hat, dec_scale, dfinal, dmesh, dext, dedge, dpre, dtot, back_s, back_r, dvec, loss_acc,
    weight_s, weight_r, halo_ss, halo_rs, back_ss, back_rs,
    *, count_all,
):
    f32, bf16 = jnp.float32, jnp.bfloat16
    layers = edge_half.shape[0]
    width = vec.shape[0]
    nodes = mesh.shape[1]
    count_vec = 4 + 4 * layers
    edges = senders.shape[1]
    points = g2m.shape[1]
    halo = nodes // 2
    tile = 512
    fields_count = inputs.shape[1]
    dp, member = lax.axis_index("dp"), lax.axis_index("mp")
    blocks = lax.axis_size("dp")
    after, before = lax.rem(dp + 1, blocks), lax.rem(dp + blocks - 1, blocks)
    greet([(dp, 1 - member), (after, member), (before, member)])
    shard = edge_half.shape[2]
    mine = pl.ds(pl.multiple_of(member * shard, shard), shard)
    theirs = pl.ds(pl.multiple_of((1 - member) * shard, shard), shard)

    def weight_copies(layer):
        pair = pl.ds(2 * layer, 2)
        return [
            remote(src, dst, weight_s.at[layer, i], weight_r.at[layer, i], (dp, 1 - member))
            for i, (src, dst) in enumerate((
                (edge_half.at[layer], got_edge.at[layer]),
                (second_half.at[pair], got_second.at[pair]),
                (node_half.at[layer], got_node.at[layer]),
            ))
        ]

    for layer in range(layers):
        for copy in weight_copies(layer):
            copy.start()

    def place_weights(layer, edge_part, node_part, second_part, at):
        edge_w[layer, :, at] = edge_part[layer]
        edge_t[layer, at, :] = turned(edge_part[layer])
        node_w[layer, :, at] = node_part[layer]
        node_t[layer, at, :] = turned(node_part[layer])
        for i in (2 * layer, 2 * layer + 1):
            second_w[i, at, :] = second_part[i]
            second_t[i, :, at] = turned(second_part[i])

    def tiles(count, body):
        def go(j, carry):
            body(pl.ds(pl.multiple_of(j * tile, tile), tile))
            return carry

        lax.fori_loop(0, count // tile, go, 0)

    row = pl.ds(member, 1)
    fields[...] = jnp.zeros_like(fields)
    goal[...] = jnp.zeros_like(goal)
    fields[0:fields_count, :] = inputs[member]
    goal[0:fields_count, :] = targets[member] / delta[...]
    dvec[...] = jnp.zeros_like(dvec)
    loss_acc[...] = jnp.zeros_like(loss_acc)

    def gain(i):
        return vec[:, i : i + 1]

    def vec_grads(i, grad, hat):
        dvec[:, i : i + 1] += jnp.sum(grad * hat, axis=1, keepdims=True)
        dvec[:, i + 1 : i + 2] += jnp.sum(grad, axis=1, keepdims=True)

    agg[...] = jnp.zeros_like(agg)

    def encode(at):
        value = dot(io_t[0], fields[:, at])
        grid[:, at] = value
        table = one_hot(g2m[row, at], 0, nodes)
        g2m_tab[:, at] = table
        agg[...] += dot_t(value.astype(bf16), table)

    tiles(points, encode)
    hat, scale = normalise(agg[...])
    enc_hat[...] = hat
    enc_scale[...] = scale
    mesh[...] = hat * gain(0) + gain(1)

    def start_halo(layer):
        value = mesh[...].astype(bf16)
        mesh_b[layer] = value
        halo_s[layer] = value[:, :halo]
        halo_copy(layer).start()

    def halo_copy(layer):
        return remote(
            halo_s.at[layer], halo_r.at[layer], halo_ss.at[layer], halo_rs.at[layer],
            (after, member),
        )

    def back_copy(layer):
        return remote(
            back_s.at[layer], back_r.at[layer], back_ss.at[layer], back_rs.at[layer],
            (before, member),
        )

    start_halo(0)
    place_weights(0, edge_half, node_half, second_half, mine)

    def build(at):
        send_tab[:, at] = one_hot(senders[row, at], 0, nodes + halo)
        recv_tab[:, at] = one_hot(receivers[row, at], 0, nodes)

    tiles(edges, build)
    for layer in range(layers):
        def look_up(at):
            own = mesh_b[layer]
            edge_in[layer, width : 2 * width, at] = dot(own, send_tab[:nodes, at]).astype(bf16)
            edge_in[layer, 2 * width :, at] = dot(own, recv_tab[:, at]).astype(bf16)

        tiles(edges, look_up)
        for copy in weight_copies(layer):
            copy.wait_recv()
        place_weights(layer, got_edge, got_node, got_second, theirs)
        halo_copy(layer).wait_recv()
        agg[...] = jnp.zeros_like(agg)

        def edge_mlp(at):
            sent = edge_in[layer, width : 2 * width, at].astype(f32) + dot(
                halo_r[layer], send_tab[nodes:, at]
            )
            if layer == 0:
                old = sent - edge_in[layer, 2 * width :, at].astype(f32)
            else:
                old = edge[:, at]
            edge_in[layer, width : 2 * width, at] = sent.astype(bf16)
            edge_in[layer, :width, at] = old.astype(bf16)
            pre = dot(edge_t[layer], edge_in[layer, :, at])
            sigma = jax.nn.sigmoid(pre)
            edge_slope[layer, :, at] = sigma * (1.0 + pre * (1.0 - sigma))
            hidden = (pre * sigma).astype(bf16)
            edge_hid[layer, :, at] = hidden
            hat, scale = normalise(dot(second_t[2 * layer], hidden))
            edge_hat[layer, :, at] = hat
            edge_scale[layer, :, at] = scale
            new = old + hat * gain(2 + 4 * layer) + gain(3 + 4 * layer)
            edge[:, at] = new
            agg[...] += dot_t(new.astype(bf16), recv_tab[:, at])

        tiles(edges, edge_mlp)
        node_in[layer, :width] = mesh_b[layer]
        node_in[layer, width:] = agg[...].astype(bf16)
        pre = dot(node_t[layer], node_in[layer])
        sigma = jax.nn.sigmoid(pre)
        node_slope[layer] = sigma * (1.0 + pre * (1.0 - sigma))
        hidden = (pre * sigma).astype(bf16)
        node_hid[layer] = hidden
        hat, scale = normalise(dot(second_t[2 * layer + 1], hidden))
        node_hat[layer] = hat
        node_scale[layer] = scale
        mesh[...] = mesh[...] + hat * gain(4 + 4 * layer) + gain(5 + 4 * layer)
        if layer + 1 < layers:
            start_halo(layer + 1)
            place_weights(layer + 1, edge_half, node_half, second_half, mine)

    mesh_b[layers] = mesh[...].astype(bf16)
    dmesh[...] = jnp.zeros_like(dmesh)
    extra[...] = jnp.zeros_like(extra)
    dext[:, :width] = jnp.zeros((width, width), f32)

    def decode(at):
        index = m2g[member, :, at]
        table = sum(one_hot(index[i : i + 1], 0, nodes).astype(f32) for i in range(3)).astype(bf16)
        m2g_tab[:, at] = table
        hat, scale = normalise(dot(mesh_b[layers], table))
        final = (grid[:, at] + hat * gain(count_vec - 2) + gain(count_vec - 1)).astype(bf16)
        resid = dot(io[1], final) - goal[:, at]
        weighted = level[...] * resid
        squares = weighted * resid
        loss_acc[...] += jnp.sum(squares, axis=0, keepdims=True)
        dpred = (weighted * (2.0 / count_all)).astype(bf16)
        dext[: dpred.shape[0], :width] += dot_t(dpred, final)
        grad = dot(io_t[1], dpred)
        dfinal[:, at] = grad
        vec_grads(count_vec - 2, grad, hat)
        ddecoded = normalise_back(grad, hat, scale, gain(count_vec - 2))
        dmesh[...] += dot_t(ddecoded.astype(bf16), table)

    tiles(points, decode)
    io_rows = io.shape[1]
    extra[io_rows : 2 * io_rows, :] = dext[:io_rows, :width].astype(bf16)
    loss_ref[...] = jnp.broadcast_to(
        jnp.sum(loss_acc[...], axis=1, keepdims=True) * (1.0 / 1024.0), loss_ref.shape
    )

    firsts, nexts, seconds = (e0, e1), (n0, n1), (s0, s1, s2, s3)
    for layer in reversed(range(layers)):
        grad, hat = dmesh[...], node_hat[layer]
        vec_grads(4 + 4 * layer, grad, hat)
        total = normalise_back(grad, hat, node_scale[layer], gain(4 + 4 * layer)).astype(bf16)
        seconds[2 * layer + 1][...] = dot_t(node_hid[layer], total).astype(bf16)
        dnode = (dot(second_w[2 * layer + 1], total) * node_slope[layer]).astype(bf16)
        nexts[layer][...] = dot_t(node_in[layer], dnode).astype(bf16)
        dmesh[...] = grad + dot(node_w[layer, :width], dnode)
        agg[...] = dot(node_w[layer, width:], dnode)
        dext[...] = jnp.zeros_like(dext)

        def edge_back(at):
            grad = dot(agg[...].astype(bf16), recv_tab[:, at])
            if layer + 1 < layers:
                grad = grad + dedge[:, at]
            hat = edge_hat[layer, :, at]
            vec_grads(2 + 4 * layer, grad, hat)
            total = normalise_back(
                grad, hat, edge_scale[layer, :, at], gain(2 + 4 * layer)
            ).astype(bf16)
            dtot[:, at] = total
            dhid = dot(second_w[2 * layer], total)
            small = (dhid * edge_slope[layer, :, at]).astype(bf16)
            dpre[:, at] = small
            dself = grad + dot(edge_w[layer, :width], small)
            dsent = dot(edge_w[layer, width : 2 * width], small)
            drecv = dot(edge_w[layer, 2 * width :], small)
            if layer == 0:
                dsent = dsent + dself
                drecv = drecv - dself
            else:
                dedge[:, at] = dself
            dext[...] += dot_t(dsent.astype(bf16), send_tab[:, at])
            dmesh[...] += dot_t(drecv.astype(bf16), recv_tab[:, at])

        tiles(edges, edge_back)
        back_s[layer] = dext[:, nodes:].astype(bf16)
        back_copy(layer).start()
        dmesh[...] += dext[:, :nodes]
        seconds[2 * layer][...] = dot_t(edge_hid[layer], dtot[...]).astype(bf16)

        def weight_grad(i, carry):
            at = pl.ds(pl.multiple_of(i * width, width), width)
            firsts[layer][at, :] = dot_t(edge_in[layer, at, :], dpre[...]).astype(bf16)
            return carry

        lax.fori_loop(0, 3, weight_grad, 0)
        back_copy(layer).wait_recv()
        dmesh[:, :halo] += back_r[layer].astype(f32)

    grad, hat = dmesh[...], enc_hat[...]
    vec_grads(0, grad, hat)
    agg[...] = normalise_back(grad, hat, enc_scale[...], gain(0))
    dext[:io_rows, :width] = jnp.zeros((io_rows, width), f32)

    def encode_back(at):
        dgrid = (dfinal[:, at] + dot(agg[...].astype(bf16), g2m_tab[:, at])).astype(bf16)
        dext[:io_rows, :width] += dot_t(fields[:, at], dgrid)
        out = dot(io[0], dgrid)[:fields_count] * count_all
        field_ref[:, at] = out
        narrow_ref[:, at] = out.astype(bf16)

    tiles(points, encode_back)
    extra[:io_rows, :] = dext[:io_rows, :width].astype(bf16)
    extra[2 * io_rows : 3 * io_rows, :] = dvec[...].T.astype(bf16)
    for layer in range(layers):
        for copy in weight_copies(layer):
            copy.wait_send()
        halo_copy(layer).wait_send()
        back_copy(layer).wait_send()


def train_step(
    inputs, targets, senders, receivers, g2m, m2g, delta, level, vec,
    edge_half, node_half, second_half, io, io_t, count_all,
):
    f32, bf16 = jnp.float32, jnp.bfloat16
    layers, width = edge_half.shape[0], vec.shape[0]
    nodes, halo = NODE_DEV, NODE_DEV // 2
    edges, points = senders.shape[1], g2m.shape[1]
    fields_count, io_rows = inputs.shape[1], io.shape[1]
    tall, node_tall = edge_half.shape[1], node_half.shape[1]
    dma = pltpu.SemaphoreType.DMA
    vmem = pl.BlockSpec(memory_space=pltpu.VMEM)
    shape = jax.ShapeDtypeStruct
    hold = pltpu.VMEM
    return pl.pallas_call(
        functools.partial(step_kernel, count_all=count_all),
        out_shape=[shape((tall, width), bf16)] * layers
        + [shape((node_tall, width), bf16)] * layers
        + [shape((width, width), bf16)] * (2 * layers)
        + [
            shape((HALF, width), bf16), shape((8, 128), f32),
            shape((fields_count, points), f32), shape((fields_count, points), bf16),
        ],
        in_specs=[vmem] * 14,
        out_specs=[vmem] * (4 * layers + 4),
        scratch_shapes=[
            hold((nodes + halo, edges), bf16), hold((nodes, edges), bf16),
            hold((nodes, points), bf16), hold((nodes, points), bf16),
            hold((io_rows, points), bf16), hold((io_rows, points), f32),
            hold((layers, tall, width), bf16), hold((layers, width, tall), bf16),
            hold((layers, node_tall, width), bf16), hold((layers, width, node_tall), bf16),
            hold((2 * layers, width, width), bf16), hold((2 * layers, width, width), bf16),
            hold(edge_half.shape, bf16), hold(node_half.shape, bf16), hold(second_half.shape, bf16),
            hold((width, points), f32), hold((width, nodes), f32), hold((1, nodes), f32),
            hold((width, nodes), f32), hold((layers + 1, width, nodes), bf16),
            hold((layers, width, halo), bf16), hold((layers, width, halo), bf16),
            hold((width, edges), f32), hold((layers, tall, edges), bf16),
            hold((layers, width, edges), f32), hold((layers, width, edges), bf16),
            hold((layers, width, edges), f32), hold((layers, 1, edges), f32),
            hold((layers, node_tall, nodes), bf16),
            hold((layers, width, nodes), f32), hold((layers, width, nodes), bf16),
            hold((layers, width, nodes), f32), hold((layers, 1, nodes), f32),
            hold((width, nodes), f32),
            hold((width, points), f32), hold((1, points), f32),
            hold((width, points), f32), hold((width, nodes), f32),
            hold((width, nodes + halo), f32), hold((width, edges), f32),
            hold((width, edges), bf16), hold((width, edges), bf16),
            hold((layers, width, halo), bf16), hold((layers, width, halo), bf16),
            hold((width, 128), f32), hold((1, 512), f32),
            dma((layers, 3)), dma((layers, 3)),
            dma((layers,)), dma((layers,)), dma((layers,)), dma((layers,)),
        ],
        compiler_params=pltpu.CompilerParams(
            collective_id=2, has_side_effects=True, vmem_limit_bytes=60 * 2**20
        ),
        name="train_step",
    )(
        inputs, targets, senders, receivers, g2m, m2g, delta, level, vec,
        edge_half, node_half, second_half, io, io_t,
    )


def adamw(weight, grad, moment, second_moment, corr_one, corr_two, decay, rate):
    moment = BETA_ONE * moment + (1.0 - BETA_ONE) * grad
    second_moment = BETA_TWO * second_moment + (1.0 - BETA_TWO) * grad * grad
    weight = weight - rate * (
        moment / corr_one / (jnp.sqrt(second_moment / corr_two) + EPSILON) + decay * weight
    )
    return (weight, moment, second_moment)


def body(
    inputs, targets, senders, receivers, g2m_dst, m2g_src, delta_scale, level_index, step_count,
    soap_owner, edge_first, node_first, second, io_weights, vectors,
    edge_first_m, node_first_m, second_m, edge_first_v, node_first_v, second_v,
    io_m, io_v, vector_m, vector_v,
    edge_left_stat, edge_left_basis, node_left_stat, node_left_basis,
    second_left_stat, second_left_basis, right_stat, right_basis,
):
    layers = edge_first.shape[0]
    micro = inputs.shape[0]
    width = vectors.shape[1]
    fields_count = inputs.shape[1]
    member = lax.axis_index("mp")
    count_all = float(micro * fields_count * inputs.shape[2] * lax.axis_size("dp"))
    io_rows = 128
    narrow = lambda a: a.astype(jnp.bfloat16)
    column = lambda a: a.astype(jnp.float32)[:, None]
    io = jnp.pad(narrow(io_weights), ((0, 0), (0, io_rows - fields_count), (0, 0)))
    level = jnp.pad(column((level_index + 1).astype(jnp.float32) / LEVELS), ((0, io_rows - fields_count), (0, 0)))
    *grads, extra, loss_tile, field_grad, field_narrow = train_step(
        inputs, targets, senders, receivers, g2m_dst, m2g_src, column(delta_scale), level,
        vectors.T, narrow(edge_first), narrow(node_first), narrow(second),
        io, jnp.swapaxes(io, 1, 2), count_all,
    )
    half, tail, norm_tile, loss_tile, field_away = reduce_grads(
        grads[: 2 * layers], grads[2 * layers :], extra, loss_tile, field_narrow
    )
    field_away = field_away.astype(jnp.float32)
    first = member == 0
    input_grad = jnp.stack(
        [jnp.where(first, field_grad, field_away), jnp.where(first, field_away, field_grad)]
    )
    loss = jnp.sum(loss_tile) / count_all
    grad_norm = jnp.sqrt(jnp.sum(norm_tile))
    clip = jnp.minimum(1.0, CLIP / (grad_norm + 1e-06))
    steps = step_count.astype(jnp.float32)
    corr_one = 1.0 - jnp.power(BETA_ONE, steps)
    corr_two = 1.0 - jnp.power(BETA_TWO, steps)

    core, chip, _, _, _ = place()
    where = jnp.stack([
        jnp.where(core == 1, 2, chip // layers),
        jnp.where(core == 1, chip, chip % layers),
        CHIPS * core + chip,
    ]).astype(jnp.int32)
    scal = jnp.stack([clip, corr_one, corr_two])
    rot, upd = soap(
        where, scal, half, tail,
        (edge_first_m, node_first_m, second_m),
        (edge_first_v, node_first_v, second_v),
        (edge_left_stat, node_left_stat, second_left_stat),
        (edge_left_basis, node_left_basis, second_left_basis),
        right_stat, right_basis, jnp.bfloat16,
    )
    gall, rall, ufirst, usecond = gather_results(half, rot, upd)

    def cut(a):
        wide = a.astype(jnp.float32)
        return (
            wide[:layers, : 3 * width], wide[layers:, :HALF], wide[:, 3 * width :],
            wide[layers:, HALF : 3 * width],
        )

    grads, turned = cut(gall), cut(rall)
    firsts, seconds_out = [], []
    for k, (mom, sec) in enumerate(
        ((edge_first_m, edge_first_v), (node_first_m, node_first_v), (second_m, second_v))
    ):
        firsts.append(BETA_ONE * mom + (1.0 - BETA_ONE) * (clip * grads[k]))
        seconds_out.append(BETA_TWO * sec + (1.0 - BETA_TWO) * turned[k] * turned[k])
    new_edge = edge_first - RATE * (
        ufirst[:layers].astype(jnp.float32) + DECAY * edge_first
    )
    new_node = node_first - RATE * (
        ufirst[layers:, :HALF].astype(jnp.float32) + DECAY * node_first
    )
    upd_second = jnp.concatenate([usecond[:, 0], usecond[:, 1]], axis=2)
    new_second = second - RATE * (upd_second.astype(jnp.float32) + DECAY * second)
    rest = grads[3].reshape(HALF, width)
    grad_io = rest.reshape(-1, io_rows, width)[:2, :fields_count]
    grad_vectors = rest[2 * io_rows : 2 * io_rows + vectors.shape[0]]
    new_io, m_io, v_io = adamw(
        io_weights, grad_io * clip, io_m, io_v, corr_one, corr_two, DECAY, RATE
    )
    new_vec, m_vec, v_vec = adamw(
        vectors, grad_vectors * clip, vector_m, vector_v, corr_one, corr_two, 0.0, VECTOR_RATE
    )
    return (
        loss,
        grad_norm,
        new_edge,
        new_edge.astype(jnp.bfloat16),
        new_node,
        new_node.astype(jnp.bfloat16),
        new_second,
        new_second.astype(jnp.bfloat16),
        new_io,
        new_io.astype(jnp.bfloat16),
        new_vec,
        new_vec.astype(jnp.bfloat16),
        *firsts,
        *seconds_out,
        m_io,
        v_io,
        m_vec,
        v_vec,
        input_grad,
    )


def solution(mesh):
    return jax.shard_map(
        body,
        mesh=mesh,
        in_specs=(
            P(None, None, "dp"),
            P(None, None, "dp"),
            P(None, "dp"),
            P(None, "dp"),
            P(None, "dp"),
            P(None, None, "dp"),
            P(),
            P(),
            P(),
            P(),
            P(None, None, "mp"),
            P(None, None, "mp"),
            P(None, "mp", None),
            P(),
            P(),
            P(),
            P(),
            P(),
            P(),
            P(),
            P(),
            P(),
            P(),
            P(),
            P(),
            P(),
            P(),
            P(),
            P(),
            P(),
            P(),
            P(),
            P(),
        ),
        out_specs=(
            P(),
            P(),
            P(None, None, "mp"),
            P(None, None, "mp"),
            P(None, None, "mp"),
            P(None, None, "mp"),
            P(None, "mp", None),
            P(None, "mp", None),
            P(),
            P(),
            P(),
            P(),
            P(),
            P(),
            P(),
            P(),
            P(),
            P(),
            P(),
            P(),
            P(),
            P(),
            P(None, None, "dp"),
        ),
        check_vma=False,
    )
```

```python
import functools

import jax
import jax.numpy as jnp
from jax import lax
from jax.experimental import pallas as pl
from jax.experimental.pallas import tpu as pltpu
from jax.sharding import PartitionSpec as P

LEVELS = 13
NODE_DEV = 512
CLIP = 0.0005
BETA_ONE = 0.9
BETA_TWO = 0.99
STAT_BETA = 0.95
EPSILON = 1e-08
RATE = 0.15
VECTOR_RATE = 0.7
DECAY = 0.01
HIGH = lax.Precision.HIGHEST

BLOCK = 128
AHEAD = 4
STAT_SCALE = 2.0**28
HALF = 512
CHIPS = 4
PLANE = 8


def mm(a, b, lhs=1, rhs=0):
    return lax.dot_general(
        a, b, (((lhs,), (rhs,)), ((), ())), precision=HIGH, preferred_element_type=jnp.float32
    )


def mm3(a, b, lhs=1, rhs=0):
    total = None
    for _ in range(3):
        high = a.astype(jnp.bfloat16)
        a = a - high.astype(jnp.float32)
        part = lax.dot_general(
            high, b, (((lhs,), (rhs,)), ((), ())), preferred_element_type=jnp.float32
        )
        total = part if total is None else total + part
    return total


def mid(a, b, lhs=1, rhs=0):
    def go(x, y):
        return lax.dot_general(
            x, y, (((lhs,), (rhs,)), ((), ())), preferred_element_type=jnp.float32
        )

    a_high, b_high = a.astype(jnp.bfloat16), b.astype(jnp.bfloat16)
    a_low = (a - a_high.astype(jnp.float32)).astype(jnp.bfloat16)
    b_low = (b - b_high.astype(jnp.float32)).astype(jnp.bfloat16)
    return go(a_high, b_low) + go(a_low, b_high) + go(a_high, b_high)


def inverse_factors(blocks):
    tiles = BLOCK // 8
    shape = (8, BLOCK)
    lane = lax.broadcasted_iota(jnp.int32, shape, 1)
    sub = lax.broadcasted_iota(jnp.int32, shape, 0)
    eye = [jnp.where(lane == sub + 8 * t, 1.0, 0.0).astype(jnp.float32) for t in range(tiles)]
    states = []
    for block in blocks:
        rows = [block[8 * t : 8 * t + 8, :] for t in range(tiles)]
        cols = {
            j: [jnp.broadcast_to(rows[t][:, j : j + 1], shape) for t in range(tiles)]
            for j in range(AHEAD)
        }
        states.append((rows, list(eye), cols))
    for j in range(BLOCK):
        first, s = divmod(j, 8)
        for rows, inv, cols in states:
            col = cols.pop(j)
            pivot = jnp.broadcast_to(col[first][s : s + 1, :], shape)
            recip = 1.0 / pivot
            row = jnp.broadcast_to(rows[first][s : s + 1, :], shape)
            inv_row = jnp.broadcast_to(inv[first][s : s + 1, :], shape)
            factor = [None] * tiles
            for t in range(first, tiles):
                factor[t] = col[t] * recip
            factor[first] = jnp.where(sub > s, factor[first], 0.0)
            for ahead in range(j + 1, min(j + AHEAD, BLOCK)):
                entry = jnp.broadcast_to(cols[ahead][first][s : s + 1, :], shape)
                for t in range(first, tiles):
                    cols[ahead][t] = cols[ahead][t] - factor[t] * entry
            for t in range(first, tiles):
                rows[t] = rows[t] - factor[t] * row
                inv[t] = inv[t] - factor[t] * inv_row
            if j + AHEAD < BLOCK:
                at = j + AHEAD
                cols[at] = [
                    jnp.broadcast_to(rows[t][:, at : at + 1], shape) if t >= first else None
                    for t in range(tiles)
                ]
    results = []
    for rows, inv, cols in states:
        scaled = []
        for t in range(tiles):
            diag = jnp.sum(rows[t] * eye[t], axis=1, keepdims=True)
            scaled.append(inv[t] * lax.rsqrt(diag))
        results.append(jnp.concatenate(scaled, axis=0))
    return results


def place():
    dp = lax.axis_index("dp")
    core = lax.rem(dp, 2)
    chip = 2 * lax.axis_index("mp") + lax.rem(lax.div(dp, 2), 2)
    return core, chip, 2 * chip + core, lax.div(dp, 4), lax.axis_size("dp") // 4


def device(core, chip, group):
    return (4 * group + 2 * lax.rem(chip, 2) + core, lax.div(chip, 2))


def other(core, chip, turn):
    spot = lax.rem(2 * chip + core + turn, PLANE)
    return lax.rem(spot, 2), lax.div(spot, 2), spot


def remote(src, dst, send, recv, target):
    return pltpu.make_async_remote_copy(
        src_ref=src, dst_ref=dst, send_sem=send, recv_sem=recv, device_id=target,
        device_id_type=pl.DeviceIdType.MESH,
    )


def greet(targets):
    barrier = pltpu.get_barrier_semaphore()
    for target in targets:
        pl.semaphore_signal(
            barrier, inc=1, device_id=target, device_id_type=pl.DeviceIdType.MESH
        )
    pl.semaphore_wait(barrier, len(targets))


def fold(value):
    rows = jnp.sum(value.reshape(value.shape[0] // 8, 8, value.shape[1]), axis=0)
    return rows[:, :128] + rows[:, 128:]


def finish_kernel(
    sizes,
    scal_ref,
    e0, e1, n0, n1, s0, s1, s2, s3, extra, loss_ref, field_ref,
    m0, m1, m2,
    v0, v1, v2,
    ls0, ls1, ls2,
    lb0, lb1, lb2,
    rs_hbm, rb_hbm,
    norm_ref, total_ref, away_ref, gall, rall, ufirst, usecond,
    from_core, acc, from_plane, part, from_group, full, tail,
    plane_loss, group_loss, plane_norm,
    stat, basis, turned_basis, moment, second, rstat, rbasis, table, gram, grad,
    left, right, inv, rgram, rinv, solved, rot_s, upd_s,
    core_s, core_r, plane_s, plane_r, group_s, group_r, full_s, full_r, tail_s, tail_r,
    ploss_s, ploss_r, gloss_s, gloss_r, norm_s, norm_r, field_s, field_r,
    far_s, far_r, near_s, near_r, sems,
):
    f32, bf16 = jnp.float32, jnp.bfloat16
    core, chip, spot, group, groups = place()
    order, width = moment.shape
    blocks, wide = order // BLOCK, order // width
    layers = m0.shape[0]
    kind = jnp.where(core == 1, 2, lax.div(chip, layers))
    matrix = CHIPS * core + chip
    keep, fresh = STAT_SCALE * STAT_BETA, STAT_SCALE * (1.0 - STAT_BETA)

    def block(i):
        return pl.ds(pl.multiple_of(i * width, width), width)

    def state_copies(k):
        size = sizes[k]
        index = chip if k == 2 else lax.rem(chip, layers)
        inside = pl.ds(0, size)
        pairs = [
            ((ls0, ls1, ls2)[k].at[index], stat.at[inside, inside]),
            ((lb0, lb1, lb2)[k].at[index], basis.at[inside, inside]),
            ((m0, m1, m2)[k].at[index], moment.at[inside]),
            ((v0, v1, v2)[k].at[index], second.at[inside]),
            (rs_hbm.at[matrix], rstat),
            (rb_hbm.at[matrix], rbasis),
        ]
        return [pltpu.make_async_copy(a, b, sems.at[i]) for i, (a, b) in enumerate(pairs)]

    def start_states():
        for k, size in enumerate(sizes):
            @pl.when(kind == k)
            def _():
                if size < order:
                    row = lax.broadcasted_iota(jnp.int32, (order, order), 0)
                    col = lax.broadcasted_iota(jnp.int32, (order, order), 1)
                    unit = jnp.where(row == col, 1.0, 0.0).astype(f32)
                    stat[...] = unit * (1.0 / STAT_SCALE)
                    basis[...] = unit
                    moment[...] = jnp.zeros_like(moment)
                    second[...] = jnp.zeros_like(second)
                for copy in state_copies(k):
                    copy.start()

    def wait_states():
        for k in range(len(sizes)):
            @pl.when(kind == k)
            def _():
                for copy in state_copies(k):
                    copy.wait()

    def tall(p):
        return 3 * width if p < 2 else HALF

    def spots(c, p, i):
        if c == 0:
            rows = pl.ds(0, HALF if i == 0 else tall(p))
            return (gall, rall, ufirst)[i].at[p, rows]
        if i == 2:
            return usecond.at[p]
        first, count = ((HALF, HALF), (3 * width, width))[i]
        return (gall, rall)[i].at[p, pl.ds(first, count)]

    def own(c, p, i, ref, other_member):
        if i == 0:
            return ref
        rows = pl.ds(0, tall(p) if c == 0 else width)
        if i == 1:
            return ref.at[rows]
        if c == 0:
            return ref.at[other_member, rows]
        side = pl.ds(pl.multiple_of(other_member * (width // 2), width // 2), width // 2)
        return ref.at[:, side]

    def branches():
        for c in range(2):
            for p in range(CHIPS):
                yield c, p, (core == c) & (chip == p)

    def send_far(i, ref, _):
        for c, p, here in branches():
            @pl.when(here)
            def _():
                to = spots(c, p, i)
                for t in range(1, CHIPS):
                    q = lax.rem(chip + t, CHIPS)
                    remote(
                        own(c, p, i, ref, lax.div(q, 2)), to, far_s.at[t - 1, i],
                        far_r.at[p, i], device(core, q, group),
                    ).start()
                mine = own(c, p, i, ref, lax.div(chip, 2))
                remote(mine, to, near_s.at[p, i], near_r.at[p, i], partner).start()
                to[...] = mine[...]

    def forward(i):
        for c in range(2):
            for p in range(CHIPS):
                @pl.when((core == c) & (chip != p))
                def _():
                    to = spots(c, p, i)
                    remote(to, to, far_s.at[0, i], far_r.at[p, i], partner).wait_recv()
                    remote(to, to, near_s.at[p, i], near_r.at[p, i], partner).start()

    rows = HALF // groups
    partner = device(1 - core, chip, group)
    plane = [device(*other(core, chip, t)[:2], group) for t in range(1, PLANE)]
    along = [device(core, chip, lax.rem(group + t, groups)) for t in range(1, groups)]
    start_states()
    greet(plane + along)

    quarter = HALF // 2
    pieces = {0: [[(ref, 0, HALF, 0)] for ref in (e0, e1, n0, n1)], 1: []}
    for p, (ref, begin) in enumerate(((e0, HALF), (e1, HALF), (extra, 0), (extra, quarter))):
        pieces[1].append([(ref, begin, quarter, 0), ((s0, s1, s2, s3)[p], 0, quarter, quarter)])

    def core_copy(p, i, piece):
        ref, begin, size, to = piece
        return remote(
            ref.at[pl.ds(begin, size)], from_core.at[p, pl.ds(to, size)],
            core_s.at[p, i], core_r.at[p, i], partner,
        )

    for c in range(2):
        @pl.when(core == c)
        def _():
            for p in range(CHIPS):
                for i, piece in enumerate(pieces[1 - c][p]):
                    core_copy(p, i, piece).start()

    loss_sends = []
    for t in range(1, PLANE):
        copy = remote(
            loss_ref, plane_loss.at[spot], ploss_s.at[t - 1], ploss_r.at[spot], plane[t - 1]
        )
        copy.start()
        loss_sends.append(copy)
    plane_loss[spot] = loss_ref[...]

    def chunk(index):
        return pl.ds(pl.multiple_of(index * rows, rows), rows)

    def plane_copy(p, turn, index):
        return remote(
            acc.at[p, chunk(index)], from_plane.at[turn - 1, chunk(index)],
            plane_s.at[index, turn - 1], plane_r.at[index, turn - 1], device(core, p, group),
        )

    for p in range(CHIPS):
        for c in range(2):
            @pl.when(core == c)
            def _():
                for i, piece in enumerate(pieces[c][p]):
                    ref, begin, size, to = piece
                    core_copy(p, i, piece).wait_recv()
                    total = ref[begin : begin + size, :].astype(f32) + from_core[
                        p, to : to + size, :
                    ].astype(f32)
                    acc[p, to : to + size, :] = total.astype(bf16)
        turn = lax.rem(p - chip + CHIPS, CHIPS)

        @pl.when(turn != 0)
        def _():
            def go(i, carry):
                plane_copy(p, turn, lax.rem(group + i, groups)).start()
                return carry

            lax.fori_loop(1, groups + 1, go, 0)

    wait_states()
    turned_basis[...] = basis[...].T

    def product(j, carry):
        at = block(j)
        table[:, at] = keep * mm(turned_basis[...], stat[:, at])
        return carry

    lax.fori_loop(0, wide, product, 0)

    def old_gram(j, carry):
        def one(i, carry):
            gram[block(i), block(j)] = mm(table[block(i), :order], table[block(j), :order], 1, 1)
            return carry

        return lax.fori_loop(0, j + 1, one, carry)

    for t in range(1, PLANE):
        _, _, source = other(core, chip, t)
        remote(
            loss_ref, plane_loss.at[source], ploss_s.at[t - 1], ploss_r.at[source], partner
        ).wait_recv()
    total = plane_loss[0]
    for t in range(1, PLANE):
        total = total + plane_loss[t]
    group_loss[group] = total
    for t in range(1, groups):
        copy = remote(
            group_loss.at[group], group_loss.at[group], gloss_s.at[t - 1], gloss_r.at[group],
            along[t - 1],
        )
        copy.start()
        loss_sends.append(copy)

    def gather_plane(index):
        total = acc[chip, chunk(index), :].astype(f32)
        for turn in range(1, CHIPS):
            plane_copy(chip, turn, index).wait_recv()
            total = total + from_plane[turn - 1, chunk(index), :].astype(f32)
        return total

    def group_copy(turn):
        target = lax.rem(group + turn, groups)
        return remote(
            part.at[chunk(target)], from_group.at[turn - 1], group_s.at[turn - 1],
            group_r.at[turn - 1], device(core, chip, target),
        )

    def plane_step(turn, carry):
        target = lax.rem(group + turn, groups)
        part[chunk(target), :] = gather_plane(target).astype(bf16)
        group_copy(turn).start()
        return carry

    lax.fori_loop(1, groups, plane_step, 0)
    lax.fori_loop(0, wide - 1, old_gram, 0)

    def group_step(turn, total):
        group_copy(turn).wait_recv()
        return total + from_group[turn - 1].astype(f32)

    total = lax.fori_loop(1, groups, group_step, gather_plane(group))
    full[chunk(group), :] = total.astype(bf16)

    def full_copy(turn, owner, target):
        return remote(
            full.at[chunk(owner)], full.at[chunk(owner)], full_s.at[turn - 1],
            full_r.at[turn - 1], device(core, chip, target),
        )

    def full_go(turn, carry):
        full_copy(turn, group, lax.rem(group + turn, groups)).start()
        return carry

    def full_wait(turn, carry):
        full_copy(turn, lax.rem(group + groups - turn, groups), group).wait_recv()
        return carry

    lax.fori_loop(1, groups, full_go, 0)
    lax.fori_loop(wide - 1, wide, old_gram, 0)
    old_moment = mm(table[:, :order], moment[...])
    stat[...] = table[:, :order]
    basis[...] = stat[...].T
    lax.fori_loop(1, groups, full_wait, 0)

    field = remote(
        field_ref, away_ref, field_s, field_r,
        device(core, lax.rem(chip + CHIPS // 2, CHIPS), group),
    )
    field.start()
    swap = remote(full.at[pl.ds(0, quarter)], tail, tail_s, tail_r, partner)
    swap.start()
    send_far(0, full, full)
    squares = full[...].astype(f32)
    plane_norm[spot] = fold(squares * squares)
    norm_sends = []
    for t in range(1, PLANE):
        copy = remote(
            plane_norm.at[spot], plane_norm.at[spot], norm_s.at[t - 1], norm_r.at[spot],
            plane[t - 1],
        )
        copy.start()
        norm_sends.append(copy)
    for t in range(1, groups):
        source = lax.rem(group + t, groups)
        remote(
            group_loss.at[source], group_loss.at[source], gloss_s.at[t - 1], gloss_r.at[source],
            partner,
        ).wait_recv()
    total = group_loss[0]
    for t in range(1, groups):
        total = total + group_loss[t]
    total_ref[...] = total
    swap.wait_recv()
    grad[...] = jnp.zeros_like(grad)
    for k, size in enumerate(sizes):
        @pl.when(kind == k)
        def _():
            held = HALF if k < 2 else width
            grad[:held, :] = full[HALF - held :, :]
            if size > HALF:
                grad[HALF:size, :] = tail[: size - HALF, :]

    raw = grad[...]
    turned_grad = mm3(turned_basis[...], raw)
    product_grad = mm3(stat[...], raw)
    square = lax.dot_general(raw, raw, (((0,), (0,)), ((), ())), preferred_element_type=f32)
    grad_moment = mm3(moment[...], raw, 0, 0).T
    for t in range(1, PLANE):
        _, _, source = other(core, chip, t)
        remote(
            plane_norm.at[source], plane_norm.at[source], norm_s.at[t - 1], norm_r.at[source],
            partner,
        ).wait_recv()
    total = plane_norm[0]
    for t in range(1, PLANE):
        total = total + plane_norm[t]
    norm_ref[...] = total
    norm = jnp.sqrt(jnp.sum(jnp.sum(total, axis=0, keepdims=True), axis=1, keepdims=True))
    clip = jnp.minimum(1.0, CLIP / (norm + 1e-06))


    turned_grad = turned_grad * clip
    product_grad = product_grad * clip
    square = square * (clip * clip)
    grad_moment = BETA_ONE * clip * grad_moment + (1.0 - BETA_ONE) * square
    left[:, :width] = fresh * product_grad + (0.5 * fresh * fresh) * mm(turned_grad, square)
    left[:, width:] = turned_grad
    right[:, :width] = turned_grad
    right[:, width:] = left[:, :width]

    def new_gram(j, carry):
        def one(i, carry):
            table[block(i), block(j)] = gram[block(i), block(j)] + mm(
                left[block(i), :], right[block(j), :], 1, 1
            )
            return carry

        return lax.fori_loop(0, j + 1, one, carry)

    lax.fori_loop(0, wide, new_gram, 0)
    table[:, order : order + width] = product_grad + fresh * mm(turned_grad, square)
    table[:, order + width :] = (
        BETA_ONE * old_moment
        + (1.0 - BETA_ONE) * product_grad
        + fresh * mm(turned_grad, grad_moment)
    )
    rstat[...] = keep * rstat[...] + fresh * square
    rbasis[...] = mm(rstat[...], rbasis[...])
    rgram[...] = mm(rbasis[...], rbasis[...], 0, 0)

    def panel(k):
        at = pl.ds(pl.multiple_of(k * BLOCK, BLOCK), BLOCK)
        table[at, :] = mm(inv[at, :], table[at, :])

        @pl.when(lax.rem(k, 2) == 0)
        def _():
            rows = pl.ds(pl.multiple_of(k * BLOCK + BLOCK, BLOCK), BLOCK)
            table[rows, :] = table[rows, :] - mm(table[at, rows], table[at, :], 0, 0)

        @pl.when(lax.rem(k, 2) == 1)
        def _():
            now = lax.div(k, 2)

            def trail(i, carry):
                table[block(i), :] = table[block(i), :] - mm(
                    table[block(now), block(i)], table[block(now), :], 0, 0
                )
                return carry

            lax.fori_loop(now + 1, wide, trail, 0)

    def two(k, carry):
        at = pl.ds(pl.multiple_of(k * BLOCK, BLOCK), BLOCK)
        inv[at, :], rinv[at, :] = inverse_factors([table[at, at], rgram[at, at]])

        @pl.when(k == 0)
        def _():
            upper = mm(rinv[:BLOCK, :], rgram[:BLOCK, BLOCK:])
            rgram[:BLOCK, BLOCK:] = upper
            rgram[BLOCK:, BLOCK:] = rgram[BLOCK:, BLOCK:] - mm(upper, upper, 0, 0)

        panel(k)
        return carry

    def one(k, carry):
        at = pl.ds(pl.multiple_of(k * BLOCK, BLOCK), BLOCK)
        inv[at, :] = inverse_factors([table[at, at]])[0]
        panel(k)
        return carry

    lax.fori_loop(0, width // BLOCK, two, 0)
    forward(0)
    lax.fori_loop(width // BLOCK, blocks, one, 0)
    left_part = mm(rbasis[:, :BLOCK], rinv[:BLOCK, :], 1, 1)
    right_part = mm(
        rbasis[:, BLOCK:] - mm(left_part, rgram[:BLOCK, BLOCK:]), rinv[BLOCK:, :], 1, 1
    )
    rbasis[:, :BLOCK] = left_part
    rbasis[:, BLOCK:] = right_part
    rot = mid(table[:, order : order + width], rbasis[...])
    rot_s[...] = rot.astype(bf16)
    send_far(1, rot_s, rot_s)
    corr_one, corr_two = scal_ref[0], scal_ref[1]
    rotated = mid(table[:, order + width :], rbasis[...])
    grown = BETA_TWO * second[...] + (1.0 - BETA_TWO) * rot * rot
    normed = rotated / corr_one / (jnp.sqrt(grown / corr_two) + EPSILON)
    second[...] = mid(normed, rbasis[...], 1, 1)

    def back(step, carry):
        k = blocks - 1 - step
        at = pl.ds(pl.multiple_of(k * BLOCK, BLOCK), BLOCK)
        part = mid(inv[at, :], second[at, :], 0, 0)
        solved[at, :] = part
        second[...] = second[...] - mid(table[:, at], part)
        return carry

    lax.fori_loop(0, blocks, back, 0)
    forward(1)
    inner = mid(left[:, width:], solved[...], 0, 0)
    update = mid(basis[...], solved[...]) + (fresh * clip) * mid(grad[...].astype(f32), inner)
    update = update.astype(bf16)
    upd_s[0] = update[:, : width // 2]
    upd_s[1] = update[:, width // 2 :]
    send_far(2, upd_s, upd_s)
    forward(2)

    field.wait()
    swap.wait_send()
    for copy in loss_sends + norm_sends:
        copy.wait_send()
    for c in range(2):
        @pl.when(core == c)
        def _():
            for p in range(CHIPS):
                for i, piece in enumerate(pieces[1 - c][p]):
                    core_copy(p, i, piece).wait_send()
    def plane_done(index, carry):
        for turn in range(1, CHIPS):
            plane_copy(lax.rem(chip + turn, CHIPS), turn, index).wait_send()
        return carry

    lax.fori_loop(0, groups, plane_done, 0)

    def group_done(turn, carry):
        group_copy(turn).wait_send()
        full_copy(turn, group, group).wait_send()
        return carry

    lax.fori_loop(1, groups, group_done, 0)
    for i in range(3):
        for c in range(2):
            @pl.when(core == c)
            def _():
                for p in range(CHIPS):
                    to = spots(1 - c, p, i)
                    remote(to, to, near_s.at[p, i], near_r.at[p, i], partner).wait_recv()
                    to = spots(c, p, i)
                    remote(to, to, near_s.at[p, i], near_r.at[p, i], partner).wait_send()
        for c, p, here in branches():
            @pl.when(here)
            def _():
                for t in range(1, CHIPS):
                    to = spots(c, p, i)
                    remote(to, to, far_s.at[t - 1, i], far_r.at[p, i], partner).wait_send()


def finish(scal, firsts, seconds, extra, loss, field, moms, seconds_old, lefts, bases, rstat, rbasis):
    groups = lax.axis_size("dp") // 4
    width = extra.shape[1]
    order = max(a.shape[1] for a in lefts)
    sizes = tuple(a.shape[1] for a in lefts)
    f32, bf16 = jnp.float32, jnp.bfloat16
    rows = HALF // groups
    away = max(groups - 1, 1)
    dma = pltpu.SemaphoreType.DMA
    vmem = pl.BlockSpec(memory_space=pltpu.VMEM)
    smem = pl.BlockSpec(memory_space=pltpu.SMEM)
    any_ = pl.BlockSpec(memory_space=pl.ANY)
    tile = (8, 128)
    shape, hold = jax.ShapeDtypeStruct, pltpu.VMEM
    return pl.pallas_call(
        functools.partial(finish_kernel, sizes),
        out_shape=[
            shape(tile, f32), shape(tile, f32), shape(field.shape, bf16),
            shape((CHIPS, 2 * HALF, width), bf16), shape((CHIPS, 2 * HALF, width), bf16),
            shape((CHIPS, order, width // 2), bf16),
            shape((CHIPS, 2, width // 2, width // 2), bf16),
        ],
        in_specs=[smem] + [vmem] * 11 + [any_] * 14,
        out_specs=[vmem] * 7,
        scratch_shapes=[
            hold((CHIPS, HALF, width), bf16), hold((CHIPS, HALF, width), bf16),
            hold((CHIPS - 1, HALF, width), bf16), hold((HALF, width), bf16),
            hold((away, rows, width), bf16), hold((HALF, width), bf16),
            hold((HALF // 2, width), bf16),
            hold((PLANE, *tile), f32), hold((groups, *tile), f32), hold((PLANE, *tile), f32),
            hold((order, order), f32), hold((order, order), f32), hold((order, order), f32),
            hold((order, width), f32), hold((order, width), f32),
            hold((width, width), f32), hold((width, width), f32),
            hold((order, order + 2 * width), f32), hold((order, order), f32),
            hold((order, width), bf16),
            hold((order, 2 * width), f32), hold((order, 2 * width), f32),
            hold((order, BLOCK), f32), hold((width, width), f32), hold((width, BLOCK), f32),
            hold((order, width), f32), hold((order, width), bf16),
            hold((2, order, width // 2), bf16),
            dma((CHIPS, 2)), dma((CHIPS, 2)),
            dma((groups, CHIPS - 1)), dma((groups, CHIPS - 1)),
            dma((away,)), dma((away,)), dma((away,)), dma((away,)),
            dma(()), dma(()),
            dma((PLANE - 1,)), dma((PLANE,)),
            dma((away,)), dma((groups,)),
            dma((PLANE - 1,)), dma((PLANE,)), dma(()), dma(()),
            dma((CHIPS - 1, 3)), dma((CHIPS, 3)), dma((CHIPS, 3)), dma((CHIPS, 3)),
            dma((6,)),
        ],
        compiler_params=pltpu.CompilerParams(
            collective_id=0, has_side_effects=True, vmem_limit_bytes=60 * 2**20
        ),
        name="finish",
    )(
        scal, *firsts, *seconds, extra, loss, field, *moms, *seconds_old, *lefts, *bases, rstat,
        rbasis,
    )


def dot(a, b):
    return jnp.dot(a, b, preferred_element_type=jnp.float32)


def dot_t(a, b):
    return lax.dot_general(a, b, (((1,), (1,)), ((), ())), preferred_element_type=jnp.float32)


def one_hot(index, first, count):
    rows = lax.broadcasted_iota(jnp.int32, (count, index.shape[1]), 0) + first
    return jnp.where(rows == index, 1.0, 0.0).astype(jnp.bfloat16)


def normalise(value):
    mean = jnp.mean(value, axis=0, keepdims=True)
    centred = value - mean
    scale = lax.rsqrt(jnp.mean(centred * centred, axis=0, keepdims=True) + 1e-05)
    return centred * scale, scale


def normalise_back(grad, hat, scale, gain):
    inner = grad * gain
    return scale * (
        inner
        - jnp.mean(inner, axis=0, keepdims=True)
        - hat * jnp.mean(inner * hat, axis=0, keepdims=True)
    )


def turned(value):
    return value.astype(jnp.float32).T.astype(jnp.bfloat16)


def step_kernel(
    inputs, targets, senders, receivers, g2m, m2g, delta, level, vec,
    edge_half, node_half, second_half, io, io_t,
    e0, e1, n0, n1, s0, s1, s2, s3, extra, loss_ref, field_ref, narrow_ref,
    send_tab, recv_tab, g2m_tab, m2g_tab, fields, goal,
    edge_w, edge_t, node_w, node_t, second_w, second_t, got_edge, got_node, got_second,
    grid, enc_hat, enc_scale, mesh, mesh_b, halo_s, halo_r,
    edge, edge_in, edge_slope, edge_hid, edge_hat, edge_scale,
    node_in, node_slope, node_hid, node_hat, node_scale, agg,
    dec_hat, dec_scale, dfinal, dmesh, dext, dedge, dpre, dtot, back_s, back_r, dvec, loss_acc,
    weight_s, weight_r, halo_ss, halo_rs, back_ss, back_rs,
    *, count_all,
):
    f32, bf16 = jnp.float32, jnp.bfloat16
    layers = edge_half.shape[0]
    width = vec.shape[0]
    nodes = mesh.shape[1]
    count_vec = 4 + 4 * layers
    edges = senders.shape[1]
    points = g2m.shape[1]
    halo = nodes // 2
    tile = 512
    fields_count = inputs.shape[1]
    dp, member = lax.axis_index("dp"), lax.axis_index("mp")
    blocks = lax.axis_size("dp")
    after, before = lax.rem(dp + 1, blocks), lax.rem(dp + blocks - 1, blocks)
    greet([(dp, 1 - member), (after, member), (before, member)])
    shard = edge_half.shape[2]
    mine = pl.ds(pl.multiple_of(member * shard, shard), shard)
    theirs = pl.ds(pl.multiple_of((1 - member) * shard, shard), shard)

    def weight_copies(layer):
        pair = pl.ds(2 * layer, 2)
        return [
            remote(src, dst, weight_s.at[layer, i], weight_r.at[layer, i], (dp, 1 - member))
            for i, (src, dst) in enumerate((
                (edge_half.at[layer], got_edge.at[layer]),
                (second_half.at[pair], got_second.at[pair]),
                (node_half.at[layer], got_node.at[layer]),
            ))
        ]

    for layer in range(layers):
        for copy in weight_copies(layer):
            copy.start()

    def place_weights(layer, edge_part, node_part, second_part, at):
        edge_w[layer, :, at] = edge_part[layer]
        edge_t[layer, at, :] = turned(edge_part[layer])
        node_w[layer, :, at] = node_part[layer]
        node_t[layer, at, :] = turned(node_part[layer])
        for i in (2 * layer, 2 * layer + 1):
            second_w[i, at, :] = second_part[i]
            second_t[i, :, at] = turned(second_part[i])

    def tiles(count, body):
        def go(j, carry):
            body(pl.ds(pl.multiple_of(j * tile, tile), tile))
            return carry

        lax.fori_loop(0, count // tile, go, 0)

    row = pl.ds(member, 1)
    fields[...] = jnp.zeros_like(fields)
    goal[...] = jnp.zeros_like(goal)
    fields[0:fields_count, :] = inputs[member]
    goal[0:fields_count, :] = targets[member] / delta[...]
    dvec[...] = jnp.zeros_like(dvec)
    loss_acc[...] = jnp.zeros_like(loss_acc)

    def gain(i):
        return vec[:, i : i + 1]

    def vec_grads(i, grad, hat):
        dvec[:, i : i + 1] += jnp.sum(grad * hat, axis=1, keepdims=True)
        dvec[:, i + 1 : i + 2] += jnp.sum(grad, axis=1, keepdims=True)

    agg[...] = jnp.zeros_like(agg)

    def encode(at):
        value = dot(io_t[0], fields[:, at])
        grid[:, at] = value
        table = one_hot(g2m[row, at], 0, nodes)
        g2m_tab[:, at] = table
        agg[...] += dot_t(value.astype(bf16), table)

    tiles(points, encode)
    hat, scale = normalise(agg[...])
    enc_hat[...] = hat
    enc_scale[...] = scale
    mesh[...] = hat * gain(0) + gain(1)

    def start_halo(layer):
        value = mesh[...].astype(bf16)
        mesh_b[layer] = value
        halo_s[layer] = value[:, :halo]
        halo_copy(layer).start()

    def halo_copy(layer):
        return remote(
            halo_s.at[layer], halo_r.at[layer], halo_ss.at[layer], halo_rs.at[layer],
            (after, member),
        )

    def back_copy(layer):
        return remote(
            back_s.at[layer], back_r.at[layer], back_ss.at[layer], back_rs.at[layer],
            (before, member),
        )

    start_halo(0)
    place_weights(0, edge_half, node_half, second_half, mine)

    def build(at):
        send_tab[:, at] = one_hot(senders[row, at], 0, nodes + halo)
        recv_tab[:, at] = one_hot(receivers[row, at], 0, nodes)

    tiles(edges, build)
    for layer in range(layers):
        def look_up(at):
            own = mesh_b[layer]
            edge_in[layer, width : 2 * width, at] = dot(own, send_tab[:nodes, at]).astype(bf16)
            edge_in[layer, 2 * width :, at] = dot(own, recv_tab[:, at]).astype(bf16)

        tiles(edges, look_up)
        for copy in weight_copies(layer):
            copy.wait_recv()
        place_weights(layer, got_edge, got_node, got_second, theirs)
        halo_copy(layer).wait_recv()
        agg[...] = jnp.zeros_like(agg)

        def edge_mlp(at):
            sent = edge_in[layer, width : 2 * width, at].astype(f32) + dot(
                halo_r[layer], send_tab[nodes:, at]
            )
            if layer == 0:
                old = sent - edge_in[layer, 2 * width :, at].astype(f32)
            else:
                old = edge[:, at]
            edge_in[layer, width : 2 * width, at] = sent.astype(bf16)
            edge_in[layer, :width, at] = old.astype(bf16)
            pre = dot(edge_t[layer], edge_in[layer, :, at])
            sigma = jax.nn.sigmoid(pre)
            edge_slope[layer, :, at] = sigma * (1.0 + pre * (1.0 - sigma))
            hidden = (pre * sigma).astype(bf16)
            edge_hid[layer, :, at] = hidden
            hat, scale = normalise(dot(second_t[2 * layer], hidden))
            edge_hat[layer, :, at] = hat
            edge_scale[layer, :, at] = scale
            new = old + hat * gain(2 + 4 * layer) + gain(3 + 4 * layer)
            edge[:, at] = new
            agg[...] += dot_t(new.astype(bf16), recv_tab[:, at])

        tiles(edges, edge_mlp)
        node_in[layer, :width] = mesh_b[layer]
        node_in[layer, width:] = agg[...].astype(bf16)
        pre = dot(node_t[layer], node_in[layer])
        sigma = jax.nn.sigmoid(pre)
        node_slope[layer] = sigma * (1.0 + pre * (1.0 - sigma))
        hidden = (pre * sigma).astype(bf16)
        node_hid[layer] = hidden
        hat, scale = normalise(dot(second_t[2 * layer + 1], hidden))
        node_hat[layer] = hat
        node_scale[layer] = scale
        mesh[...] = mesh[...] + hat * gain(4 + 4 * layer) + gain(5 + 4 * layer)
        if layer + 1 < layers:
            start_halo(layer + 1)
            place_weights(layer + 1, edge_half, node_half, second_half, mine)

    mesh_b[layers] = mesh[...].astype(bf16)
    dmesh[...] = jnp.zeros_like(dmesh)
    extra[...] = jnp.zeros_like(extra)
    dext[:, :width] = jnp.zeros((width, width), f32)

    def decode(at):
        index = m2g[member, :, at]
        table = sum(one_hot(index[i : i + 1], 0, nodes).astype(f32) for i in range(3)).astype(bf16)
        m2g_tab[:, at] = table
        hat, scale = normalise(dot(mesh_b[layers], table))
        final = (grid[:, at] + hat * gain(count_vec - 2) + gain(count_vec - 1)).astype(bf16)
        resid = dot(io[1], final) - goal[:, at]
        weighted = level[...] * resid
        squares = weighted * resid
        loss_acc[...] += jnp.sum(squares, axis=0, keepdims=True)
        dpred = (weighted * (2.0 / count_all)).astype(bf16)
        dext[: dpred.shape[0], :width] += dot_t(dpred, final)
        grad = dot(io_t[1], dpred)
        dfinal[:, at] = grad
        vec_grads(count_vec - 2, grad, hat)
        ddecoded = normalise_back(grad, hat, scale, gain(count_vec - 2))
        dmesh[...] += dot_t(ddecoded.astype(bf16), table)

    tiles(points, decode)
    io_rows = io.shape[1]
    extra[io_rows : 2 * io_rows, :] = dext[:io_rows, :width].astype(bf16)
    loss_ref[...] = jnp.broadcast_to(
        jnp.sum(loss_acc[...], axis=1, keepdims=True) * (1.0 / 1024.0), loss_ref.shape
    )

    firsts, nexts, seconds = (e0, e1), (n0, n1), (s0, s1, s2, s3)
    for layer in reversed(range(layers)):
        grad, hat = dmesh[...], node_hat[layer]
        vec_grads(4 + 4 * layer, grad, hat)
        total = normalise_back(grad, hat, node_scale[layer], gain(4 + 4 * layer)).astype(bf16)
        seconds[2 * layer + 1][...] = dot_t(node_hid[layer], total).astype(bf16)
        dnode = (dot(second_w[2 * layer + 1], total) * node_slope[layer]).astype(bf16)
        nexts[layer][...] = dot_t(node_in[layer], dnode).astype(bf16)
        dmesh[...] = grad + dot(node_w[layer, :width], dnode)
        agg[...] = dot(node_w[layer, width:], dnode)
        dext[...] = jnp.zeros_like(dext)

        def edge_back(at):
            grad = dot(agg[...].astype(bf16), recv_tab[:, at])
            if layer + 1 < layers:
                grad = grad + dedge[:, at]
            hat = edge_hat[layer, :, at]
            vec_grads(2 + 4 * layer, grad, hat)
            total = normalise_back(
                grad, hat, edge_scale[layer, :, at], gain(2 + 4 * layer)
            ).astype(bf16)
            dtot[:, at] = total
            dhid = dot(second_w[2 * layer], total)
            small = (dhid * edge_slope[layer, :, at]).astype(bf16)
            dpre[:, at] = small
            dself = grad + dot(edge_w[layer, :width], small)
            dsent = dot(edge_w[layer, width : 2 * width], small)
            drecv = dot(edge_w[layer, 2 * width :], small)
            if layer == 0:
                dsent = dsent + dself
                drecv = drecv - dself
            else:
                dedge[:, at] = dself
            dext[...] += dot_t(dsent.astype(bf16), send_tab[:, at])
            dmesh[...] += dot_t(drecv.astype(bf16), recv_tab[:, at])

        tiles(edges, edge_back)
        back_s[layer] = dext[:, nodes:].astype(bf16)
        back_copy(layer).start()
        dmesh[...] += dext[:, :nodes]
        seconds[2 * layer][...] = dot_t(edge_hid[layer], dtot[...]).astype(bf16)

        def weight_grad(i, carry):
            at = pl.ds(pl.multiple_of(i * width, width), width)
            firsts[layer][at, :] = dot_t(edge_in[layer, at, :], dpre[...]).astype(bf16)
            return carry

        lax.fori_loop(0, 3, weight_grad, 0)
        back_copy(layer).wait_recv()
        dmesh[:, :halo] += back_r[layer].astype(f32)

    grad, hat = dmesh[...], enc_hat[...]
    vec_grads(0, grad, hat)
    agg[...] = normalise_back(grad, hat, enc_scale[...], gain(0))
    dext[:io_rows, :width] = jnp.zeros((io_rows, width), f32)

    def encode_back(at):
        dgrid = (dfinal[:, at] + dot(agg[...].astype(bf16), g2m_tab[:, at])).astype(bf16)
        dext[:io_rows, :width] += dot_t(fields[:, at], dgrid)
        out = dot(io[0], dgrid)[:fields_count] * count_all
        field_ref[:, at] = out
        narrow_ref[:, at] = out.astype(bf16)

    tiles(points, encode_back)
    extra[:io_rows, :] = dext[:io_rows, :width].astype(bf16)
    extra[2 * io_rows : 3 * io_rows, :] = dvec[...].T.astype(bf16)
    for layer in range(layers):
        for copy in weight_copies(layer):
            copy.wait_send()
        halo_copy(layer).wait_send()
        back_copy(layer).wait_send()


def train_step(
    inputs, targets, senders, receivers, g2m, m2g, delta, level, vec,
    edge_half, node_half, second_half, io, io_t, count_all,
):
    f32, bf16 = jnp.float32, jnp.bfloat16
    layers, width = edge_half.shape[0], vec.shape[0]
    nodes, halo = NODE_DEV, NODE_DEV // 2
    edges, points = senders.shape[1], g2m.shape[1]
    fields_count, io_rows = inputs.shape[1], io.shape[1]
    tall, node_tall = edge_half.shape[1], node_half.shape[1]
    dma = pltpu.SemaphoreType.DMA
    vmem = pl.BlockSpec(memory_space=pltpu.VMEM)
    shape = jax.ShapeDtypeStruct
    hold = pltpu.VMEM
    return pl.pallas_call(
        functools.partial(step_kernel, count_all=count_all),
        out_shape=[shape((tall, width), bf16)] * layers
        + [shape((node_tall, width), bf16)] * layers
        + [shape((width, width), bf16)] * (2 * layers)
        + [
            shape((HALF, width), bf16), shape((8, 128), f32),
            shape((fields_count, points), f32), shape((fields_count, points), bf16),
        ],
        in_specs=[vmem] * 14,
        out_specs=[vmem] * (4 * layers + 4),
        scratch_shapes=[
            hold((nodes + halo, edges), bf16), hold((nodes, edges), bf16),
            hold((nodes, points), bf16), hold((nodes, points), bf16),
            hold((io_rows, points), bf16), hold((io_rows, points), f32),
            hold((layers, tall, width), bf16), hold((layers, width, tall), bf16),
            hold((layers, node_tall, width), bf16), hold((layers, width, node_tall), bf16),
            hold((2 * layers, width, width), bf16), hold((2 * layers, width, width), bf16),
            hold(edge_half.shape, bf16), hold(node_half.shape, bf16), hold(second_half.shape, bf16),
            hold((width, points), f32), hold((width, nodes), f32), hold((1, nodes), f32),
            hold((width, nodes), f32), hold((layers + 1, width, nodes), bf16),
            hold((layers, width, halo), bf16), hold((layers, width, halo), bf16),
            hold((width, edges), f32), hold((layers, tall, edges), bf16),
            hold((layers, width, edges), f32), hold((layers, width, edges), bf16),
            hold((layers, width, edges), f32), hold((layers, 1, edges), f32),
            hold((layers, node_tall, nodes), bf16),
            hold((layers, width, nodes), f32), hold((layers, width, nodes), bf16),
            hold((layers, width, nodes), f32), hold((layers, 1, nodes), f32),
            hold((width, nodes), f32),
            hold((width, points), f32), hold((1, points), f32),
            hold((width, points), f32), hold((width, nodes), f32),
            hold((width, nodes + halo), f32), hold((width, edges), f32),
            hold((width, edges), bf16), hold((width, edges), bf16),
            hold((layers, width, halo), bf16), hold((layers, width, halo), bf16),
            hold((width, 128), f32), hold((1, 512), f32),
            dma((layers, 3)), dma((layers, 3)),
            dma((layers,)), dma((layers,)), dma((layers,)), dma((layers,)),
        ],
        compiler_params=pltpu.CompilerParams(
            collective_id=2, has_side_effects=True, vmem_limit_bytes=60 * 2**20
        ),
        name="train_step",
    )(
        inputs, targets, senders, receivers, g2m, m2g, delta, level, vec,
        edge_half, node_half, second_half, io, io_t,
    )


def adamw(weight, grad, moment, second_moment, corr_one, corr_two, decay, rate):
    moment = BETA_ONE * moment + (1.0 - BETA_ONE) * grad
    second_moment = BETA_TWO * second_moment + (1.0 - BETA_TWO) * grad * grad
    weight = weight - rate * (
        moment / corr_one / (jnp.sqrt(second_moment / corr_two) + EPSILON) + decay * weight
    )
    return (weight, moment, second_moment)


def body(
    inputs, targets, senders, receivers, g2m_dst, m2g_src, delta_scale, level_index, step_count,
    soap_owner, edge_first, node_first, second, io_weights, vectors,
    edge_first_m, node_first_m, second_m, edge_first_v, node_first_v, second_v,
    io_m, io_v, vector_m, vector_v,
    edge_left_stat, edge_left_basis, node_left_stat, node_left_basis,
    second_left_stat, second_left_basis, right_stat, right_basis,
):
    layers = edge_first.shape[0]
    micro = inputs.shape[0]
    width = vectors.shape[1]
    fields_count = inputs.shape[1]
    member = lax.axis_index("mp")
    count_all = float(micro * fields_count * inputs.shape[2] * lax.axis_size("dp"))
    io_rows = 128
    narrow = lambda a: a.astype(jnp.bfloat16)
    column = lambda a: a.astype(jnp.float32)[:, None]
    io = jnp.pad(narrow(io_weights), ((0, 0), (0, io_rows - fields_count), (0, 0)))
    level = jnp.pad(column((level_index + 1).astype(jnp.float32) / LEVELS), ((0, io_rows - fields_count), (0, 0)))
    *grads, extra, loss_tile, field_grad, field_narrow = train_step(
        inputs, targets, senders, receivers, g2m_dst, m2g_src, column(delta_scale), level,
        vectors.T, narrow(edge_first), narrow(node_first), narrow(second),
        io, jnp.swapaxes(io, 1, 2), count_all,
    )
    steps = step_count.astype(jnp.float32)
    corr_one = 1.0 - jnp.power(BETA_ONE, steps)
    corr_two = 1.0 - jnp.power(BETA_TWO, steps)
    norm_tile, loss_tile, field_away, gall, rall, ufirst, usecond = finish(
        jnp.stack([corr_one, corr_two]), grads[: 2 * layers], grads[2 * layers :], extra,
        loss_tile, field_narrow,
        (edge_first_m, node_first_m, second_m),
        (edge_first_v, node_first_v, second_v),
        (edge_left_stat, node_left_stat, second_left_stat),
        (edge_left_basis, node_left_basis, second_left_basis),
        right_stat, right_basis,
    )
    field_away = field_away.astype(jnp.float32)
    first = member == 0
    input_grad = jnp.stack(
        [jnp.where(first, field_grad, field_away), jnp.where(first, field_away, field_grad)]
    )
    loss = jnp.sum(loss_tile) / count_all
    grad_norm = jnp.sqrt(jnp.sum(norm_tile))
    clip = jnp.minimum(1.0, CLIP / (grad_norm + 1e-06))

    def cut(a):
        wide = a.astype(jnp.float32)
        return (
            wide[:layers, : 3 * width], wide[layers:, :HALF], wide[:, 3 * width :],
            wide[layers:, HALF : 3 * width],
        )

    grads, turned = cut(gall), cut(rall)
    firsts, seconds_out = [], []
    for k, (mom, sec) in enumerate(
        ((edge_first_m, edge_first_v), (node_first_m, node_first_v), (second_m, second_v))
    ):
        firsts.append(BETA_ONE * mom + (1.0 - BETA_ONE) * (clip * grads[k]))
        seconds_out.append(BETA_TWO * sec + (1.0 - BETA_TWO) * turned[k] * turned[k])
    new_edge = edge_first - RATE * (
        ufirst[:layers].astype(jnp.float32) + DECAY * edge_first
    )
    new_node = node_first - RATE * (
        ufirst[layers:, :HALF].astype(jnp.float32) + DECAY * node_first
    )
    upd_second = jnp.concatenate([usecond[:, 0], usecond[:, 1]], axis=2)
    new_second = second - RATE * (upd_second.astype(jnp.float32) + DECAY * second)
    rest = grads[3].reshape(HALF, width)
    grad_io = rest.reshape(-1, io_rows, width)[:2, :fields_count]
    grad_vectors = rest[2 * io_rows : 2 * io_rows + vectors.shape[0]]
    new_io, m_io, v_io = adamw(
        io_weights, grad_io * clip, io_m, io_v, corr_one, corr_two, DECAY, RATE
    )
    new_vec, m_vec, v_vec = adamw(
        vectors, grad_vectors * clip, vector_m, vector_v, corr_one, corr_two, 0.0, VECTOR_RATE
    )
    return (
        loss,
        grad_norm,
        new_edge,
        new_edge.astype(jnp.bfloat16),
        new_node,
        new_node.astype(jnp.bfloat16),
        new_second,
        new_second.astype(jnp.bfloat16),
        new_io,
        new_io.astype(jnp.bfloat16),
        new_vec,
        new_vec.astype(jnp.bfloat16),
        *firsts,
        *seconds_out,
        m_io,
        v_io,
        m_vec,
        v_vec,
        input_grad,
    )


def solution(mesh):
    return jax.shard_map(
        body,
        mesh=mesh,
        in_specs=(
            P(None, None, "dp"),
            P(None, None, "dp"),
            P(None, "dp"),
            P(None, "dp"),
            P(None, "dp"),
            P(None, None, "dp"),
            P(),
            P(),
            P(),
            P(),
            P(None, None, "mp"),
            P(None, None, "mp"),
            P(None, "mp", None),
            P(),
            P(),
            P(),
            P(),
            P(),
            P(),
            P(),
            P(),
            P(),
            P(),
            P(),
            P(),
            P(),
            P(),
            P(),
            P(),
            P(),
            P(),
            P(),
            P(),
        ),
        out_specs=(
            P(),
            P(),
            P(None, None, "mp"),
            P(None, None, "mp"),
            P(None, None, "mp"),
            P(None, None, "mp"),
            P(None, "mp", None),
            P(None, "mp", None),
            P(),
            P(),
            P(),
            P(),
            P(),
            P(),
            P(),
            P(),
            P(),
            P(),
            P(),
            P(),
            P(),
            P(),
            P(None, None, "dp"),
        ),
        check_vma=False,
    )
```

```python
import functools

import jax
import jax.numpy as jnp
from jax import lax
from jax.experimental import pallas as pl
from jax.experimental.pallas import tpu as pltpu
from jax.sharding import PartitionSpec as P

LEVELS = 13
NODE_DEV = 512
CLIP = 0.0005
BETA_ONE = 0.9
BETA_TWO = 0.99
STAT_BETA = 0.95
EPSILON = 1e-08
RATE = 0.15
VECTOR_RATE = 0.7
DECAY = 0.01
HIGH = lax.Precision.HIGHEST

BLOCK = 128
AHEAD = 4
STAT_SCALE = 2.0**28
HALF = 512
CHIPS = 4
PLANE = 8


def mm(a, b, lhs=1, rhs=0):
    return lax.dot_general(
        a, b, (((lhs,), (rhs,)), ((), ())), precision=HIGH, preferred_element_type=jnp.float32
    )


def mm3(a, b, lhs=1, rhs=0):
    total = None
    for _ in range(3):
        high = a.astype(jnp.bfloat16)
        a = a - high.astype(jnp.float32)
        part = lax.dot_general(
            high, b, (((lhs,), (rhs,)), ((), ())), preferred_element_type=jnp.float32
        )
        total = part if total is None else total + part
    return total


def mid(a, b, lhs=1, rhs=0):
    def go(x, y):
        return lax.dot_general(
            x, y, (((lhs,), (rhs,)), ((), ())), preferred_element_type=jnp.float32
        )

    a_high, b_high = a.astype(jnp.bfloat16), b.astype(jnp.bfloat16)
    a_low = (a - a_high.astype(jnp.float32)).astype(jnp.bfloat16)
    b_low = (b - b_high.astype(jnp.float32)).astype(jnp.bfloat16)
    return go(a_high, b_low) + go(a_low, b_high) + go(a_high, b_high)


def half_inverses(blocks):
    size = BLOCK // 2
    tiles = size // 8
    shape = (8, BLOCK)
    sub = lax.broadcasted_iota(jnp.int32, shape, 0)
    row = lax.broadcasted_iota(jnp.int32, (size, size), 0)
    unit = jnp.where(row == lax.broadcasted_iota(jnp.int32, (size, size), 1), 1.0, 0.0)

    def line(tile, s):
        return jnp.broadcast_to(tile[s : s + 1, :], shape)

    states = []
    for block in blocks:
        wide = jnp.concatenate([block, unit.astype(jnp.float32)], axis=1)
        rows = [wide[8 * t : 8 * t + 8, :] for t in range(tiles)]
        cols = {
            j: [jnp.broadcast_to(rows[t][:, j : j + 1], shape) for t in range(tiles)]
            for j in range(AHEAD)
        }
        states.append([rows, cols, line(cols[0][0], 0), [jnp.ones(shape, jnp.float32)] * tiles])
    for j in range(size):
        first, s = divmod(j, 8)
        for state in states:
            rows, cols, pivot, scale = state
            recip = 1.0 / pivot
            scale[first] = jnp.where(sub == s, pivot, scale[first])
            if j + 1 < size:
                near, at = divmod(j + 1, 8)
                entry = line(cols[j + 1][first], s)
                state[2] = line(cols[j + 1][near], at) - entry * entry * recip
            col = cols.pop(j)
            factor = [None if t < first else col[t] * recip for t in range(tiles)]
            factor[first] = jnp.where(sub > s, factor[first], 0.0)
            for ahead in range(j + 1, min(j + AHEAD, size)):
                entry = line(cols[ahead][first], s)
                for t in range(first, tiles):
                    cols[ahead][t] = cols[ahead][t] - factor[t] * entry
            row = line(rows[first], s)
            for t in range(first, tiles):
                rows[t] = rows[t] - factor[t] * row
            if j + AHEAD < size:
                at = j + AHEAD
                cols[at] = [
                    jnp.broadcast_to(rows[t][:, at : at + 1], shape) if t >= first else None
                    for t in range(tiles)
                ]
    results = []
    for rows, _, _, scale in states:
        whole = jnp.concatenate([rows[t] * lax.rsqrt(scale[t]) for t in range(tiles)], axis=0)
        results.append(whole[:, size:])
    return results


def inverse_factors(blocks):
    half = BLOCK // 2
    tops = half_inverses([block[:half, :half] for block in blocks])
    ups = [mm(top, block[:half, half:]) for top, block in zip(tops, blocks)]
    lows = half_inverses([block[half:, half:] - mm(up, up, 0, 0) for up, block in zip(ups, blocks)])
    results = []
    for top, up, low in zip(tops, ups, lows):
        cross = mm(low, mm(up, top, 0, 0))
        results.append(jnp.concatenate([
            jnp.concatenate([top, jnp.zeros_like(top)], axis=1),
            jnp.concatenate([-cross, low], axis=1),
        ], axis=0))
    return results


def place():
    dp = lax.axis_index("dp")
    core = lax.rem(dp, 2)
    chip = 2 * lax.axis_index("mp") + lax.rem(lax.div(dp, 2), 2)
    return core, chip, 2 * chip + core, lax.div(dp, 4), lax.axis_size("dp") // 4


def device(core, chip, group):
    return (4 * group + 2 * lax.rem(chip, 2) + core, lax.div(chip, 2))


def other(core, chip, turn):
    spot = lax.rem(2 * chip + core + turn, PLANE)
    return lax.rem(spot, 2), lax.div(spot, 2), spot


def remote(src, dst, send, recv, target):
    return pltpu.make_async_remote_copy(
        src_ref=src, dst_ref=dst, send_sem=send, recv_sem=recv, device_id=target,
        device_id_type=pl.DeviceIdType.MESH,
    )


def greet(targets):
    barrier = pltpu.get_barrier_semaphore()
    for target in targets:
        pl.semaphore_signal(
            barrier, inc=1, device_id=target, device_id_type=pl.DeviceIdType.MESH
        )
    pl.semaphore_wait(barrier, len(targets))


def fold(value):
    rows = jnp.sum(value.reshape(value.shape[0] // 8, 8, value.shape[1]), axis=0)
    return rows[:, :128] + rows[:, 128:]


def finish_kernel(
    sizes,
    scal_ref,
    e0, e1, n0, n1, s0, s1, s2, s3, extra, loss_ref, field_ref,
    m0, m1, m2,
    v0, v1, v2,
    ls0, ls1, ls2,
    lb0, lb1, lb2,
    rs_hbm, rb_hbm,
    norm_ref, total_ref, away_ref, rest_ref, ufirst, usecond, om0, om1, om2, ov0, ov1, ov2,
    gall, rall, from_core, acc, from_plane, part, from_group, full, tail,
    plane_loss, group_loss, plane_norm,
    stat, basis, turned_basis, moment, second, rstat, rbasis, table, gram, grad,
    left, right, inv, rgram, rinv, solved, old_moment, rot_s, upd_s,
    core_s, core_r, plane_s, plane_r, group_s, group_r, full_s, full_r, tail_s, tail_r,
    ploss_s, ploss_r, gloss_s, gloss_r, norm_s, norm_r, field_s, field_r,
    far_s, far_r, near_s, near_r, sems, old_sems, own_s,
):
    f32, bf16 = jnp.float32, jnp.bfloat16
    core, chip, spot, group, groups = place()
    order, width = moment.shape
    blocks, wide = order // BLOCK, order // width
    layers = m0.shape[0]
    kind = jnp.where(core == 1, 2, lax.div(chip, layers))
    matrix = CHIPS * core + chip
    keep, fresh = STAT_SCALE * STAT_BETA, STAT_SCALE * (1.0 - STAT_BETA)

    def block(i):
        return pl.ds(pl.multiple_of(i * width, width), width)

    def state_copies(k):
        size = sizes[k]
        index = chip if k == 2 else lax.rem(chip, layers)
        inside = pl.ds(0, size)
        pairs = [
            ((ls0, ls1, ls2)[k].at[index], stat.at[inside, inside]),
            ((lb0, lb1, lb2)[k].at[index], basis.at[inside, inside]),
            ((m0, m1, m2)[k].at[index], moment.at[inside]),
            ((v0, v1, v2)[k].at[index], second.at[inside]),
            (rs_hbm.at[matrix], rstat),
            (rb_hbm.at[matrix], rbasis),
        ]
        return [pltpu.make_async_copy(a, b, sems.at[i]) for i, (a, b) in enumerate(pairs)]

    def start_states():
        for k, size in enumerate(sizes):
            @pl.when(kind == k)
            def _():
                if size < order:
                    def pad(i, carry):
                        band = pl.ds(pl.multiple_of(i * 32, 32), 32)
                        row = lax.broadcasted_iota(jnp.int32, (32, order), 0) + i * 32
                        col = lax.broadcasted_iota(jnp.int32, (32, order), 1)
                        unit = jnp.where(row == col, 1.0, 0.0).astype(f32)
                        stat[band, :] = unit * (1.0 / STAT_SCALE)
                        basis[band, :] = unit
                        moment[band, :] = jnp.zeros((32, width), f32)
                        second[band, :] = jnp.zeros((32, width), f32)
                        return carry

                    lax.fori_loop(0, order // 32, pad, 0)
                for copy in state_copies(k):
                    copy.start()

    def all_copies(which):
        olds, news = ((m0, m1, m2), (v0, v1, v2))[which], ((om0, om1, om2), (ov0, ov1, ov2))[which]
        return [
            pltpu.make_async_copy(old, new, old_sems.at[which, k])
            for k, (old, new) in enumerate(zip(olds, news))
        ]

    def wait_states():
        for k in range(len(sizes)):
            @pl.when(kind == k)
            def _():
                for copy in state_copies(k):
                    copy.wait()

    def tall(p):
        return 3 * width if p < 2 else HALF

    def spots(c, p, i):
        if c == 0:
            rows = pl.ds(0, HALF if i == 0 else tall(p))
            return (gall, rall, ufirst)[i].at[p, rows]
        if i == 2:
            return usecond.at[p]
        first, count = ((HALF, HALF), (3 * width, width))[i]
        return (gall, rall)[i].at[p, pl.ds(first, count)]

    def own(c, p, i, ref, other_member):
        if i == 0:
            return ref
        rows = pl.ds(0, tall(p) if c == 0 else width)
        if i == 1:
            return ref.at[rows]
        if c == 0:
            return ref.at[other_member, rows]
        side = pl.ds(pl.multiple_of(other_member * (width // 2), width // 2), width // 2)
        return ref.at[:, side]

    def branches():
        for c in range(2):
            for p in range(CHIPS):
                yield c, p, (core == c) & (chip == p)

    def send_far(i, ref, _):
        for c, p, here in branches():
            @pl.when(here)
            def _():
                to = spots(c, p, i)
                for t in range(1, CHIPS):
                    q = lax.rem(chip + t, CHIPS)
                    remote(
                        own(c, p, i, ref, lax.div(q, 2)), to, far_s.at[t - 1, i],
                        far_r.at[p, i], device(core, q, group),
                    ).start()
                mine = own(c, p, i, ref, lax.div(chip, 2))
                remote(mine, to, near_s.at[p, i], near_r.at[p, i], partner).start()
                pltpu.make_async_copy(mine, to, own_s.at[i]).start()

    def forward(i):
        for c in range(2):
            for p in range(CHIPS):
                @pl.when((core == c) & (chip != p))
                def _():
                    to = spots(c, p, i)
                    remote(to, to, far_s.at[0, i], far_r.at[p, i], partner).wait_recv()
                    remote(to, to, near_s.at[p, i], near_r.at[p, i], partner).start()

    rows = HALF // groups
    partner = device(1 - core, chip, group)
    plane = [device(*other(core, chip, t)[:2], group) for t in range(1, PLANE)]
    along = [device(core, chip, lax.rem(group + t, groups)) for t in range(1, groups)]
    start_states()
    for which in range(2):
        for copy in all_copies(which):
            copy.start()
    greet(plane + along)

    quarter = HALF // 2
    pieces = {0: [[(ref, 0, HALF, 0)] for ref in (e0, e1, n0, n1)], 1: []}
    for p, (ref, begin) in enumerate(((e0, HALF), (e1, HALF), (extra, 0), (extra, quarter))):
        pieces[1].append([(ref, begin, quarter, 0), ((s0, s1, s2, s3)[p], 0, quarter, quarter)])

    def core_copy(p, i, piece):
        ref, begin, size, to = piece
        return remote(
            ref.at[pl.ds(begin, size)], from_core.at[p, pl.ds(to, size)],
            core_s.at[p, i], core_r.at[p, i], partner,
        )

    for c in range(2):
        @pl.when(core == c)
        def _():
            for p in range(CHIPS):
                for i, piece in enumerate(pieces[1 - c][p]):
                    core_copy(p, i, piece).start()

    loss_sends = []
    for t in range(1, PLANE):
        copy = remote(
            loss_ref, plane_loss.at[spot], ploss_s.at[t - 1], ploss_r.at[spot], plane[t - 1]
        )
        copy.start()
        loss_sends.append(copy)
    plane_loss[spot] = loss_ref[...]

    def chunk(index):
        return pl.ds(pl.multiple_of(index * rows, rows), rows)

    def plane_copy(p, turn, index):
        return remote(
            acc.at[p, chunk(index)], from_plane.at[turn - 1, chunk(index)],
            plane_s.at[index, turn - 1], plane_r.at[index, turn - 1], device(core, p, group),
        )

    for p in range(CHIPS):
        for c in range(2):
            @pl.when(core == c)
            def _():
                for i, piece in enumerate(pieces[c][p]):
                    ref, begin, size, to = piece
                    core_copy(p, i, piece).wait_recv()
                    total = ref[begin : begin + size, :].astype(f32) + from_core[
                        p, to : to + size, :
                    ].astype(f32)
                    acc[p, to : to + size, :] = total.astype(bf16)
        turn = lax.rem(p - chip + CHIPS, CHIPS)

        @pl.when(turn != 0)
        def _():
            def go(i, carry):
                plane_copy(p, turn, lax.rem(group + i, groups)).start()
                return carry

            lax.fori_loop(1, groups + 1, go, 0)

    wait_states()
    turned_basis[...] = basis[...].T

    def product(j, carry):
        at = block(j)
        table[:, at] = keep * mm(turned_basis[...], stat[:, at])
        return carry

    lax.fori_loop(0, wide, product, 0)

    def old_gram(j, carry):
        def one(i, carry):
            gram[block(i), block(j)] = mm(table[block(i), :order], table[block(j), :order], 1, 1)
            return carry

        return lax.fori_loop(0, j + 1, one, carry)

    for t in range(1, PLANE):
        _, _, source = other(core, chip, t)
        remote(
            loss_ref, plane_loss.at[source], ploss_s.at[t - 1], ploss_r.at[source], partner
        ).wait_recv()
    total = plane_loss[0]
    for t in range(1, PLANE):
        total = total + plane_loss[t]
    group_loss[group] = total
    for t in range(1, groups):
        copy = remote(
            group_loss.at[group], group_loss.at[group], gloss_s.at[t - 1], gloss_r.at[group],
            along[t - 1],
        )
        copy.start()
        loss_sends.append(copy)

    def gather_plane(index):
        total = acc[chip, chunk(index), :].astype(f32)
        for turn in range(1, CHIPS):
            plane_copy(chip, turn, index).wait_recv()
            total = total + from_plane[turn - 1, chunk(index), :].astype(f32)
        return total

    def group_copy(turn):
        target = lax.rem(group + turn, groups)
        return remote(
            part.at[chunk(target)], from_group.at[turn - 1], group_s.at[turn - 1],
            group_r.at[turn - 1], device(core, chip, target),
        )

    def plane_step(turn, carry):
        target = lax.rem(group + turn, groups)
        part[chunk(target), :] = gather_plane(target).astype(bf16)
        group_copy(turn).start()
        return carry

    lax.fori_loop(1, groups, plane_step, 0)
    lax.fori_loop(0, wide - 1, old_gram, 0)

    def group_step(turn, total):
        group_copy(turn).wait_recv()
        return total + from_group[turn - 1].astype(f32)

    total = lax.fori_loop(1, groups, group_step, gather_plane(group))
    full[chunk(group), :] = total.astype(bf16)

    def full_copy(turn, owner, target):
        return remote(
            full.at[chunk(owner)], full.at[chunk(owner)], full_s.at[turn - 1],
            full_r.at[turn - 1], device(core, chip, target),
        )

    def full_go(turn, carry):
        full_copy(turn, group, lax.rem(group + turn, groups)).start()
        return carry

    def full_wait(turn, carry):
        full_copy(turn, lax.rem(group + groups - turn, groups), group).wait_recv()
        return carry

    lax.fori_loop(1, groups, full_go, 0)
    lax.fori_loop(wide - 1, wide, old_gram, 0)

    def moment_rows(i, carry):
        old_moment[block(i), :] = mm(table[block(i), :order], moment[...])
        return carry

    lax.fori_loop(0, wide, moment_rows, 0)
    stat[...] = table[:, :order]
    basis[...] = stat[...].T
    lax.fori_loop(1, groups, full_wait, 0)

    field = remote(
        field_ref, away_ref, field_s, field_r,
        device(core, lax.rem(chip + CHIPS // 2, CHIPS), group),
    )
    field.start()
    swap = remote(full.at[pl.ds(0, quarter)], tail, tail_s, tail_r, partner)
    swap.start()
    send_far(0, full, full)
    squares = full[...].astype(f32)
    plane_norm[spot] = fold(squares * squares)
    norm_sends = []
    for t in range(1, PLANE):
        copy = remote(
            plane_norm.at[spot], plane_norm.at[spot], norm_s.at[t - 1], norm_r.at[spot],
            plane[t - 1],
        )
        copy.start()
        norm_sends.append(copy)
    for t in range(1, groups):
        source = lax.rem(group + t, groups)
        remote(
            group_loss.at[source], group_loss.at[source], gloss_s.at[t - 1], gloss_r.at[source],
            partner,
        ).wait_recv()
    total = group_loss[0]
    for t in range(1, groups):
        total = total + group_loss[t]
    total_ref[...] = total
    swap.wait_recv()
    grad[...] = jnp.zeros_like(grad)
    for k, size in enumerate(sizes):
        @pl.when(kind == k)
        def _():
            held = HALF if k < 2 else width
            grad[:held, :] = full[HALF - held :, :]
            if size > HALF:
                grad[HALF:size, :] = tail[: size - HALF, :]

    raw = grad[...]

    def grad_rows(i, carry):
        left[block(i), width:] = mm3(turned_basis[block(i), :], grad[...])
        left[block(i), :width] = mm3(stat[block(i), :], grad[...])
        return carry

    lax.fori_loop(0, wide, grad_rows, 0)
    square = lax.dot_general(raw, raw, (((0,), (0,)), ((), ())), preferred_element_type=f32)
    grad_moment = mm3(moment[...], raw, 0, 0).T
    for t in range(1, PLANE):
        _, _, source = other(core, chip, t)
        remote(
            plane_norm.at[source], plane_norm.at[source], norm_s.at[t - 1], norm_r.at[source],
            partner,
        ).wait_recv()
    total = plane_norm[0]
    for t in range(1, PLANE):
        total = total + plane_norm[t]
    norm_ref[...] = total
    norm = jnp.sqrt(jnp.sum(jnp.sum(total, axis=0, keepdims=True), axis=1, keepdims=True))
    clip = jnp.minimum(1.0, CLIP / (norm + 1e-06))


    turned_grad = left[:, width:] * clip
    product_grad = left[:, :width] * clip
    square = square * (clip * clip)
    grad_moment = BETA_ONE * clip * grad_moment + (1.0 - BETA_ONE) * square
    left[:, :width] = fresh * product_grad + (0.5 * fresh * fresh) * mm(turned_grad, square)
    left[:, width:] = turned_grad
    right[:, :width] = turned_grad
    right[:, width:] = left[:, :width]

    def new_gram(j, carry):
        def one(i, carry):
            table[block(i), block(j)] = gram[block(i), block(j)] + mm(
                left[block(i), :], right[block(j), :], 1, 1
            )
            return carry

        return lax.fori_loop(0, j + 1, one, carry)

    lax.fori_loop(0, wide, new_gram, 0)
    table[:, order : order + width] = product_grad + fresh * mm(turned_grad, square)
    table[:, order + width :] = (
        BETA_ONE * old_moment[...]
        + (1.0 - BETA_ONE) * product_grad
        + fresh * mm(turned_grad, grad_moment)
    )
    rstat[...] = keep * rstat[...] + fresh * square
    rbasis[...] = mm(rstat[...], rbasis[...])
    rgram[...] = mm(rbasis[...], rbasis[...], 0, 0)

    def panel(k):
        at = pl.ds(pl.multiple_of(k * BLOCK, BLOCK), BLOCK)
        table[at, :] = mm(inv[at, :], table[at, :])

        @pl.when(lax.rem(k, 2) == 0)
        def _():
            rows = pl.ds(pl.multiple_of(k * BLOCK + BLOCK, BLOCK), BLOCK)
            table[rows, :] = table[rows, :] - mm(table[at, rows], table[at, :], 0, 0)

        @pl.when(lax.rem(k, 2) == 1)
        def _():
            now = lax.div(k, 2)

            def trail(i, carry):
                table[block(i), :] = table[block(i), :] - mm(
                    table[block(now), block(i)], table[block(now), :], 0, 0
                )
                return carry

            lax.fori_loop(now + 1, wide, trail, 0)

    def two(k, carry):
        at = pl.ds(pl.multiple_of(k * BLOCK, BLOCK), BLOCK)
        inv[at, :], rinv[at, :] = inverse_factors([table[at, at], rgram[at, at]])

        @pl.when(k == 0)
        def _():
            upper = mm(rinv[:BLOCK, :], rgram[:BLOCK, BLOCK:])
            rgram[:BLOCK, BLOCK:] = upper
            rgram[BLOCK:, BLOCK:] = rgram[BLOCK:, BLOCK:] - mm(upper, upper, 0, 0)

        panel(k)
        return carry

    def one(k, carry):
        at = pl.ds(pl.multiple_of(k * BLOCK, BLOCK), BLOCK)
        inv[at, :] = inverse_factors([table[at, at]])[0]
        panel(k)
        return carry

    lax.fori_loop(0, width // BLOCK, two, 0)
    forward(0)
    lax.fori_loop(width // BLOCK, blocks, one, 0)
    left_part = mm(rbasis[:, :BLOCK], rinv[:BLOCK, :], 1, 1)
    right_part = mm(
        rbasis[:, BLOCK:] - mm(left_part, rgram[:BLOCK, BLOCK:]), rinv[BLOCK:, :], 1, 1
    )
    rbasis[:, :BLOCK] = left_part
    rbasis[:, BLOCK:] = right_part
    rot = mid(table[:, order : order + width], rbasis[...])
    rot_s[...] = rot.astype(bf16)
    send_far(1, rot_s, rot_s)
    corr_one, corr_two = scal_ref[0], scal_ref[1]
    rotated = mid(table[:, order + width :], rbasis[...])
    grown = BETA_TWO * second[...] + (1.0 - BETA_TWO) * rot * rot
    normed = rotated / corr_one / (jnp.sqrt(grown / corr_two) + EPSILON)
    second[...] = mid(normed, rbasis[...], 1, 1)

    def back(step, carry):
        k = blocks - 1 - step
        at = pl.ds(pl.multiple_of(k * BLOCK, BLOCK), BLOCK)
        part = mid(inv[at, :], second[at, :], 0, 0)
        solved[at, :] = part
        second[...] = second[...] - mid(table[:, at], part)
        return carry

    lax.fori_loop(0, blocks, back, 0)
    forward(1)
    inner = mid(left[:, width:], solved[...], 0, 0)

    def update_rows(i, carry):
        at = block(i)
        update = mid(basis[at, :], solved[...]) + (fresh * clip) * mid(grad[at, :].astype(f32), inner)
        update = update.astype(bf16)
        upd_s[0, at, :] = update[:, : width // 2]
        upd_s[1, at, :] = update[:, width // 2 :]
        return carry

    lax.fori_loop(0, wide, update_rows, 0)
    send_far(2, upd_s, upd_s)
    def arrive(i):
        ref = (full, rot_s, upd_s)[i]
        for c, p, here in branches():
            @pl.when(here)
            def _():
                mine = own(c, p, i, ref, lax.div(chip, 2))
                pltpu.make_async_copy(mine, spots(c, p, i), own_s.at[i]).wait()

        for c in range(2):
            @pl.when(core == c)
            def _():
                for p in range(CHIPS):
                    to = spots(1 - c, p, i)
                    remote(to, to, near_s.at[p, i], near_r.at[p, i], partner).wait_recv()

    for which in range(2):
        for copy in all_copies(which):
            copy.wait()
        arrive(which)
        for k, new in enumerate(((om0, om1, om2), (ov0, ov1, ov2))[which]):
            high = sizes[k] // width

            def moments(step, carry):
                i, b = lax.div(step, high), lax.rem(step, high)
                p = i + layers if k == 1 else i
                value = (gall, rall)[which][p, block(b + 3 if k == 2 else b), :].astype(f32)
                if which == 0:
                    new[i, block(b), :] = BETA_ONE * new[i, block(b), :] + (1.0 - BETA_ONE) * (
                        clip * value
                    )
                else:
                    new[i, block(b), :] = (
                        BETA_TWO * new[i, block(b), :] + (1.0 - BETA_TWO) * value * value
                    )
                return carry

            lax.fori_loop(0, new.shape[0] * high, moments, 0)
    for p in range(2):
        rest_ref[p] = gall[p + 2, HALF : 3 * width, :]
    forward(2)
    arrive(2)

    field.wait()
    swap.wait_send()
    for copy in loss_sends + norm_sends:
        copy.wait_send()
    for c in range(2):
        @pl.when(core == c)
        def _():
            for p in range(CHIPS):
                for i, piece in enumerate(pieces[1 - c][p]):
                    core_copy(p, i, piece).wait_send()
    def plane_done(index, carry):
        for turn in range(1, CHIPS):
            plane_copy(lax.rem(chip + turn, CHIPS), turn, index).wait_send()
        return carry

    lax.fori_loop(0, groups, plane_done, 0)

    def group_done(turn, carry):
        group_copy(turn).wait_send()
        full_copy(turn, group, group).wait_send()
        return carry

    lax.fori_loop(1, groups, group_done, 0)
    for i in range(3):
        for c in range(2):
            @pl.when(core == c)
            def _():
                for p in range(CHIPS):
                    to = spots(c, p, i)
                    remote(to, to, near_s.at[p, i], near_r.at[p, i], partner).wait_send()
        for c, p, here in branches():
            @pl.when(here)
            def _():
                for t in range(1, CHIPS):
                    to = spots(c, p, i)
                    remote(to, to, far_s.at[t - 1, i], far_r.at[p, i], partner).wait_send()


def finish(scal, firsts, seconds, extra, loss, field, moms, seconds_old, lefts, bases, rstat, rbasis):
    groups = lax.axis_size("dp") // 4
    width = extra.shape[1]
    order = max(a.shape[1] for a in lefts)
    sizes = tuple(a.shape[1] for a in lefts)
    f32, bf16 = jnp.float32, jnp.bfloat16
    rows = HALF // groups
    away = max(groups - 1, 1)
    dma = pltpu.SemaphoreType.DMA
    vmem = pl.BlockSpec(memory_space=pltpu.VMEM)
    smem = pl.BlockSpec(memory_space=pltpu.SMEM)
    any_ = pl.BlockSpec(memory_space=pl.ANY)
    tile = (8, 128)
    shape, hold = jax.ShapeDtypeStruct, pltpu.VMEM
    return pl.pallas_call(
        functools.partial(finish_kernel, sizes),
        out_shape=[
            shape(tile, f32), shape(tile, f32), shape(field.shape, bf16),
            shape((2, width, width), bf16),
            shape((CHIPS, order, width // 2), bf16),
            shape((CHIPS, 2, width // 2, width // 2), bf16),
        ] + [shape(a.shape, f32) for a in (*moms, *seconds_old)],
        in_specs=[smem] + [vmem] * 11 + [any_] * 14,
        out_specs=[vmem] * 12,
        scratch_shapes=[
            hold((CHIPS, 2 * HALF, width), bf16), hold((CHIPS, 2 * HALF, width), bf16),
            hold((CHIPS, HALF, width), bf16), hold((CHIPS, HALF, width), bf16),
            hold((CHIPS - 1, HALF, width), bf16), hold((HALF, width), bf16),
            hold((away, rows, width), bf16), hold((HALF, width), bf16),
            hold((HALF // 2, width), bf16),
            hold((PLANE, *tile), f32), hold((groups, *tile), f32), hold((PLANE, *tile), f32),
            hold((order, order), f32), hold((order, order), f32), hold((order, order), f32),
            hold((order, width), f32), hold((order, width), f32),
            hold((width, width), f32), hold((width, width), f32),
            hold((order, order + 2 * width), f32), hold((order, order), f32),
            hold((order, width), bf16),
            hold((order, 2 * width), f32), hold((order, 2 * width), f32),
            hold((order, BLOCK), f32), hold((width, width), f32), hold((width, BLOCK), f32),
            hold((order, width), f32), hold((order, width), f32), hold((order, width), bf16),
            hold((2, order, width // 2), bf16),
            dma((CHIPS, 2)), dma((CHIPS, 2)),
            dma((groups, CHIPS - 1)), dma((groups, CHIPS - 1)),
            dma((away,)), dma((away,)), dma((away,)), dma((away,)),
            dma(()), dma(()),
            dma((PLANE - 1,)), dma((PLANE,)),
            dma((away,)), dma((groups,)),
            dma((PLANE - 1,)), dma((PLANE,)), dma(()), dma(()),
            dma((CHIPS - 1, 3)), dma((CHIPS, 3)), dma((CHIPS, 3)), dma((CHIPS, 3)),
            dma((6,)), dma((2, 3)), dma((3,)),
        ],
        compiler_params=pltpu.CompilerParams(
            collective_id=0, has_side_effects=True, vmem_limit_bytes=60 * 2**20
        ),
        name="finish",
    )(
        scal, *firsts, *seconds, extra, loss, field, *moms, *seconds_old, *lefts, *bases, rstat,
        rbasis,
    )


def dot(a, b):
    return jnp.dot(a, b, preferred_element_type=jnp.float32)


def dot_t(a, b):
    return lax.dot_general(a, b, (((1,), (1,)), ((), ())), preferred_element_type=jnp.float32)


def one_hot(index, first, count):
    rows = lax.broadcasted_iota(jnp.int32, (count, index.shape[1]), 0) + first
    return jnp.where(rows == index, 1.0, 0.0).astype(jnp.bfloat16)


def normalise(value):
    mean = jnp.mean(value, axis=0, keepdims=True)
    centred = value - mean
    scale = lax.rsqrt(jnp.mean(centred * centred, axis=0, keepdims=True) + 1e-05)
    return centred * scale, scale


def normalise_back(grad, hat, scale, gain):
    inner = grad * gain
    return scale * (
        inner
        - jnp.mean(inner, axis=0, keepdims=True)
        - hat * jnp.mean(inner * hat, axis=0, keepdims=True)
    )


def turned(value):
    return value.astype(jnp.float32).T.astype(jnp.bfloat16)


def step_kernel(
    inputs, targets, senders_hbm, receivers_hbm, g2m_hbm, m2g, delta_hbm, level_hbm,
    vec_hbm, edge_hbm, node_hbm, second_hbm, io_wide,
    e0, e1, n0, n1, s0, s1, s2, s3, extra, loss_ref, field_ref, narrow_ref,
    send_tab, recv_tab, g2m_tab, m2g_tab, fields, goal,
    edge_w, edge_t, node_w, node_t, second_w, second_t, got_edge, got_node, got_second,
    grid, enc_hat, enc_scale, mesh, mesh_b, halo_s, halo_r,
    edge, edge_in, edge_slope, edge_hid, edge_hat, edge_scale,
    node_in, node_slope, node_hid, node_hat, node_scale, agg,
    dec_hat, dec_scale, dfinal, dmesh, dext, dedge, dpre, dtot, back_s, back_r, dvec, loss_acc,
    senders, receivers, g2m, delta_row, level_row, vec_rows,
    edge_wide, node_wide, second_wide,
    edge_half, node_half, second_half, io, io_t, vec, small,
    weight_s, weight_r, halo_ss, halo_rs, back_ss, back_rs, fetch,
    *, count_all,
):
    f32, bf16 = jnp.float32, jnp.bfloat16
    layers = edge_half.shape[0]
    width = vec_rows.shape[1]
    nodes = mesh.shape[1]
    count_vec = 4 + 4 * layers
    edges = senders.shape[1]
    points = g2m.shape[1]
    halo = nodes // 2
    tile = 1024
    fields_count = inputs.shape[1]
    dp, member = lax.axis_index("dp"), lax.axis_index("mp")
    blocks = lax.axis_size("dp")
    after, before = lax.rem(dp + 1, blocks), lax.rem(dp + blocks - 1, blocks)
    fetches = [
        pltpu.make_async_copy(src, dst, fetch.at[i])
        for i, (src, dst) in enumerate((
            (edge_hbm, edge_wide), (node_hbm, node_wide), (second_hbm, second_wide),
            (senders_hbm, senders), (receivers_hbm, receivers), (g2m_hbm, g2m),
            (delta_hbm, delta_row), (level_hbm, level_row), (vec_hbm, vec_rows),
        ))
    ]
    for copy in fetches:
        copy.start()
    io[...] = jnp.zeros_like(io)
    vec[...] = jnp.zeros_like(vec)
    small[...] = jnp.zeros_like(small)
    greet([(dp, 1 - member), (after, member), (before, member)])
    for copy in fetches[:3]:
        copy.wait()
    edge_half[...] = edge_wide[...].astype(bf16)
    node_half[...] = node_wide[...].astype(bf16)
    second_half[...] = second_wide[...].astype(bf16)
    shard = edge_half.shape[2]
    mine = pl.ds(pl.multiple_of(member * shard, shard), shard)
    theirs = pl.ds(pl.multiple_of((1 - member) * shard, shard), shard)

    def weight_copies(layer):
        pair = pl.ds(2 * layer, 2)
        return [
            remote(src, dst, weight_s.at[layer, i], weight_r.at[layer, i], (dp, 1 - member))
            for i, (src, dst) in enumerate((
                (edge_half.at[layer], got_edge.at[layer]),
                (second_half.at[pair], got_second.at[pair]),
                (node_half.at[layer], got_node.at[layer]),
            ))
        ]

    for layer in range(layers):
        for copy in weight_copies(layer):
            copy.start()

    def place_weights(layer, edge_part, node_part, second_part, at):
        edge_w[layer, :, at] = edge_part[layer]
        edge_t[layer, at, :] = turned(edge_part[layer])
        node_w[layer, :, at] = node_part[layer]
        node_t[layer, at, :] = turned(node_part[layer])
        for i in (2 * layer, 2 * layer + 1):
            second_w[i, at, :] = second_part[i]
            second_t[i, :, at] = turned(second_part[i])

    def tiles(count, body):
        tile = count

        def go(j, carry):
            body(pl.ds(pl.multiple_of(j * tile, tile), tile))
            return carry

        lax.fori_loop(0, count // tile, go, 0)

    row = pl.ds(member, 1)
    for copy in fetches[3:]:
        copy.wait()
    for i in range(2):
        io[i, :fields_count, :] = io_wide[i].astype(bf16)
        io_t[i] = turned(io[i])
    vec[: vec_rows.shape[0], :] = vec_rows[...]
    vec[...] = vec[...].T
    small[0:1, :fields_count] = delta_row[...]
    small[1:2, :fields_count] = (level_row[...] + 1).astype(f32) / LEVELS
    small[...] = small[...].T
    fields[...] = jnp.zeros_like(fields)
    goal[...] = jnp.zeros_like(goal)
    fields[0:fields_count, :] = inputs[member]
    goal[0:fields_count, :] = targets[member] / small[:fields_count, 0:1]
    dvec[...] = jnp.zeros_like(dvec)
    loss_acc[...] = jnp.zeros_like(loss_acc)

    def gain(i):
        return vec[:, i : i + 1]

    def vec_grads(i, grad, hat):
        dvec[:, i : i + 1] += jnp.sum(grad * hat, axis=1, keepdims=True)
        dvec[:, i + 1 : i + 2] += jnp.sum(grad, axis=1, keepdims=True)

    agg[...] = jnp.zeros_like(agg)

    def encode(at):
        value = dot(io_t[0], fields[:, at])
        grid[:, at] = value
        table = one_hot(g2m[row, at], 0, nodes)
        g2m_tab[:, at] = table
        agg[...] += dot_t(value.astype(bf16), table)

    tiles(points, encode)
    hat, scale = normalise(agg[...])
    enc_hat[...] = hat
    enc_scale[...] = scale
    mesh[...] = hat * gain(0) + gain(1)

    def start_halo(layer):
        value = mesh[...].astype(bf16)
        mesh_b[layer] = value
        halo_s[layer] = value[:, :halo]
        halo_copy(layer).start()

    def halo_copy(layer):
        return remote(
            halo_s.at[layer], halo_r.at[layer], halo_ss.at[layer], halo_rs.at[layer],
            (after, member),
        )

    def back_copy(layer):
        return remote(
            back_s.at[layer], back_r.at[layer], back_ss.at[layer], back_rs.at[layer],
            (before, member),
        )

    start_halo(0)
    place_weights(0, edge_half, node_half, second_half, mine)

    def build(at):
        send_tab[:, at] = one_hot(senders[row, at], 0, nodes + halo)
        recv_tab[:, at] = one_hot(receivers[row, at], 0, nodes)

    tiles(edges, build)
    for layer in range(layers):
        def look_up(at):
            own = mesh_b[layer]
            edge_in[layer, width : 2 * width, at] = dot(own, send_tab[:nodes, at]).astype(bf16)
            edge_in[layer, 2 * width :, at] = dot(own, recv_tab[:, at]).astype(bf16)

        tiles(edges, look_up)
        for copy in weight_copies(layer):
            copy.wait_recv()
        place_weights(layer, got_edge, got_node, got_second, theirs)
        halo_copy(layer).wait_recv()
        agg[...] = jnp.zeros_like(agg)

        def edge_mlp(at):
            sent = edge_in[layer, width : 2 * width, at].astype(f32) + dot(
                halo_r[layer], send_tab[nodes:, at]
            )
            if layer == 0:
                old = sent - edge_in[layer, 2 * width :, at].astype(f32)
            else:
                old = edge[:, at]
            edge_in[layer, width : 2 * width, at] = sent.astype(bf16)
            edge_in[layer, :width, at] = old.astype(bf16)
            pre = dot(edge_t[layer], edge_in[layer, :, at])
            sigma = jax.nn.sigmoid(pre)
            edge_slope[layer, :, at] = sigma * (1.0 + pre * (1.0 - sigma))
            hidden = (pre * sigma).astype(bf16)
            edge_hid[layer, :, at] = hidden
            hat, scale = normalise(dot(second_t[2 * layer], hidden))
            edge_hat[layer, :, at] = hat
            edge_scale[layer, :, at] = scale
            new = old + hat * gain(2 + 4 * layer) + gain(3 + 4 * layer)
            edge[:, at] = new
            agg[...] += dot_t(new.astype(bf16), recv_tab[:, at])

        tiles(edges, edge_mlp)
        node_in[layer, :width] = mesh_b[layer]
        node_in[layer, width:] = agg[...].astype(bf16)
        pre = dot(node_t[layer], node_in[layer])
        sigma = jax.nn.sigmoid(pre)
        node_slope[layer] = sigma * (1.0 + pre * (1.0 - sigma))
        hidden = (pre * sigma).astype(bf16)
        node_hid[layer] = hidden
        hat, scale = normalise(dot(second_t[2 * layer + 1], hidden))
        node_hat[layer] = hat
        node_scale[layer] = scale
        mesh[...] = mesh[...] + hat * gain(4 + 4 * layer) + gain(5 + 4 * layer)
        if layer + 1 < layers:
            start_halo(layer + 1)
            place_weights(layer + 1, edge_half, node_half, second_half, mine)

    mesh_b[layers] = mesh[...].astype(bf16)
    dmesh[...] = jnp.zeros_like(dmesh)
    extra[...] = jnp.zeros_like(extra)
    dext[:, :width] = jnp.zeros((width, width), f32)

    def decode(at):
        index = m2g[member, :, at]
        table = sum(one_hot(index[i : i + 1], 0, nodes).astype(f32) for i in range(3)).astype(bf16)
        m2g_tab[:, at] = table
        hat, scale = normalise(dot(mesh_b[layers], table))
        final = (grid[:, at] + hat * gain(count_vec - 2) + gain(count_vec - 1)).astype(bf16)
        resid = dot(io[1], final) - goal[:, at]
        weighted = small[:, 1:2] * resid
        squares = weighted * resid
        loss_acc[...] += jnp.sum(squares, axis=0, keepdims=True)
        dpred = (weighted * (2.0 / count_all)).astype(bf16)
        dext[: dpred.shape[0], :width] += dot_t(dpred, final)
        grad = dot(io_t[1], dpred)
        dfinal[:, at] = grad
        vec_grads(count_vec - 2, grad, hat)
        ddecoded = normalise_back(grad, hat, scale, gain(count_vec - 2))
        dmesh[...] += dot_t(ddecoded.astype(bf16), table)

    tiles(points, decode)
    io_rows = io.shape[1]
    extra[io_rows : 2 * io_rows, :] = dext[:io_rows, :width].astype(bf16)
    loss_ref[...] = jnp.broadcast_to(
        jnp.sum(loss_acc[...], axis=1, keepdims=True) * (1.0 / 1024.0), loss_ref.shape
    )

    firsts, nexts, seconds = (e0, e1), (n0, n1), (s0, s1, s2, s3)
    for layer in reversed(range(layers)):
        grad, hat = dmesh[...], node_hat[layer]
        vec_grads(4 + 4 * layer, grad, hat)
        total = normalise_back(grad, hat, node_scale[layer], gain(4 + 4 * layer)).astype(bf16)
        seconds[2 * layer + 1][...] = dot_t(node_hid[layer], total).astype(bf16)
        dnode = (dot(second_w[2 * layer + 1], total) * node_slope[layer]).astype(bf16)
        nexts[layer][...] = dot_t(node_in[layer], dnode).astype(bf16)
        dmesh[...] = grad + dot(node_w[layer, :width], dnode)
        agg[...] = dot(node_w[layer, width:], dnode)
        dext[...] = jnp.zeros_like(dext)

        def edge_back(at):
            grad = dot(agg[...].astype(bf16), recv_tab[:, at])
            if layer + 1 < layers:
                grad = grad + dedge[:, at]
            hat = edge_hat[layer, :, at]
            vec_grads(2 + 4 * layer, grad, hat)
            total = normalise_back(
                grad, hat, edge_scale[layer, :, at], gain(2 + 4 * layer)
            ).astype(bf16)
            dtot[:, at] = total
            dhid = dot(second_w[2 * layer], total)
            small = (dhid * edge_slope[layer, :, at]).astype(bf16)
            dpre[:, at] = small
            dself = grad + dot(edge_w[layer, :width], small)
            dsent = dot(edge_w[layer, width : 2 * width], small)
            drecv = dot(edge_w[layer, 2 * width :], small)
            if layer == 0:
                dsent = dsent + dself
                drecv = drecv - dself
            else:
                dedge[:, at] = dself
            dext[...] += dot_t(dsent.astype(bf16), send_tab[:, at])
            dmesh[...] += dot_t(drecv.astype(bf16), recv_tab[:, at])

        tiles(edges, edge_back)
        back_s[layer] = dext[:, nodes:].astype(bf16)
        back_copy(layer).start()
        dmesh[...] += dext[:, :nodes]
        seconds[2 * layer][...] = dot_t(edge_hid[layer], dtot[...]).astype(bf16)

        def weight_grad(i, carry):
            at = pl.ds(pl.multiple_of(i * width, width), width)
            firsts[layer][at, :] = dot_t(edge_in[layer, at, :], dpre[...]).astype(bf16)
            return carry

        lax.fori_loop(0, 3, weight_grad, 0)
        back_copy(layer).wait_recv()
        dmesh[:, :halo] += back_r[layer].astype(f32)

    grad, hat = dmesh[...], enc_hat[...]
    vec_grads(0, grad, hat)
    agg[...] = normalise_back(grad, hat, enc_scale[...], gain(0))
    dext[:io_rows, :width] = jnp.zeros((io_rows, width), f32)

    def encode_back(at):
        dgrid = (dfinal[:, at] + dot(agg[...].astype(bf16), g2m_tab[:, at])).astype(bf16)
        dext[:io_rows, :width] += dot_t(fields[:, at], dgrid)
        out = dot(io[0], dgrid)[:fields_count] * count_all
        field_ref[:, at] = out
        narrow_ref[:, at] = out.astype(bf16)

    tiles(points, encode_back)
    extra[:io_rows, :] = dext[:io_rows, :width].astype(bf16)
    extra[2 * io_rows : 3 * io_rows, :] = dvec[...].T.astype(bf16)
    for layer in range(layers):
        for copy in weight_copies(layer):
            copy.wait_send()
        halo_copy(layer).wait_send()
        back_copy(layer).wait_send()


def train_step(
    inputs, targets, senders, receivers, g2m, m2g, delta, level, vec,
    edge_half, node_half, second_half, io, count_all,
):
    f32, bf16 = jnp.float32, jnp.bfloat16
    layers, width = edge_half.shape[0], vec.shape[1]
    nodes, halo = NODE_DEV, NODE_DEV // 2
    edges, points = senders.shape[1], g2m.shape[1]
    fields_count, io_rows = inputs.shape[1], BLOCK
    i32 = jnp.int32
    any_ = pl.BlockSpec(memory_space=pl.ANY)
    tall, node_tall = edge_half.shape[1], node_half.shape[1]
    dma = pltpu.SemaphoreType.DMA
    vmem = pl.BlockSpec(memory_space=pltpu.VMEM)
    shape = jax.ShapeDtypeStruct
    hold = pltpu.VMEM
    return pl.pallas_call(
        functools.partial(step_kernel, count_all=count_all),
        out_shape=[shape((tall, width), bf16)] * layers
        + [shape((node_tall, width), bf16)] * layers
        + [shape((width, width), bf16)] * (2 * layers)
        + [
            shape((HALF, width), bf16), shape((8, 128), f32),
            shape((fields_count, points), f32), shape((fields_count, points), bf16),
        ],
        in_specs=[vmem] * 2 + [any_] * 3 + [vmem] + [any_] * 6 + [vmem],
        out_specs=[vmem] * (4 * layers + 4),
        scratch_shapes=[
            hold((nodes + halo, edges), bf16), hold((nodes, edges), bf16),
            hold((nodes, points), bf16), hold((nodes, points), bf16),
            hold((io_rows, points), bf16), hold((io_rows, points), f32),
            hold((layers, tall, width), bf16), hold((layers, width, tall), bf16),
            hold((layers, node_tall, width), bf16), hold((layers, width, node_tall), bf16),
            hold((2 * layers, width, width), bf16), hold((2 * layers, width, width), bf16),
            hold(edge_half.shape, bf16), hold(node_half.shape, bf16), hold(second_half.shape, bf16),
            hold((width, points), f32), hold((width, nodes), f32), hold((1, nodes), f32),
            hold((width, nodes), f32), hold((layers + 1, width, nodes), bf16),
            hold((layers, width, halo), bf16), hold((layers, width, halo), bf16),
            hold((width, edges), f32), hold((layers, tall, edges), bf16),
            hold((layers, width, edges), f32), hold((layers, width, edges), bf16),
            hold((layers, width, edges), f32), hold((layers, 1, edges), f32),
            hold((layers, node_tall, nodes), bf16),
            hold((layers, width, nodes), f32), hold((layers, width, nodes), bf16),
            hold((layers, width, nodes), f32), hold((layers, 1, nodes), f32),
            hold((width, nodes), f32),
            hold((width, points), f32), hold((1, points), f32),
            hold((width, points), f32), hold((width, nodes), f32),
            hold((width, nodes + halo), f32), hold((width, edges), f32),
            hold((width, edges), bf16), hold((width, edges), bf16),
            hold((layers, width, halo), bf16), hold((layers, width, halo), bf16),
            hold((width, 128), f32), hold((1, 1024), f32),
            hold(senders.shape, i32), hold(receivers.shape, i32), hold(g2m.shape, i32),
            hold(delta.shape, f32), hold(level.shape, i32),
            hold(vec.shape, f32), hold(edge_half.shape, f32), hold(node_half.shape, f32),
            hold(second_half.shape, f32),
            hold(edge_half.shape, bf16), hold(node_half.shape, bf16),
            hold(second_half.shape, bf16), hold((2, io_rows, width), bf16),
            hold((2, width, io_rows), bf16), hold((width, width), f32), hold((128, 128), f32),
            dma((layers, 3)), dma((layers, 3)),
            dma((layers,)), dma((layers,)), dma((layers,)), dma((layers,)), dma((9,)),
        ],
        compiler_params=pltpu.CompilerParams(
            collective_id=2, has_side_effects=True, vmem_limit_bytes=60 * 2**20
        ),
        name="train_step",
    )(
        inputs, targets, senders, receivers, g2m, m2g, delta, level, vec,
        edge_half, node_half, second_half, io,
    )


def adamw(weight, grad, moment, second_moment, corr_one, corr_two, decay, rate):
    moment = BETA_ONE * moment + (1.0 - BETA_ONE) * grad
    second_moment = BETA_TWO * second_moment + (1.0 - BETA_TWO) * grad * grad
    weight = weight - rate * (
        moment / corr_one / (jnp.sqrt(second_moment / corr_two) + EPSILON) + decay * weight
    )
    return (weight, moment, second_moment)


def body(
    inputs, targets, senders, receivers, g2m_dst, m2g_src, delta_scale, level_index, step_count,
    soap_owner, edge_first, node_first, second, io_weights, vectors,
    edge_first_m, node_first_m, second_m, edge_first_v, node_first_v, second_v,
    io_m, io_v, vector_m, vector_v,
    edge_left_stat, edge_left_basis, node_left_stat, node_left_basis,
    second_left_stat, second_left_basis, right_stat, right_basis,
):
    layers = edge_first.shape[0]
    micro = inputs.shape[0]
    width = vectors.shape[1]
    fields_count = inputs.shape[1]
    member = lax.axis_index("mp")
    count_all = float(micro * fields_count * inputs.shape[2] * lax.axis_size("dp"))
    io_rows = BLOCK
    *grads, extra, loss_tile, field_grad, field_narrow = train_step(
        inputs, targets, senders, receivers, g2m_dst, m2g_src, delta_scale[None],
        level_index[None], vectors, edge_first, node_first, second, io_weights, count_all,
    )
    steps = step_count.astype(jnp.float32)
    corr_one = 1.0 - jnp.power(BETA_ONE, steps)
    corr_two = 1.0 - jnp.power(BETA_TWO, steps)
    norm_tile, loss_tile, field_away, rest, ufirst, usecond, *moments = finish(
        jnp.stack([corr_one, corr_two]), grads[: 2 * layers], grads[2 * layers :], extra,
        loss_tile, field_narrow,
        (edge_first_m, node_first_m, second_m),
        (edge_first_v, node_first_v, second_v),
        (edge_left_stat, node_left_stat, second_left_stat),
        (edge_left_basis, node_left_basis, second_left_basis),
        right_stat, right_basis,
    )
    field_away = field_away.astype(jnp.float32)
    first = member == 0
    input_grad = jnp.stack(
        [jnp.where(first, field_grad, field_away), jnp.where(first, field_away, field_grad)]
    )
    loss = jnp.sum(loss_tile) / count_all
    grad_norm = jnp.sqrt(jnp.sum(norm_tile))
    clip = jnp.minimum(1.0, CLIP / (grad_norm + 1e-06))

    firsts, seconds_out = moments[:3], moments[3:]
    new_edge = edge_first - RATE * (
        ufirst[:layers].astype(jnp.float32) + DECAY * edge_first
    )
    new_node = node_first - RATE * (
        ufirst[layers:, :HALF].astype(jnp.float32) + DECAY * node_first
    )
    upd_second = jnp.concatenate([usecond[:, 0], usecond[:, 1]], axis=2)
    new_second = second - RATE * (upd_second.astype(jnp.float32) + DECAY * second)
    rest = rest.astype(jnp.float32).reshape(HALF, width)
    grad_io = rest.reshape(-1, io_rows, width)[:2, :fields_count]
    grad_vectors = rest[2 * io_rows : 2 * io_rows + vectors.shape[0]]
    new_io, m_io, v_io = adamw(
        io_weights, grad_io * clip, io_m, io_v, corr_one, corr_two, DECAY, RATE
    )
    new_vec, m_vec, v_vec = adamw(
        vectors, grad_vectors * clip, vector_m, vector_v, corr_one, corr_two, 0.0, VECTOR_RATE
    )
    return (
        loss,
        grad_norm,
        new_edge,
        new_edge.astype(jnp.bfloat16),
        new_node,
        new_node.astype(jnp.bfloat16),
        new_second,
        new_second.astype(jnp.bfloat16),
        new_io,
        new_io.astype(jnp.bfloat16),
        new_vec,
        new_vec.astype(jnp.bfloat16),
        *firsts,
        *seconds_out,
        m_io,
        v_io,
        m_vec,
        v_vec,
        input_grad,
    )


def solution(mesh):
    return jax.shard_map(
        body,
        mesh=mesh,
        in_specs=(
            P(None, None, "dp"),
            P(None, None, "dp"),
            P(None, "dp"),
            P(None, "dp"),
            P(None, "dp"),
            P(None, None, "dp"),
            P(),
            P(),
            P(),
            P(),
            P(None, None, "mp"),
            P(None, None, "mp"),
            P(None, "mp", None),
            P(),
            P(),
            P(),
            P(),
            P(),
            P(),
            P(),
            P(),
            P(),
            P(),
            P(),
            P(),
            P(),
            P(),
            P(),
            P(),
            P(),
            P(),
            P(),
            P(),
        ),
        out_specs=(
            P(),
            P(),
            P(None, None, "mp"),
            P(None, None, "mp"),
            P(None, None, "mp"),
            P(None, None, "mp"),
            P(None, "mp", None),
            P(None, "mp", None),
            P(),
            P(),
            P(),
            P(),
            P(),
            P(),
            P(),
            P(),
            P(),
            P(),
            P(),
            P(),
            P(),
            P(),
            P(None, None, "dp"),
        ),
        check_vma=False,
    )
```

```python
import functools

import jax
import jax.numpy as jnp
from jax import lax
from jax.experimental import pallas as pl
from jax.experimental.pallas import tpu as pltpu
from jax.sharding import PartitionSpec as P

LEVELS = 13
NODE_DEV = 512
CLIP = 0.0005
BETA_ONE = 0.9
BETA_TWO = 0.99
STAT_BETA = 0.95
EPSILON = 1e-08
RATE = 0.15
VECTOR_RATE = 0.7
DECAY = 0.01
HIGH = lax.Precision.HIGHEST

BLOCK = 128
AHEAD = 8
STAT_SCALE = 2.0**28
HALF = 512
CHIPS = 4
PLANE = 8


def mm(a, b, lhs=1, rhs=0):
    return lax.dot_general(
        a, b, (((lhs,), (rhs,)), ((), ())), precision=HIGH, preferred_element_type=jnp.float32
    )


def mm3(a, b, lhs=1, rhs=0):
    total = None
    for _ in range(3):
        high = a.astype(jnp.bfloat16)
        a = a - high.astype(jnp.float32)
        part = lax.dot_general(
            high, b, (((lhs,), (rhs,)), ((), ())), preferred_element_type=jnp.float32
        )
        total = part if total is None else total + part
    return total


def mid(a, b, lhs=1, rhs=0):
    def go(x, y):
        return lax.dot_general(
            x, y, (((lhs,), (rhs,)), ((), ())), preferred_element_type=jnp.float32
        )

    a_high, b_high = a.astype(jnp.bfloat16), b.astype(jnp.bfloat16)
    a_low = (a - a_high.astype(jnp.float32)).astype(jnp.bfloat16)
    b_low = (b - b_high.astype(jnp.float32)).astype(jnp.bfloat16)
    return go(a_high, b_low) + go(a_low, b_high) + go(a_high, b_high)


def half_inverses(blocks):
    size = BLOCK // 2
    tiles = size // 8
    shape = (8, BLOCK)
    sub = lax.broadcasted_iota(jnp.int32, shape, 0)
    row = lax.broadcasted_iota(jnp.int32, (size, size), 0)
    unit = jnp.where(row == lax.broadcasted_iota(jnp.int32, (size, size), 1), 1.0, 0.0)

    def line(tile, s):
        return jnp.broadcast_to(tile[s : s + 1, :], shape)

    states = []
    for block in blocks:
        wide = jnp.concatenate([block, unit.astype(jnp.float32)], axis=1)
        rows = [wide[8 * t : 8 * t + 8, :] for t in range(tiles)]
        cols = {
            j: [jnp.broadcast_to(rows[t][:, j : j + 1], shape) for t in range(tiles)]
            for j in range(AHEAD)
        }
        states.append([rows, cols, line(cols[0][0], 0), [jnp.ones(shape, jnp.float32)] * tiles])
    for j in range(size):
        first, s = divmod(j, 8)
        for state in states:
            rows, cols, pivot, scale = state
            recip = 1.0 / pivot
            scale[first] = jnp.where(sub == s, pivot, scale[first])
            if j + 1 < size:
                near, at = divmod(j + 1, 8)
                entry = line(cols[j + 1][first], s)
                state[2] = line(cols[j + 1][near], at) - entry * entry * recip
            col = cols.pop(j)
            factor = [None if t < first else col[t] * recip for t in range(tiles)]
            factor[first] = jnp.where(sub > s, factor[first], 0.0)
            for ahead in range(j + 1, min(j + AHEAD, size)):
                entry = line(cols[ahead][first], s)
                for t in range(first, tiles):
                    cols[ahead][t] = cols[ahead][t] - factor[t] * entry
            row = line(rows[first], s)
            for t in range(first, tiles):
                rows[t] = rows[t] - factor[t] * row
            if j + AHEAD < size:
                at = j + AHEAD
                cols[at] = [
                    jnp.broadcast_to(rows[t][:, at : at + 1], shape) if t >= first else None
                    for t in range(tiles)
                ]
    results = []
    for rows, _, _, scale in states:
        whole = jnp.concatenate([rows[t] * lax.rsqrt(scale[t]) for t in range(tiles)], axis=0)
        results.append(whole[:, size:])
    return results


def inverse_factors(blocks):
    half = BLOCK // 2
    tops = half_inverses([block[:half, :half] for block in blocks])
    ups = [mm(top, block[:half, half:]) for top, block in zip(tops, blocks)]
    lows = half_inverses([block[half:, half:] - mm(up, up, 0, 0) for up, block in zip(ups, blocks)])
    results = []
    for top, up, low in zip(tops, ups, lows):
        cross = mm(low, mm(up, top, 0, 0))
        results.append(jnp.concatenate([
            jnp.concatenate([top, jnp.zeros_like(top)], axis=1),
            jnp.concatenate([-cross, low], axis=1),
        ], axis=0))
    return results


def place():
    dp = lax.axis_index("dp")
    core = lax.rem(dp, 2)
    chip = 2 * lax.axis_index("mp") + lax.rem(lax.div(dp, 2), 2)
    return core, chip, 2 * chip + core, lax.div(dp, 4), lax.axis_size("dp") // 4


def device(core, chip, group):
    return (4 * group + 2 * lax.rem(chip, 2) + core, lax.div(chip, 2))


def other(core, chip, turn):
    spot = lax.rem(2 * chip + core + turn, PLANE)
    return lax.rem(spot, 2), lax.div(spot, 2), spot


def remote(src, dst, send, recv, target):
    return pltpu.make_async_remote_copy(
        src_ref=src, dst_ref=dst, send_sem=send, recv_sem=recv, device_id=target,
        device_id_type=pl.DeviceIdType.MESH,
    )


def greet(targets):
    barrier = pltpu.get_barrier_semaphore()
    for target in targets:
        pl.semaphore_signal(
            barrier, inc=1, device_id=target, device_id_type=pl.DeviceIdType.MESH
        )
    pl.semaphore_wait(barrier, len(targets))


def fold(value):
    rows = jnp.sum(value.reshape(value.shape[0] // 8, 8, value.shape[1]), axis=0)
    return rows[:, :128] + rows[:, 128:]


def finish_kernel(
    sizes,
    scal_ref,
    e0, e1, n0, n1, s0, s1, s2, s3, extra, loss_ref, field_ref,
    m0, m1, m2,
    v0, v1, v2,
    ls0, ls1, ls2,
    lb0, lb1, lb2,
    rs_hbm, rb_hbm,
    norm_ref, total_ref, away_ref, rest_ref, ufirst, usecond, om0, om1, om2, ov0, ov1, ov2,
    gall, rall, from_core, acc, from_plane, part, from_group, full, tail,
    plane_loss, group_loss, plane_norm,
    stat, basis, turned_basis, moment, second, rstat, rbasis, table, gram, grad,
    left, right, inv, rgram, rinv, solved, old_moment, rot_s, upd_s,
    core_s, core_r, plane_s, plane_r, group_s, group_r, full_s, full_r, tail_s, tail_r,
    ploss_s, ploss_r, gloss_s, gloss_r, norm_s, norm_r, field_s, field_r,
    far_s, far_r, near_s, near_r, sems, old_sems, own_s,
):
    f32, bf16 = jnp.float32, jnp.bfloat16
    core, chip, spot, group, groups = place()
    order, width = moment.shape
    blocks, wide = order // BLOCK, order // width
    layers = m0.shape[0]
    kind = jnp.where(core == 1, 2, lax.div(chip, layers))
    matrix = CHIPS * core + chip
    keep, fresh = STAT_SCALE * STAT_BETA, STAT_SCALE * (1.0 - STAT_BETA)

    def block(i):
        return pl.ds(pl.multiple_of(i * width, width), width)

    def state_copies(k):
        size = sizes[k]
        index = chip if k == 2 else lax.rem(chip, layers)
        inside = pl.ds(0, size)
        pairs = [
            ((ls0, ls1, ls2)[k].at[index], stat.at[inside, inside]),
            ((lb0, lb1, lb2)[k].at[index], basis.at[inside, inside]),
            ((m0, m1, m2)[k].at[index], moment.at[inside]),
            ((v0, v1, v2)[k].at[index], second.at[inside]),
            (rs_hbm.at[matrix], rstat),
            (rb_hbm.at[matrix], rbasis),
        ]
        return [pltpu.make_async_copy(a, b, sems.at[i]) for i, (a, b) in enumerate(pairs)]

    def start_states():
        for k, size in enumerate(sizes):
            @pl.when(kind == k)
            def _():
                if size < order:
                    def pad(i, carry):
                        band = pl.ds(pl.multiple_of(i * 32, 32), 32)
                        row = lax.broadcasted_iota(jnp.int32, (32, order), 0) + i * 32
                        col = lax.broadcasted_iota(jnp.int32, (32, order), 1)
                        unit = jnp.where(row == col, 1.0, 0.0).astype(f32)
                        stat[band, :] = unit * (1.0 / STAT_SCALE)
                        basis[band, :] = unit
                        moment[band, :] = jnp.zeros((32, width), f32)
                        second[band, :] = jnp.zeros((32, width), f32)
                        return carry

                    lax.fori_loop(0, order // 32, pad, 0)
                for copy in state_copies(k):
                    copy.start()

    def all_copies(which):
        olds, news = ((m0, m1, m2), (v0, v1, v2))[which], ((om0, om1, om2), (ov0, ov1, ov2))[which]
        return [
            pltpu.make_async_copy(old, new, old_sems.at[which, k])
            for k, (old, new) in enumerate(zip(olds, news))
        ]

    def wait_states():
        for k in range(len(sizes)):
            @pl.when(kind == k)
            def _():
                for copy in state_copies(k):
                    copy.wait()

    def tall(p):
        return 3 * width if p < 2 else HALF

    def spots(c, p, i):
        if c == 0:
            rows = pl.ds(0, HALF if i == 0 else tall(p))
            return (gall, rall, ufirst)[i].at[p, rows]
        if i == 2:
            return usecond.at[p]
        first, count = ((HALF, HALF), (3 * width, width))[i]
        return (gall, rall)[i].at[p, pl.ds(first, count)]

    def own(c, p, i, ref, other_member):
        if i == 0:
            return ref
        rows = pl.ds(0, tall(p) if c == 0 else width)
        if i == 1:
            return ref.at[rows]
        if c == 0:
            return ref.at[other_member, rows]
        side = pl.ds(pl.multiple_of(other_member * (width // 2), width // 2), width // 2)
        return ref.at[:, side]

    def branches():
        for c in range(2):
            for p in range(CHIPS):
                yield c, p, (core == c) & (chip == p)

    def send_far(i, ref, _):
        for c, p, here in branches():
            @pl.when(here)
            def _():
                to = spots(c, p, i)
                for t in range(1, CHIPS):
                    q = lax.rem(chip + t, CHIPS)
                    remote(
                        own(c, p, i, ref, lax.div(q, 2)), to, far_s.at[t - 1, i],
                        far_r.at[p, i], device(core, q, group),
                    ).start()
                mine = own(c, p, i, ref, lax.div(chip, 2))
                remote(mine, to, near_s.at[p, i], near_r.at[p, i], partner).start()
                pltpu.make_async_copy(mine, to, own_s.at[i]).start()

    def forward(i):
        for c in range(2):
            for p in range(CHIPS):
                @pl.when((core == c) & (chip != p))
                def _():
                    to = spots(c, p, i)
                    remote(to, to, far_s.at[0, i], far_r.at[p, i], partner).wait_recv()
                    remote(to, to, near_s.at[p, i], near_r.at[p, i], partner).start()

    rows = HALF // groups
    partner = device(1 - core, chip, group)
    plane = [device(*other(core, chip, t)[:2], group) for t in range(1, PLANE)]
    along = [device(core, chip, lax.rem(group + t, groups)) for t in range(1, groups)]
    start_states()
    for which in range(2):
        for copy in all_copies(which):
            copy.start()
    greet(plane + along)

    quarter = HALF // 2
    pieces = {0: [[(ref, 0, HALF, 0)] for ref in (e0, e1, n0, n1)], 1: []}
    for p, (ref, begin) in enumerate(((e0, HALF), (e1, HALF), (extra, 0), (extra, quarter))):
        pieces[1].append([(ref, begin, quarter, 0), ((s0, s1, s2, s3)[p], 0, quarter, quarter)])

    def core_copy(p, i, piece):
        ref, begin, size, to = piece
        return remote(
            ref.at[pl.ds(begin, size)], from_core.at[p, pl.ds(to, size)],
            core_s.at[p, i], core_r.at[p, i], partner,
        )

    for c in range(2):
        @pl.when(core == c)
        def _():
            for p in range(CHIPS):
                for i, piece in enumerate(pieces[1 - c][p]):
                    core_copy(p, i, piece).start()

    loss_sends = []
    for t in range(1, PLANE):
        copy = remote(
            loss_ref, plane_loss.at[spot], ploss_s.at[t - 1], ploss_r.at[spot], plane[t - 1]
        )
        copy.start()
        loss_sends.append(copy)
    plane_loss[spot] = loss_ref[...]

    def chunk(index):
        return pl.ds(pl.multiple_of(index * rows, rows), rows)

    def plane_copy(p, turn, index):
        return remote(
            acc.at[p, chunk(index)], from_plane.at[turn - 1, chunk(index)],
            plane_s.at[index, turn - 1], plane_r.at[index, turn - 1], device(core, p, group),
        )

    for p in range(CHIPS):
        for c in range(2):
            @pl.when(core == c)
            def _():
                for i, piece in enumerate(pieces[c][p]):
                    ref, begin, size, to = piece
                    core_copy(p, i, piece).wait_recv()
                    total = ref[begin : begin + size, :].astype(f32) + from_core[
                        p, to : to + size, :
                    ].astype(f32)
                    acc[p, to : to + size, :] = total.astype(bf16)
        turn = lax.rem(p - chip + CHIPS, CHIPS)

        @pl.when(turn != 0)
        def _():
            def go(i, carry):
                plane_copy(p, turn, lax.rem(group + i, groups)).start()
                return carry

            lax.fori_loop(1, groups + 1, go, 0)

    wait_states()
    turned_basis[...] = basis[...].T

    def product(j, carry):
        at = block(j)
        table[:, at] = keep * mm(turned_basis[...], stat[:, at])
        return carry

    lax.fori_loop(0, wide, product, 0)

    def old_gram(j, carry):
        def one(i, carry):
            gram[block(i), block(j)] = mm(table[block(i), :order], table[block(j), :order], 1, 1)
            return carry

        return lax.fori_loop(0, j + 1, one, carry)

    for t in range(1, PLANE):
        _, _, source = other(core, chip, t)
        remote(
            loss_ref, plane_loss.at[source], ploss_s.at[t - 1], ploss_r.at[source], partner
        ).wait_recv()
    total = plane_loss[0]
    for t in range(1, PLANE):
        total = total + plane_loss[t]
    group_loss[group] = total
    for t in range(1, groups):
        copy = remote(
            group_loss.at[group], group_loss.at[group], gloss_s.at[t - 1], gloss_r.at[group],
            along[t - 1],
        )
        copy.start()
        loss_sends.append(copy)

    def gather_plane(index):
        total = acc[chip, chunk(index), :].astype(f32)
        for turn in range(1, CHIPS):
            plane_copy(chip, turn, index).wait_recv()
            total = total + from_plane[turn - 1, chunk(index), :].astype(f32)
        return total

    def group_copy(turn):
        target = lax.rem(group + turn, groups)
        return remote(
            part.at[chunk(target)], from_group.at[turn - 1], group_s.at[turn - 1],
            group_r.at[turn - 1], device(core, chip, target),
        )

    def plane_step(turn, carry):
        target = lax.rem(group + turn, groups)
        part[chunk(target), :] = gather_plane(target).astype(bf16)
        group_copy(turn).start()
        return carry

    lax.fori_loop(1, groups, plane_step, 0)
    lax.fori_loop(0, wide - 1, old_gram, 0)

    def group_step(turn, total):
        group_copy(turn).wait_recv()
        return total + from_group[turn - 1].astype(f32)

    total = lax.fori_loop(1, groups, group_step, gather_plane(group))
    full[chunk(group), :] = total.astype(bf16)

    def full_copy(turn, owner, target):
        return remote(
            full.at[chunk(owner)], full.at[chunk(owner)], full_s.at[turn - 1],
            full_r.at[turn - 1], device(core, chip, target),
        )

    def full_go(turn, carry):
        full_copy(turn, group, lax.rem(group + turn, groups)).start()
        return carry

    def full_wait(turn, carry):
        full_copy(turn, lax.rem(group + groups - turn, groups), group).wait_recv()
        return carry

    lax.fori_loop(1, groups, full_go, 0)
    lax.fori_loop(wide - 1, wide, old_gram, 0)

    def moment_rows(i, carry):
        old_moment[block(i), :] = mm(table[block(i), :order], moment[...])
        return carry

    lax.fori_loop(0, wide, moment_rows, 0)
    stat[...] = table[:, :order]
    basis[...] = stat[...].T
    lax.fori_loop(1, groups, full_wait, 0)

    field = remote(
        field_ref, away_ref, field_s, field_r,
        device(core, lax.rem(chip + CHIPS // 2, CHIPS), group),
    )
    field.start()
    swap = remote(full.at[pl.ds(0, quarter)], tail, tail_s, tail_r, partner)
    swap.start()
    send_far(0, full, full)
    squares = full[...].astype(f32)
    plane_norm[spot] = fold(squares * squares)
    norm_sends = []
    for t in range(1, PLANE):
        copy = remote(
            plane_norm.at[spot], plane_norm.at[spot], norm_s.at[t - 1], norm_r.at[spot],
            plane[t - 1],
        )
        copy.start()
        norm_sends.append(copy)
    for t in range(1, groups):
        source = lax.rem(group + t, groups)
        remote(
            group_loss.at[source], group_loss.at[source], gloss_s.at[t - 1], gloss_r.at[source],
            partner,
        ).wait_recv()
    total = group_loss[0]
    for t in range(1, groups):
        total = total + group_loss[t]
    total_ref[...] = total
    swap.wait_recv()
    grad[...] = jnp.zeros_like(grad)
    for k, size in enumerate(sizes):
        @pl.when(kind == k)
        def _():
            held = HALF if k < 2 else width
            grad[:held, :] = full[HALF - held :, :]
            if size > HALF:
                grad[HALF:size, :] = tail[: size - HALF, :]

    raw = grad[...]

    def grad_rows(i, carry):
        left[block(i), width:] = mm3(turned_basis[block(i), :], grad[...])
        left[block(i), :width] = mm3(stat[block(i), :], grad[...])
        return carry

    lax.fori_loop(0, wide, grad_rows, 0)
    square = lax.dot_general(raw, raw, (((0,), (0,)), ((), ())), preferred_element_type=f32)
    grad_moment = mm3(moment[...], raw, 0, 0).T
    for t in range(1, PLANE):
        _, _, source = other(core, chip, t)
        remote(
            plane_norm.at[source], plane_norm.at[source], norm_s.at[t - 1], norm_r.at[source],
            partner,
        ).wait_recv()
    total = plane_norm[0]
    for t in range(1, PLANE):
        total = total + plane_norm[t]
    norm_ref[...] = total
    norm = jnp.sqrt(jnp.sum(jnp.sum(total, axis=0, keepdims=True), axis=1, keepdims=True))
    clip = jnp.minimum(1.0, CLIP / (norm + 1e-06))


    turned_grad = left[:, width:] * clip
    product_grad = left[:, :width] * clip
    square = square * (clip * clip)
    grad_moment = BETA_ONE * clip * grad_moment + (1.0 - BETA_ONE) * square
    left[:, :width] = fresh * product_grad + (0.5 * fresh * fresh) * mm(turned_grad, square)
    left[:, width:] = turned_grad
    right[:, :width] = turned_grad
    right[:, width:] = left[:, :width]

    def new_gram(j, carry):
        def one(i, carry):
            table[block(i), block(j)] = gram[block(i), block(j)] + mm(
                left[block(i), :], right[block(j), :], 1, 1
            )
            return carry

        return lax.fori_loop(0, j + 1, one, carry)

    lax.fori_loop(0, wide, new_gram, 0)
    table[:, order : order + width] = product_grad + fresh * mm(turned_grad, square)
    table[:, order + width :] = (
        BETA_ONE * old_moment[...]
        + (1.0 - BETA_ONE) * product_grad
        + fresh * mm(turned_grad, grad_moment)
    )
    rstat[...] = keep * rstat[...] + fresh * square
    rbasis[...] = mm(rstat[...], rbasis[...])
    rgram[...] = mm(rbasis[...], rbasis[...], 0, 0)

    def panel(k):
        at = pl.ds(pl.multiple_of(k * BLOCK, BLOCK), BLOCK)
        table[at, :] = mm(inv[at, :], table[at, :])

        @pl.when(lax.rem(k, 2) == 0)
        def _():
            rows = pl.ds(pl.multiple_of(k * BLOCK + BLOCK, BLOCK), BLOCK)
            table[rows, :] = table[rows, :] - mm(table[at, rows], table[at, :], 0, 0)

        @pl.when(lax.rem(k, 2) == 1)
        def _():
            now = lax.div(k, 2)

            def trail(i, carry):
                table[block(i), :] = table[block(i), :] - mm(
                    table[block(now), block(i)], table[block(now), :], 0, 0
                )
                return carry

            lax.fori_loop(now + 1, wide, trail, 0)

    def two(k, carry):
        at = pl.ds(pl.multiple_of(k * BLOCK, BLOCK), BLOCK)
        inv[at, :], rinv[at, :] = inverse_factors([table[at, at], rgram[at, at]])

        @pl.when(k == 0)
        def _():
            upper = mm(rinv[:BLOCK, :], rgram[:BLOCK, BLOCK:])
            rgram[:BLOCK, BLOCK:] = upper
            rgram[BLOCK:, BLOCK:] = rgram[BLOCK:, BLOCK:] - mm(upper, upper, 0, 0)

        panel(k)
        return carry

    def one(k, carry):
        at = pl.ds(pl.multiple_of(k * BLOCK, BLOCK), BLOCK)
        inv[at, :] = inverse_factors([table[at, at]])[0]
        panel(k)
        return carry

    lax.fori_loop(0, width // BLOCK, two, 0)
    forward(0)
    lax.fori_loop(width // BLOCK, blocks, one, 0)
    left_part = mm(rbasis[:, :BLOCK], rinv[:BLOCK, :], 1, 1)
    right_part = mm(
        rbasis[:, BLOCK:] - mm(left_part, rgram[:BLOCK, BLOCK:]), rinv[BLOCK:, :], 1, 1
    )
    rbasis[:, :BLOCK] = left_part
    rbasis[:, BLOCK:] = right_part
    rot = mid(table[:, order : order + width], rbasis[...])
    rot_s[...] = rot.astype(bf16)
    send_far(1, rot_s, rot_s)
    corr_one, corr_two = scal_ref[0], scal_ref[1]
    rotated = mid(table[:, order + width :], rbasis[...])
    grown = BETA_TWO * second[...] + (1.0 - BETA_TWO) * rot * rot
    normed = rotated / corr_one / (jnp.sqrt(grown / corr_two) + EPSILON)
    second[...] = mid(normed, rbasis[...], 1, 1)

    def back(step, carry):
        k = blocks - 1 - step
        at = pl.ds(pl.multiple_of(k * BLOCK, BLOCK), BLOCK)
        part = mid(inv[at, :], second[at, :], 0, 0)
        solved[at, :] = part
        second[...] = second[...] - mid(table[:, at], part)
        return carry

    lax.fori_loop(0, blocks, back, 0)
    forward(1)
    inner = mid(left[:, width:], solved[...], 0, 0)

    def update_rows(i, carry):
        at = block(i)
        update = mid(basis[at, :], solved[...]) + (fresh * clip) * mid(grad[at, :].astype(f32), inner)
        update = update.astype(bf16)
        upd_s[0, at, :] = update[:, : width // 2]
        upd_s[1, at, :] = update[:, width // 2 :]
        return carry

    lax.fori_loop(0, wide, update_rows, 0)
    send_far(2, upd_s, upd_s)
    def arrive(i):
        ref = (full, rot_s, upd_s)[i]
        for c, p, here in branches():
            @pl.when(here)
            def _():
                mine = own(c, p, i, ref, lax.div(chip, 2))
                pltpu.make_async_copy(mine, spots(c, p, i), own_s.at[i]).wait()

        for c in range(2):
            @pl.when(core == c)
            def _():
                for p in range(CHIPS):
                    to = spots(1 - c, p, i)
                    remote(to, to, near_s.at[p, i], near_r.at[p, i], partner).wait_recv()

    for which in range(2):
        for copy in all_copies(which):
            copy.wait()
        arrive(which)
        for k, new in enumerate(((om0, om1, om2), (ov0, ov1, ov2))[which]):
            high = sizes[k] // width

            def moments(step, carry):
                i, b = lax.div(step, high), lax.rem(step, high)
                p = i + layers if k == 1 else i
                value = (gall, rall)[which][p, block(b + 3 if k == 2 else b), :].astype(f32)
                if which == 0:
                    new[i, block(b), :] = BETA_ONE * new[i, block(b), :] + (1.0 - BETA_ONE) * (
                        clip * value
                    )
                else:
                    new[i, block(b), :] = (
                        BETA_TWO * new[i, block(b), :] + (1.0 - BETA_TWO) * value * value
                    )
                return carry

            lax.fori_loop(0, new.shape[0] * high, moments, 0)
    for p in range(2):
        rest_ref[p] = gall[p + 2, HALF : 3 * width, :]
    forward(2)
    arrive(2)

    field.wait()
    swap.wait_send()
    for copy in loss_sends + norm_sends:
        copy.wait_send()
    for c in range(2):
        @pl.when(core == c)
        def _():
            for p in range(CHIPS):
                for i, piece in enumerate(pieces[1 - c][p]):
                    core_copy(p, i, piece).wait_send()
    def plane_done(index, carry):
        for turn in range(1, CHIPS):
            plane_copy(lax.rem(chip + turn, CHIPS), turn, index).wait_send()
        return carry

    lax.fori_loop(0, groups, plane_done, 0)

    def group_done(turn, carry):
        group_copy(turn).wait_send()
        full_copy(turn, group, group).wait_send()
        return carry

    lax.fori_loop(1, groups, group_done, 0)
    for i in range(3):
        for c in range(2):
            @pl.when(core == c)
            def _():
                for p in range(CHIPS):
                    to = spots(c, p, i)
                    remote(to, to, near_s.at[p, i], near_r.at[p, i], partner).wait_send()
        for c, p, here in branches():
            @pl.when(here)
            def _():
                for t in range(1, CHIPS):
                    to = spots(c, p, i)
                    remote(to, to, far_s.at[t - 1, i], far_r.at[p, i], partner).wait_send()


def finish(scal, firsts, seconds, extra, loss, field, moms, seconds_old, lefts, bases, rstat, rbasis):
    groups = lax.axis_size("dp") // 4
    width = extra.shape[1]
    order = max(a.shape[1] for a in lefts)
    sizes = tuple(a.shape[1] for a in lefts)
    f32, bf16 = jnp.float32, jnp.bfloat16
    rows = HALF // groups
    away = max(groups - 1, 1)
    dma = pltpu.SemaphoreType.DMA
    vmem = pl.BlockSpec(memory_space=pltpu.VMEM)
    smem = pl.BlockSpec(memory_space=pltpu.SMEM)
    any_ = pl.BlockSpec(memory_space=pl.ANY)
    tile = (8, 128)
    shape, hold = jax.ShapeDtypeStruct, pltpu.VMEM
    return pl.pallas_call(
        functools.partial(finish_kernel, sizes),
        out_shape=[
            shape(tile, f32), shape(tile, f32), shape(field.shape, bf16),
            shape((2, width, width), bf16),
            shape((CHIPS, order, width // 2), bf16),
            shape((CHIPS, 2, width // 2, width // 2), bf16),
        ] + [shape(a.shape, f32) for a in (*moms, *seconds_old)],
        in_specs=[smem] + [vmem] * 11 + [any_] * 14,
        out_specs=[vmem] * 12,
        scratch_shapes=[
            hold((CHIPS, 2 * HALF, width), bf16), hold((CHIPS, 2 * HALF, width), bf16),
            hold((CHIPS, HALF, width), bf16), hold((CHIPS, HALF, width), bf16),
            hold((CHIPS - 1, HALF, width), bf16), hold((HALF, width), bf16),
            hold((away, rows, width), bf16), hold((HALF, width), bf16),
            hold((HALF // 2, width), bf16),
            hold((PLANE, *tile), f32), hold((groups, *tile), f32), hold((PLANE, *tile), f32),
            hold((order, order), f32), hold((order, order), f32), hold((order, order), f32),
            hold((order, width), f32), hold((order, width), f32),
            hold((width, width), f32), hold((width, width), f32),
            hold((order, order + 2 * width), f32), hold((order, order), f32),
            hold((order, width), bf16),
            hold((order, 2 * width), f32), hold((order, 2 * width), f32),
            hold((order, BLOCK), f32), hold((width, width), f32), hold((width, BLOCK), f32),
            hold((order, width), f32), hold((order, width), f32), hold((order, width), bf16),
            hold((2, order, width // 2), bf16),
            dma((CHIPS, 2)), dma((CHIPS, 2)),
            dma((groups, CHIPS - 1)), dma((groups, CHIPS - 1)),
            dma((away,)), dma((away,)), dma((away,)), dma((away,)),
            dma(()), dma(()),
            dma((PLANE - 1,)), dma((PLANE,)),
            dma((away,)), dma((groups,)),
            dma((PLANE - 1,)), dma((PLANE,)), dma(()), dma(()),
            dma((CHIPS - 1, 3)), dma((CHIPS, 3)), dma((CHIPS, 3)), dma((CHIPS, 3)),
            dma((6,)), dma((2, 3)), dma((3,)),
        ],
        compiler_params=pltpu.CompilerParams(
            collective_id=0, has_side_effects=True, vmem_limit_bytes=60 * 2**20
        ),
        name="finish",
    )(
        scal, *firsts, *seconds, extra, loss, field, *moms, *seconds_old, *lefts, *bases, rstat,
        rbasis,
    )


def dot(a, b):
    return jnp.dot(a, b, preferred_element_type=jnp.float32)


def dot_t(a, b):
    return lax.dot_general(a, b, (((1,), (1,)), ((), ())), preferred_element_type=jnp.float32)


def one_hot(index, first, count):
    rows = lax.broadcasted_iota(jnp.int32, (count, index.shape[1]), 0) + first
    return jnp.where(rows == index, 1.0, 0.0).astype(jnp.bfloat16)


def normalise(value):
    mean = jnp.mean(value, axis=0, keepdims=True)
    centred = value - mean
    scale = lax.rsqrt(jnp.mean(centred * centred, axis=0, keepdims=True) + 1e-05)
    return centred * scale, scale


def normalise_back(grad, hat, scale, gain):
    inner = grad * gain
    return scale * (
        inner
        - jnp.mean(inner, axis=0, keepdims=True)
        - hat * jnp.mean(inner * hat, axis=0, keepdims=True)
    )


def turned(value):
    return value.astype(jnp.float32).T.astype(jnp.bfloat16)


def step_kernel(
    inputs, targets, senders_hbm, receivers_hbm, g2m_hbm, m2g, delta_hbm, level_hbm,
    vec_hbm, edge_hbm, node_hbm, second_hbm, io_wide,
    e0, e1, n0, n1, s0, s1, s2, s3, extra, loss_ref, field_ref, narrow_ref,
    send_tab, recv_tab, g2m_tab, m2g_tab, fields, goal,
    edge_w, edge_t, node_w, node_t, second_w, second_t, got_edge, got_node, got_second,
    grid, enc_hat, enc_scale, mesh, mesh_b, halo_s, halo_r,
    edge, edge_in, edge_slope, edge_hid, edge_hat, edge_scale,
    node_in, node_slope, node_hid, node_hat, node_scale, agg,
    dec_hat, dec_scale, dfinal, dmesh, dext, dedge, dpre, dtot, back_s, back_r, dvec, loss_acc,
    senders, receivers, g2m, delta_row, level_row, vec_rows,
    edge_wide, node_wide, second_wide,
    edge_half, node_half, second_half, io, io_t, vec, small,
    weight_s, weight_r, halo_ss, halo_rs, back_ss, back_rs, fetch,
    *, count_all,
):
    f32, bf16 = jnp.float32, jnp.bfloat16
    layers = edge_half.shape[0]
    width = vec_rows.shape[1]
    nodes = mesh.shape[1]
    count_vec = 4 + 4 * layers
    edges = senders.shape[1]
    points = g2m.shape[1]
    halo = nodes // 2
    tile = 1024
    fields_count = inputs.shape[1]
    dp, member = lax.axis_index("dp"), lax.axis_index("mp")
    blocks = lax.axis_size("dp")
    after, before = lax.rem(dp + 1, blocks), lax.rem(dp + blocks - 1, blocks)
    fetches = [
        pltpu.make_async_copy(src, dst, fetch.at[i])
        for i, (src, dst) in enumerate((
            (edge_hbm, edge_wide), (node_hbm, node_wide), (second_hbm, second_wide),
            (senders_hbm, senders), (receivers_hbm, receivers), (g2m_hbm, g2m),
            (delta_hbm, delta_row), (level_hbm, level_row), (vec_hbm, vec_rows),
        ))
    ]
    for copy in fetches:
        copy.start()
    io[...] = jnp.zeros_like(io)
    vec[...] = jnp.zeros_like(vec)
    small[...] = jnp.zeros_like(small)
    greet([(dp, 1 - member), (after, member), (before, member)])
    for copy in fetches[:3]:
        copy.wait()
    edge_half[...] = edge_wide[...].astype(bf16)
    node_half[...] = node_wide[...].astype(bf16)
    second_half[...] = second_wide[...].astype(bf16)
    shard = edge_half.shape[2]
    mine = pl.ds(pl.multiple_of(member * shard, shard), shard)
    theirs = pl.ds(pl.multiple_of((1 - member) * shard, shard), shard)

    def weight_copies(layer):
        pair = pl.ds(2 * layer, 2)
        return [
            remote(src, dst, weight_s.at[layer, i], weight_r.at[layer, i], (dp, 1 - member))
            for i, (src, dst) in enumerate((
                (edge_half.at[layer], got_edge.at[layer]),
                (second_half.at[pair], got_second.at[pair]),
                (node_half.at[layer], got_node.at[layer]),
            ))
        ]

    for layer in range(layers):
        for copy in weight_copies(layer):
            copy.start()

    def place_weights(layer, edge_part, node_part, second_part, at):
        edge_w[layer, :, at] = edge_part[layer]
        edge_t[layer, at, :] = turned(edge_part[layer])
        node_w[layer, :, at] = node_part[layer]
        node_t[layer, at, :] = turned(node_part[layer])
        for i in (2 * layer, 2 * layer + 1):
            second_w[i, at, :] = second_part[i]
            second_t[i, :, at] = turned(second_part[i])

    def tiles(count, body):
        tile = count

        def go(j, carry):
            body(pl.ds(pl.multiple_of(j * tile, tile), tile))
            return carry

        lax.fori_loop(0, count // tile, go, 0)

    row = pl.ds(member, 1)
    for copy in fetches[3:]:
        copy.wait()
    for i in range(2):
        io[i, :fields_count, :] = io_wide[i].astype(bf16)
        io_t[i] = turned(io[i])
    vec[: vec_rows.shape[0], :] = vec_rows[...]
    vec[...] = vec[...].T
    small[0:1, :fields_count] = delta_row[...]
    small[1:2, :fields_count] = (level_row[...] + 1).astype(f32) / LEVELS
    small[...] = small[...].T
    fields[...] = jnp.zeros_like(fields)
    goal[...] = jnp.zeros_like(goal)
    fields[0:fields_count, :] = inputs[member]
    goal[0:fields_count, :] = targets[member] / small[:fields_count, 0:1]
    dvec[...] = jnp.zeros_like(dvec)
    loss_acc[...] = jnp.zeros_like(loss_acc)

    def gain(i):
        return vec[:, i : i + 1]

    def vec_grads(i, grad, hat):
        dvec[:, i : i + 1] += jnp.sum(grad * hat, axis=1, keepdims=True)
        dvec[:, i + 1 : i + 2] += jnp.sum(grad, axis=1, keepdims=True)

    agg[...] = jnp.zeros_like(agg)

    def encode(at):
        value = dot(io_t[0], fields[:, at])
        grid[:, at] = value
        table = one_hot(g2m[row, at], 0, nodes)
        g2m_tab[:, at] = table
        agg[...] += dot_t(value.astype(bf16), table)

    tiles(points, encode)
    hat, scale = normalise(agg[...])
    enc_hat[...] = hat
    enc_scale[...] = scale
    mesh[...] = hat * gain(0) + gain(1)

    def start_halo(layer):
        value = mesh[...].astype(bf16)
        mesh_b[layer] = value
        halo_s[layer] = value[:, :halo]
        halo_copy(layer).start()

    def halo_copy(layer):
        return remote(
            halo_s.at[layer], halo_r.at[layer], halo_ss.at[layer], halo_rs.at[layer],
            (after, member),
        )

    def back_copy(layer):
        return remote(
            back_s.at[layer], back_r.at[layer], back_ss.at[layer], back_rs.at[layer],
            (before, member),
        )

    start_halo(0)
    place_weights(0, edge_half, node_half, second_half, mine)

    def build(at):
        send_tab[:, at] = one_hot(senders[row, at], 0, nodes + halo)
        recv_tab[:, at] = one_hot(receivers[row, at], 0, nodes)

    tiles(edges, build)
    for layer in range(layers):
        def look_up(at):
            own = mesh_b[layer]
            edge_in[layer, width : 2 * width, at] = dot(own, send_tab[:nodes, at]).astype(bf16)
            edge_in[layer, 2 * width :, at] = dot(own, recv_tab[:, at]).astype(bf16)

        tiles(edges, look_up)
        for copy in weight_copies(layer):
            copy.wait_recv()
        place_weights(layer, got_edge, got_node, got_second, theirs)
        halo_copy(layer).wait_recv()
        agg[...] = jnp.zeros_like(agg)

        def edge_mlp(at):
            sent = edge_in[layer, width : 2 * width, at].astype(f32) + dot(
                halo_r[layer], send_tab[nodes:, at]
            )
            if layer == 0:
                old = sent - edge_in[layer, 2 * width :, at].astype(f32)
            else:
                old = edge[:, at]
            edge_in[layer, width : 2 * width, at] = sent.astype(bf16)
            edge_in[layer, :width, at] = old.astype(bf16)
            pre = dot(edge_t[layer], edge_in[layer, :, at])
            sigma = jax.nn.sigmoid(pre)
            edge_slope[layer, :, at] = sigma * (1.0 + pre * (1.0 - sigma))
            hidden = (pre * sigma).astype(bf16)
            edge_hid[layer, :, at] = hidden
            hat, scale = normalise(dot(second_t[2 * layer], hidden))
            edge_hat[layer, :, at] = hat
            edge_scale[layer, :, at] = scale
            new = old + hat * gain(2 + 4 * layer) + gain(3 + 4 * layer)
            edge[:, at] = new
            agg[...] += dot_t(new.astype(bf16), recv_tab[:, at])

        tiles(edges, edge_mlp)
        node_in[layer, :width] = mesh_b[layer]
        node_in[layer, width:] = agg[...].astype(bf16)
        pre = dot(node_t[layer], node_in[layer])
        sigma = jax.nn.sigmoid(pre)
        node_slope[layer] = sigma * (1.0 + pre * (1.0 - sigma))
        hidden = (pre * sigma).astype(bf16)
        node_hid[layer] = hidden
        hat, scale = normalise(dot(second_t[2 * layer + 1], hidden))
        node_hat[layer] = hat
        node_scale[layer] = scale
        mesh[...] = mesh[...] + hat * gain(4 + 4 * layer) + gain(5 + 4 * layer)
        if layer + 1 < layers:
            start_halo(layer + 1)
            place_weights(layer + 1, edge_half, node_half, second_half, mine)

    mesh_b[layers] = mesh[...].astype(bf16)
    dmesh[...] = jnp.zeros_like(dmesh)
    extra[...] = jnp.zeros_like(extra)
    dext[:, :width] = jnp.zeros((width, width), f32)

    def decode(at):
        index = m2g[member, :, at]
        table = sum(one_hot(index[i : i + 1], 0, nodes).astype(f32) for i in range(3)).astype(bf16)
        m2g_tab[:, at] = table
        hat, scale = normalise(dot(mesh_b[layers], table))
        final = (grid[:, at] + hat * gain(count_vec - 2) + gain(count_vec - 1)).astype(bf16)
        resid = dot(io[1], final) - goal[:, at]
        weighted = small[:, 1:2] * resid
        squares = weighted * resid
        loss_acc[...] += jnp.sum(squares, axis=0, keepdims=True)
        dpred = (weighted * (2.0 / count_all)).astype(bf16)
        dext[: dpred.shape[0], :width] += dot_t(dpred, final)
        grad = dot(io_t[1], dpred)
        dfinal[:, at] = grad
        vec_grads(count_vec - 2, grad, hat)
        ddecoded = normalise_back(grad, hat, scale, gain(count_vec - 2))
        dmesh[...] += dot_t(ddecoded.astype(bf16), table)

    tiles(points, decode)
    io_rows = io.shape[1]
    extra[io_rows : 2 * io_rows, :] = dext[:io_rows, :width].astype(bf16)
    loss_ref[...] = jnp.broadcast_to(
        jnp.sum(loss_acc[...], axis=1, keepdims=True) * (1.0 / 1024.0), loss_ref.shape
    )

    firsts, nexts, seconds = (e0, e1), (n0, n1), (s0, s1, s2, s3)
    for layer in reversed(range(layers)):
        grad, hat = dmesh[...], node_hat[layer]
        vec_grads(4 + 4 * layer, grad, hat)
        total = normalise_back(grad, hat, node_scale[layer], gain(4 + 4 * layer)).astype(bf16)
        seconds[2 * layer + 1][...] = dot_t(node_hid[layer], total).astype(bf16)
        dnode = (dot(second_w[2 * layer + 1], total) * node_slope[layer]).astype(bf16)
        nexts[layer][...] = dot_t(node_in[layer], dnode).astype(bf16)
        dmesh[...] = grad + dot(node_w[layer, :width], dnode)
        agg[...] = dot(node_w[layer, width:], dnode)
        dext[...] = jnp.zeros_like(dext)

        def edge_back(at):
            grad = dot(agg[...].astype(bf16), recv_tab[:, at])
            if layer + 1 < layers:
                grad = grad + dedge[:, at]
            hat = edge_hat[layer, :, at]
            vec_grads(2 + 4 * layer, grad, hat)
            total = normalise_back(
                grad, hat, edge_scale[layer, :, at], gain(2 + 4 * layer)
            ).astype(bf16)
            dtot[:, at] = total
            dhid = dot(second_w[2 * layer], total)
            small = (dhid * edge_slope[layer, :, at]).astype(bf16)
            dpre[:, at] = small
            dself = grad + dot(edge_w[layer, :width], small)
            dsent = dot(edge_w[layer, width : 2 * width], small)
            drecv = dot(edge_w[layer, 2 * width :], small)
            if layer == 0:
                dsent = dsent + dself
                drecv = drecv - dself
            else:
                dedge[:, at] = dself
            dext[...] += dot_t(dsent.astype(bf16), send_tab[:, at])
            dmesh[...] += dot_t(drecv.astype(bf16), recv_tab[:, at])

        tiles(edges, edge_back)
        back_s[layer] = dext[:, nodes:].astype(bf16)
        back_copy(layer).start()
        dmesh[...] += dext[:, :nodes]
        seconds[2 * layer][...] = dot_t(edge_hid[layer], dtot[...]).astype(bf16)

        def weight_grad(i, carry):
            at = pl.ds(pl.multiple_of(i * width, width), width)
            firsts[layer][at, :] = dot_t(edge_in[layer, at, :], dpre[...]).astype(bf16)
            return carry

        lax.fori_loop(0, 3, weight_grad, 0)
        back_copy(layer).wait_recv()
        dmesh[:, :halo] += back_r[layer].astype(f32)

    grad, hat = dmesh[...], enc_hat[...]
    vec_grads(0, grad, hat)
    agg[...] = normalise_back(grad, hat, enc_scale[...], gain(0))
    dext[:io_rows, :width] = jnp.zeros((io_rows, width), f32)

    def encode_back(at):
        dgrid = (dfinal[:, at] + dot(agg[...].astype(bf16), g2m_tab[:, at])).astype(bf16)
        dext[:io_rows, :width] += dot_t(fields[:, at], dgrid)
        out = dot(io[0], dgrid)[:fields_count] * count_all
        field_ref[:, at] = out
        narrow_ref[:, at] = out.astype(bf16)

    tiles(points, encode_back)
    extra[:io_rows, :] = dext[:io_rows, :width].astype(bf16)
    extra[2 * io_rows : 3 * io_rows, :] = dvec[...].T.astype(bf16)
    for layer in range(layers):
        for copy in weight_copies(layer):
            copy.wait_send()
        halo_copy(layer).wait_send()
        back_copy(layer).wait_send()


def train_step(
    inputs, targets, senders, receivers, g2m, m2g, delta, level, vec,
    edge_half, node_half, second_half, io, count_all,
):
    f32, bf16 = jnp.float32, jnp.bfloat16
    layers, width = edge_half.shape[0], vec.shape[1]
    nodes, halo = NODE_DEV, NODE_DEV // 2
    edges, points = senders.shape[1], g2m.shape[1]
    fields_count, io_rows = inputs.shape[1], BLOCK
    i32 = jnp.int32
    any_ = pl.BlockSpec(memory_space=pl.ANY)
    tall, node_tall = edge_half.shape[1], node_half.shape[1]
    dma = pltpu.SemaphoreType.DMA
    vmem = pl.BlockSpec(memory_space=pltpu.VMEM)
    shape = jax.ShapeDtypeStruct
    hold = pltpu.VMEM
    return pl.pallas_call(
        functools.partial(step_kernel, count_all=count_all),
        out_shape=[shape((tall, width), bf16)] * layers
        + [shape((node_tall, width), bf16)] * layers
        + [shape((width, width), bf16)] * (2 * layers)
        + [
            shape((HALF, width), bf16), shape((8, 128), f32),
            shape((fields_count, points), f32), shape((fields_count, points), bf16),
        ],
        in_specs=[vmem] * 2 + [any_] * 3 + [vmem] + [any_] * 6 + [vmem],
        out_specs=[vmem] * (4 * layers + 4),
        scratch_shapes=[
            hold((nodes + halo, edges), bf16), hold((nodes, edges), bf16),
            hold((nodes, points), bf16), hold((nodes, points), bf16),
            hold((io_rows, points), bf16), hold((io_rows, points), f32),
            hold((layers, tall, width), bf16), hold((layers, width, tall), bf16),
            hold((layers, node_tall, width), bf16), hold((layers, width, node_tall), bf16),
            hold((2 * layers, width, width), bf16), hold((2 * layers, width, width), bf16),
            hold(edge_half.shape, bf16), hold(node_half.shape, bf16), hold(second_half.shape, bf16),
            hold((width, points), f32), hold((width, nodes), f32), hold((1, nodes), f32),
            hold((width, nodes), f32), hold((layers + 1, width, nodes), bf16),
            hold((layers, width, halo), bf16), hold((layers, width, halo), bf16),
            hold((width, edges), f32), hold((layers, tall, edges), bf16),
            hold((layers, width, edges), f32), hold((layers, width, edges), bf16),
            hold((layers, width, edges), f32), hold((layers, 1, edges), f32),
            hold((layers, node_tall, nodes), bf16),
            hold((layers, width, nodes), f32), hold((layers, width, nodes), bf16),
            hold((layers, width, nodes), f32), hold((layers, 1, nodes), f32),
            hold((width, nodes), f32),
            hold((width, points), f32), hold((1, points), f32),
            hold((width, points), f32), hold((width, nodes), f32),
            hold((width, nodes + halo), f32), hold((width, edges), f32),
            hold((width, edges), bf16), hold((width, edges), bf16),
            hold((layers, width, halo), bf16), hold((layers, width, halo), bf16),
            hold((width, 128), f32), hold((1, 1024), f32),
            hold(senders.shape, i32), hold(receivers.shape, i32), hold(g2m.shape, i32),
            hold(delta.shape, f32), hold(level.shape, i32),
            hold(vec.shape, f32), hold(edge_half.shape, f32), hold(node_half.shape, f32),
            hold(second_half.shape, f32),
            hold(edge_half.shape, bf16), hold(node_half.shape, bf16),
            hold(second_half.shape, bf16), hold((2, io_rows, width), bf16),
            hold((2, width, io_rows), bf16), hold((width, width), f32), hold((128, 128), f32),
            dma((layers, 3)), dma((layers, 3)),
            dma((layers,)), dma((layers,)), dma((layers,)), dma((layers,)), dma((9,)),
        ],
        compiler_params=pltpu.CompilerParams(
            collective_id=2, has_side_effects=True, vmem_limit_bytes=60 * 2**20
        ),
        name="train_step",
    )(
        inputs, targets, senders, receivers, g2m, m2g, delta, level, vec,
        edge_half, node_half, second_half, io,
    )


def adamw(weight, grad, moment, second_moment, corr_one, corr_two, decay, rate):
    moment = BETA_ONE * moment + (1.0 - BETA_ONE) * grad
    second_moment = BETA_TWO * second_moment + (1.0 - BETA_TWO) * grad * grad
    weight = weight - rate * (
        moment / corr_one / (jnp.sqrt(second_moment / corr_two) + EPSILON) + decay * weight
    )
    return (weight, moment, second_moment)


def body(
    inputs, targets, senders, receivers, g2m_dst, m2g_src, delta_scale, level_index, step_count,
    soap_owner, edge_first, node_first, second, io_weights, vectors,
    edge_first_m, node_first_m, second_m, edge_first_v, node_first_v, second_v,
    io_m, io_v, vector_m, vector_v,
    edge_left_stat, edge_left_basis, node_left_stat, node_left_basis,
    second_left_stat, second_left_basis, right_stat, right_basis,
):
    layers = edge_first.shape[0]
    micro = inputs.shape[0]
    width = vectors.shape[1]
    fields_count = inputs.shape[1]
    member = lax.axis_index("mp")
    count_all = float(micro * fields_count * inputs.shape[2] * lax.axis_size("dp"))
    io_rows = BLOCK
    *grads, extra, loss_tile, field_grad, field_narrow = train_step(
        inputs, targets, senders, receivers, g2m_dst, m2g_src, delta_scale[None],
        level_index[None], vectors, edge_first, node_first, second, io_weights, count_all,
    )
    steps = step_count.astype(jnp.float32)
    corr_one = 1.0 - jnp.power(BETA_ONE, steps)
    corr_two = 1.0 - jnp.power(BETA_TWO, steps)
    norm_tile, loss_tile, field_away, rest, ufirst, usecond, *moments = finish(
        jnp.stack([corr_one, corr_two]), grads[: 2 * layers], grads[2 * layers :], extra,
        loss_tile, field_narrow,
        (edge_first_m, node_first_m, second_m),
        (edge_first_v, node_first_v, second_v),
        (edge_left_stat, node_left_stat, second_left_stat),
        (edge_left_basis, node_left_basis, second_left_basis),
        right_stat, right_basis,
    )
    field_away = field_away.astype(jnp.float32)
    first = member == 0
    input_grad = jnp.stack(
        [jnp.where(first, field_grad, field_away), jnp.where(first, field_away, field_grad)]
    )
    loss = jnp.sum(loss_tile) / count_all
    grad_norm = jnp.sqrt(jnp.sum(norm_tile))
    clip = jnp.minimum(1.0, CLIP / (grad_norm + 1e-06))

    firsts, seconds_out = moments[:3], moments[3:]
    new_edge = edge_first - RATE * (
        ufirst[:layers].astype(jnp.float32) + DECAY * edge_first
    )
    new_node = node_first - RATE * (
        ufirst[layers:, :HALF].astype(jnp.float32) + DECAY * node_first
    )
    upd_second = jnp.concatenate([usecond[:, 0], usecond[:, 1]], axis=2)
    new_second = second - RATE * (upd_second.astype(jnp.float32) + DECAY * second)
    rest = rest.astype(jnp.float32).reshape(HALF, width)
    grad_io = rest.reshape(-1, io_rows, width)[:2, :fields_count]
    grad_vectors = rest[2 * io_rows : 2 * io_rows + vectors.shape[0]]
    new_io, m_io, v_io = adamw(
        io_weights, grad_io * clip, io_m, io_v, corr_one, corr_two, DECAY, RATE
    )
    new_vec, m_vec, v_vec = adamw(
        vectors, grad_vectors * clip, vector_m, vector_v, corr_one, corr_two, 0.0, VECTOR_RATE
    )
    return (
        loss,
        grad_norm,
        new_edge,
        new_edge.astype(jnp.bfloat16),
        new_node,
        new_node.astype(jnp.bfloat16),
        new_second,
        new_second.astype(jnp.bfloat16),
        new_io,
        new_io.astype(jnp.bfloat16),
        new_vec,
        new_vec.astype(jnp.bfloat16),
        *firsts,
        *seconds_out,
        m_io,
        v_io,
        m_vec,
        v_vec,
        input_grad,
    )


def solution(mesh):
    return jax.shard_map(
        body,
        mesh=mesh,
        in_specs=(
            P(None, None, "dp"),
            P(None, None, "dp"),
            P(None, "dp"),
            P(None, "dp"),
            P(None, "dp"),
            P(None, None, "dp"),
            P(),
            P(),
            P(),
            P(),
            P(None, None, "mp"),
            P(None, None, "mp"),
            P(None, "mp", None),
            P(),
            P(),
            P(),
            P(),
            P(),
            P(),
            P(),
            P(),
            P(),
            P(),
            P(),
            P(),
            P(),
            P(),
            P(),
            P(),
            P(),
            P(),
            P(),
            P(),
        ),
        out_specs=(
            P(),
            P(),
            P(None, None, "mp"),
            P(None, None, "mp"),
            P(None, None, "mp"),
            P(None, None, "mp"),
            P(None, "mp", None),
            P(None, "mp", None),
            P(),
            P(),
            P(),
            P(),
            P(),
            P(),
            P(),
            P(),
            P(),
            P(),
            P(),
            P(),
            P(),
            P(),
            P(None, None, "dp"),
        ),
        check_vma=False,
    )
```
